128 devices in a mesh: blk: 32 (over y, z, x_hi), rhs: 4 (over x_lo, core).
Axes of the slice: x: 4 (x_hi: 2, x_lo: 2; x = x_hi * 2 + x_lo), y: 4, z: 4, core: 2. Of those that a mesh axis runs over, the one named last changes fastest.
Arguments:
- strips: float32 [256, 25, 128, 128], P('blk'), may hold values from -0.109375 to 0.109375
- near_cols: int32 [256, 25], P('blk'), may hold values from 0 to 255, as said below
- vector_block: float32 [32768, 2048], P(('blk', 'rhs')), may hold values from -6 to 6
- basis: float32 [4, 32768, 2048], P(None, ('blk', 'rhs')), may hold values from -0.03125 to 0.03125
Outputs:
- new_block: float32 [32768, 2048], P(('blk', 'rhs'))
- coeffs: float32 [4, 16, 128, 128], replicated
- factor: float32 [16, 128, 128], replicated
The draws below stay inside these ranges and needn't reach their ends.
Inputs may be any that keep to these rules, and one draw needn't show every extreme that they name: `near_cols`: each row block has 25 distinct column blocks; slot 0 is the row block itself; every column block lies within 24 blocks of its row block, counted cyclically modulo 256, and some row block has a column block exactly 24 blocks above it.
All inputs are finite; a program needn't handle non-finite values.
Results may differ from the reference program's by a relative error of at most 0.0003.
Values sent between devices are 32-bit elements; how exact they have to be, the bound alone decides.
A program may use at most 256 MiB of HBM per device.

```python
import jax
import jax.numpy as jnp
from jax import lax

BLOCK = 128
NEAR = 25
NRHS = 2048
GROUP = 128
BASIS = 4
RB = 256
ROWS = 32768
BAND = 24


def draw_near_cols(key, part):
    offsets_all = jnp.concatenate([jnp.arange(-BAND, 0), jnp.arange(1, BAND + 1)]).astype(jnp.int32)
    row_keys = jax.random.split(jax.random.fold_in(key, 7), RB)
    perms = jax.vmap(lambda single: jax.random.permutation(single, offsets_all))(row_keys)
    chosen = jax.random.randint(jax.random.fold_in(key, 11), (), 0, RB)
    slots = jnp.arange(2 * BAND)[None, :]
    leading = perms[:, :1]
    forced = jnp.where(perms == BAND, leading, jnp.where(slots == 0, BAND, perms))
    row_ids = jnp.arange(RB)[:, None]
    perms = jnp.where(row_ids == chosen, forced, perms)
    offsets = jnp.concatenate([jnp.zeros((RB, 1), jnp.int32), perms[:, :NEAR - 1]], axis=1)
    return jnp.mod(row_ids + offsets, RB).astype(jnp.int32)


def levels(stream_key, shape, cuts, smallest, top_value):
    def one(axis_at, shards_of):
        heights = jax.random.uniform(jax.random.fold_in(jax.random.fold_in(stream_key, 6), axis_at), (shards_of,), jnp.float32, smallest / len(cuts), top_value / len(cuts))
        return jnp.repeat(jnp.exp(heights), shape[axis_at] // shards_of).reshape((-1,) + (1,) * (len(shape) - axis_at - 1))

    loudness = one(*cuts[0])
    for cut in cuts[1:]:
        loudness = loudness * one(*cut)
    return loudness


def normal_values(rng, shape, scale, limit, cuts=(), kind=jnp.bfloat16):
    entries = scale * jax.random.normal(rng, shape, jnp.float32)
    if cuts:
        entries = entries * levels(rng, shape, cuts, -0.22, 0.18)
    return jnp.clip(entries, -limit, limit).astype(kind)


def setup_inputs(seed: int = 0) -> dict:
    key_list = jax.random.split(jax.random.key(seed), 5)
    strips = normal_values(key_list[0], (RB, NEAR, BLOCK, BLOCK), (NEAR * BLOCK) ** -0.5, 0.109375, ((0, 32),), jnp.float32)
    near_cols = draw_near_cols(jax.random.fold_in(key_list[4], 71), 0)
    vector_block = normal_values(key_list[2], (ROWS, NRHS), 1.0, 6.0, ((0, 128),), jnp.float32)
    basis = normal_values(key_list[3], (BASIS, ROWS, NRHS), ROWS ** -0.5, 0.03125, ((1, 128),), jnp.float32)
    return {"strips": strips, "near_cols": near_cols, "vector_block": vector_block, "basis": basis}


HIGHEST = lax.Precision.HIGHEST

def reference(strips, near_cols, vector_block, basis):
    block = strips.shape[2]
    total_rows, width = vector_block.shape
    pieces = vector_block.reshape(total_rows // block, block, width)

    def one_strip(operands):
        strip, columns = operands
        chosen = pieces[columns.astype(jnp.int32)]
        return jnp.einsum('kab,kbc->ac', strip, chosen, precision=HIGHEST)
    image = lax.map(one_strip, (strips, near_cols)).reshape(total_rows, width)
    groups = width // GROUP
    grouped = image.reshape(total_rows, groups, GROUP)
    basis_grouped = basis.reshape(basis.shape[0], total_rows, groups, GROUP)
    coeffs = jnp.einsum('mnga,ngb->mgab', basis_grouped, grouped, precision=HIGHEST)
    residual = grouped - jnp.einsum('mnga,mgab->ngb', basis_grouped, coeffs, precision=HIGHEST)
    gram = jnp.einsum('nga,ngb->gab', residual, residual, precision=HIGHEST)
    factor = jnp.linalg.cholesky(gram)
    solved = jax.scipy.linalg.solve_triangular(factor, jnp.transpose(residual, (1, 2, 0)), lower=True)
    new_block = jnp.transpose(solved, (2, 0, 1)).reshape(total_rows, width)
    return (new_block, coeffs, factor)
```

```python
import functools

import jax
import jax.numpy as jnp
from jax import lax
from jax.experimental import pallas as pl
from jax.experimental.pallas import tpu as pltpu
from jax.sharding import PartitionSpec as P

HOPS = 3
GROUP = 128
MESH = pl.DeviceIdType.MESH
HIGHEST = lax.Precision.HIGHEST
BF16, F32 = jnp.bfloat16, jnp.float32
VMEM_SPEC = pl.BlockSpec(memory_space=pltpu.VMEM)


def split(value):
    high = value.astype(BF16)
    low = (value - high.astype(F32)).astype(BF16)
    return high, low


def dot1(a, b, ca, cb):
    return lax.dot_general(a, b, (((ca,), (cb,)), ((), ())), preferred_element_type=F32)


def dot3(a, b, ca, cb):
    ah, al = split(a)
    bh, bl = split(b)
    return dot1(ah, bh, ca, cb) + (dot1(ah, bl, ca, cb) + dot1(al, bh, ca, cb))


ORDERS = ((0, 1, 2), (1, 2, 0), (2, 0, 1))


def coordinates():
    blk, rhs = lax.axis_index("blk"), lax.axis_index("rhs")
    x = (blk % 2) * 2 + rhs // 2
    return (x, blk // 8, (blk // 2) % 4), rhs % 2


def device_of(place, core):
    x, y, z = place
    return {"blk": (y * 4 + z) * 2 + x // 2, "rhs": (x % 2) * 2 + core}


def moved(place, axis, by):
    at = list(place)
    at[axis] = (at[axis] + by) % 4
    return tuple(at)


def all_sum_kernel(shares, x_ref, out_ref, from_core, *rest):
    parts = len(shares)
    received, acc = rest[: 3 * parts], rest[3 * parts : 5 * parts]
    send_sem, recv_sem = rest[5 * parts :]
    place, core = coordinates()
    half = x_ref.shape[0] // 2
    partner = device_of(place, 1 - core)
    peers = [device_of(moved(place, axis, by), core) for axis in range(3) for by in (1, 2, 3)]

    barrier = pltpu.get_barrier_semaphore()
    for peer in [partner] + peers:
        pl.semaphore_signal(barrier, inc=1, device_id=peer, device_id_type=MESH)
    pl.semaphore_wait(barrier, 10)

    counter = [0]

    def copy(src, dst, device):
        at = counter[0]
        counter[0] += 1
        made = pltpu.make_async_remote_copy(
            src_ref=src, dst_ref=dst, send_sem=send_sem.at[at], recv_sem=recv_sem.at[at],
            device_id=device, device_id_type=MESH,
        )
        made.start()
        return made

    offsets, total = [], 0
    for share in shares:
        offsets.append(total)
        total += 64 * share
    mine, other = core * half, (1 - core) * half

    first = [
        copy(x_ref.at[pl.ds(other + offset, 64 * share)], from_core.at[pl.ds(offset, 64 * share)], partner)
        for offset, share in zip(offsets, shares)
    ]
    pending = []
    for part, (offset, share) in enumerate(zip(offsets, shares)):
        first[part].wait_recv()
        rows = pl.ds(offset, 64 * share)
        from_core[rows] = from_core[rows] + x_ref[pl.ds(mine + offset, 64 * share)]

    sources = [from_core.at[pl.ds(offset, 64 * share)] for offset, share in zip(offsets, shares)]
    for stage in range(3):
        copies = []
        for part, share in enumerate(shares):
            axis = ORDERS[part][stage]
            size = share * 4 ** (2 - stage)
            block = []
            for by in (1, 2, 3):
                to = (place[axis] + by) % 4
                block.append(copy(
                    sources[part].at[pl.ds(to * size, size)],
                    received[3 * part + stage].at[by - 1],
                    device_of(moved(place, axis, by), core),
                ))
            copies.append(block)
        for part, share in enumerate(shares):
            axis = ORDERS[part][stage]
            size = share * 4 ** (2 - stage)
            for made in copies[part]:
                made.wait_recv()
            got = received[3 * part + stage]
            value = sources[part][pl.ds(place[axis] * size, size)] + got[0] + got[1] + got[2]
            if stage < 2:
                acc[2 * part + stage][...] = value
                sources[part] = acc[2 * part + stage]
            else:
                sources[part] = value
        pending += [made for block in copies for made in block]

    starts = []
    for part, share in enumerate(shares):
        at = mine + offsets[part]
        for stage in range(3):
            at = at + place[ORDERS[part][stage]] * share * 4 ** (2 - stage)
        starts.append(at)
        out_ref[pl.ds(at, share)] = sources[part]
    for stage in (2, 1, 0):
        copies = []
        for part, share in enumerate(shares):
            axis = ORDERS[part][stage]
            size = share * 4 ** (2 - stage)
            at = mine + offsets[part]
            for before in range(stage + 1):
                at = at + place[ORDERS[part][before]] * share * 4 ** (2 - before)
            rows = out_ref.at[pl.ds(at, size)]
            for by in (1, 2, 3):
                copies.append(copy(rows, rows, device_of(moved(place, axis, by), core)))
        for made in copies:
            made.wait_recv()
        pending += copies
    rows = out_ref.at[pl.ds(mine, half)]
    last = copy(rows, rows, partner)
    last.wait_recv()
    for made in first + pending + [last]:
        made.wait_send()


def all_sum(value, shares, collective_id):
    rows = value.shape[0]
    scratch = [pltpu.VMEM((rows // 2, 128), F32)]
    for share in shares:
        scratch += [pltpu.VMEM((3, share * 4 ** (2 - stage), 128), F32) for stage in range(3)]
    for share in shares:
        scratch += [pltpu.VMEM((share * 4 ** (2 - stage), 128), F32) for stage in range(2)]
    copies = 2 * 9 * len(shares) + len(shares) + 1
    return pl.pallas_call(
        functools.partial(all_sum_kernel, shares),
        out_shape=jax.ShapeDtypeStruct(value.shape, F32),
        in_specs=[VMEM_SPEC],
        out_specs=VMEM_SPEC,
        scratch_shapes=scratch + [pltpu.SemaphoreType.DMA((copies,)), pltpu.SemaphoreType.DMA((copies,))],
        compiler_params=pltpu.CompilerParams(collective_id=collective_id, has_side_effects=True),
        name=f"all_sum_{rows}",
    )(value)


def coeffs_kernel(basis_ref, image_ref, out_ref):
    ih, il = split(image_ref[...])
    for m in range(basis_ref.shape[0]):
        bh, bl = split(basis_ref[m])
        out_ref[m, 0] = dot1(bh, ih, 0, 0) + (dot1(bh, il, 0, 0) + dot1(bl, ih, 0, 0))


def local_coeffs(basis, image):
    count, rows, width = basis.shape
    groups = width // GROUP
    return pl.pallas_call(
        coeffs_kernel,
        grid=(groups,),
        out_shape=jax.ShapeDtypeStruct((count, groups, GROUP, GROUP), F32),
        in_specs=[
            pl.BlockSpec((count, rows, GROUP), lambda g: (0, 0, g)),
            pl.BlockSpec((rows, GROUP), lambda g: (0, g)),
        ],
        out_specs=pl.BlockSpec((count, 1, GROUP, GROUP), lambda g: (0, g, 0, 0)),
        name="local_coeffs",
    )(basis, image)


def residual_kernel(basis_ref, image_ref, coeffs_ref, residual_ref, gram_ref):
    value = image_ref[...]
    for m in range(basis_ref.shape[0]):
        value = value - dot3(basis_ref[m], coeffs_ref[m, 0], 1, 0)
    residual_ref[...] = value
    gram_ref[0] = dot3(value, value, 0, 0)


def local_residual(basis, image, coeffs):
    count, rows, width = basis.shape
    groups = width // GROUP
    return pl.pallas_call(
        residual_kernel,
        grid=(groups,),
        out_shape=(
            jax.ShapeDtypeStruct((rows, width), F32),
            jax.ShapeDtypeStruct((groups, GROUP, GROUP), F32),
        ),
        in_specs=[
            pl.BlockSpec((count, rows, GROUP), lambda g: (0, 0, g)),
            pl.BlockSpec((rows, GROUP), lambda g: (0, g)),
            pl.BlockSpec((count, 1, GROUP, GROUP), lambda g: (0, g, 0, 0)),
        ],
        out_specs=(
            pl.BlockSpec((rows, GROUP), lambda g: (0, g)),
            pl.BlockSpec((1, GROUP, GROUP), lambda g: (g, 0, 0)),
        ),
        name="local_residual",
    )(basis, image, coeffs)


STEP = 32


def factor_kernel(gram_ref, residual_ref, new_ref, factor_ref, a_ref, b_ref):
    groups = gram_ref.shape[0]
    a_ref[...] = gram_ref[...]
    shape = (GROUP, GROUP)
    row_of = lax.broadcasted_iota(jnp.int32, shape, 0)
    lane_of = lax.broadcasted_iota(jnp.int32, shape, 1)
    eye = jnp.where(row_of == lane_of, 1.0, 0.0).astype(F32)
    b_ref[...] = jnp.broadcast_to(eye[None], (groups,) + shape)
    lane = lax.broadcasted_iota(jnp.int32, (1, 8, GROUP), 2)
    sub = lax.broadcasted_iota(jnp.int32, (1, 8, GROUP), 1)
    for block in range(GROUP // STEP):
        s = block * STEP
        o = (s + 64) % GROUP
        tiles = []
        for t in range(STEP // 8):
            rows = a_ref[:, s + 8 * t : s + 8 * t + 8, :]
            ones = jnp.where(lane == o + 8 * t + sub, 1.0, 0.0).astype(F32)
            tiles.append(jnp.where((lane >= s) & (lane < s + STEP), rows, ones))
        for j in range(STEP):
            at, within = j // 8, j % 8
            row = tiles[at][:, within : within + 1, :]
            scaled = row / tiles[at][:, within : within + 1, s + j : s + j + 1]
            for t in range(at, STEP // 8):
                column = tiles[t][:, :, s + j : s + j + 1]
                if t == at:
                    column = jnp.where(sub > within, column, 0.0)
                tiles[t] = tiles[t] - column * scaled
        for t in range(STEP // 8):
            diagonal = jnp.sum(jnp.where(lane == s + 8 * t + sub, tiles[t], 0.0), axis=2, keepdims=True)
            tiles[t] = tiles[t] * (1.0 / jnp.sqrt(diagonal))
        panel = jnp.concatenate(tiles, axis=1)
        for g in range(groups):
            inverse = panel[g, :, o : o + STEP]
            wa = jnp.dot(inverse, a_ref[g, s : s + STEP, :], precision=HIGHEST, preferred_element_type=F32)
            wb = jnp.dot(inverse, b_ref[g, s : s + STEP, :], precision=HIGHEST, preferred_element_type=F32)
            a_ref[g, s : s + STEP, :] = wa
            b_ref[g, s : s + STEP, :] = wb
            if s + STEP < GROUP:
                below = slice(s + STEP, GROUP)
                left = wa.T[s + STEP :, :]
                a_ref[g, below, :] = a_ref[g, below, :] - jnp.dot(left, wa, precision=HIGHEST, preferred_element_type=F32)
                b_ref[g, below, :] = b_ref[g, below, :] - jnp.dot(left, wb, precision=HIGHEST, preferred_element_type=F32)
    for g in range(groups):
        factor_ref[g] = jnp.where(row_of >= lane_of, a_ref[g].T, 0.0)
        inverse = jnp.where(row_of >= lane_of, b_ref[g], 0.0)
        columns = slice(g * GROUP, (g + 1) * GROUP)
        new_ref[:, columns] = dot3(residual_ref[:, columns], inverse, 1, 1)


def factor_and_solve(gram, residual):
    return pl.pallas_call(
        factor_kernel,
        out_shape=(jax.ShapeDtypeStruct(residual.shape, F32), jax.ShapeDtypeStruct(gram.shape, F32)),
        in_specs=[VMEM_SPEC, VMEM_SPEC],
        out_specs=(VMEM_SPEC, VMEM_SPEC),
        scratch_shapes=[pltpu.VMEM(gram.shape, F32), pltpu.VMEM(gram.shape, F32)],
        name="factor_and_solve",
    )(gram, residual)


def from_behind(value, axis, by):
    devices = lax.axis_size(axis)
    return lax.ppermute(value, axis, [(i, (i + by) % devices) for i in range(devices)])


def apply_strips(window, positions, strips):
    block = strips.shape[2]
    width = window.shape[1]
    pieces = window.reshape(window.shape[0] // block, block, width)
    chosen = pieces[positions]
    result = jnp.einsum("ikab,ikbc->iac", strips, chosen, precision=HIGHEST)
    return result.reshape(strips.shape[0] * block, width)


def apply_near_field(strips, near_cols, vector_block):
    local_blocks = strips.shape[0]
    total_blocks = local_blocks * lax.axis_size("blk")
    row_form = lax.all_to_all(vector_block, "rhs", split_axis=1, concat_axis=0, tiled=True)
    gathered = []
    for offset in range(-HOPS, HOPS + 1):
        if offset == 0:
            gathered.append(row_form)
        else:
            gathered.append(from_behind(row_form, "blk", -offset))
    window = jnp.concatenate(gathered, axis=0)
    first_block = (lax.axis_index("blk") - HOPS) * local_blocks
    positions = jnp.mod(near_cols - first_block, total_blocks)
    image = apply_strips(window, positions, strips)
    return lax.all_to_all(image, "rhs", split_axis=0, concat_axis=1, tiled=True)


def local(strips, near_cols, vector_block, basis):
    image = apply_near_field(strips, near_cols, vector_block)
    partial_coeffs = local_coeffs(basis, image)
    flat = partial_coeffs.reshape(-1, GROUP)
    coeffs = all_sum(flat, (24, 24, 16), 1).reshape(partial_coeffs.shape)
    residual, partial_gram = local_residual(basis, image, coeffs)
    gram = all_sum(partial_gram.reshape(-1, GROUP), (8, 8), 2).reshape(partial_gram.shape)
    new_block, factor = factor_and_solve(gram, residual)
    return (new_block, coeffs, factor)


def solution(mesh):
    placed = (
        P("blk", None, None, None),
        P("blk", None),
        P(("blk", "rhs"), None),
        P(None, ("blk", "rhs"), None),
    )
    return jax.shard_map(
        local,
        mesh=mesh,
        in_specs=placed,
        out_specs=(P(("blk", "rhs"), None), P(), P()),
        check_vma=False,
    )
```

```python
import functools

import jax
import jax.numpy as jnp
from jax import lax
from jax.experimental import pallas as pl
from jax.experimental.pallas import tpu as pltpu
from jax.sharding import PartitionSpec as P

HOPS = 3
GROUP = 128
MESH = pl.DeviceIdType.MESH
HIGHEST = lax.Precision.HIGHEST
BF16, F32 = jnp.bfloat16, jnp.float32
VMEM_SPEC = pl.BlockSpec(memory_space=pltpu.VMEM)


def split(value):
    high = value.astype(BF16)
    low = (value - high.astype(F32)).astype(BF16)
    return high, low


def dot1(a, b, ca, cb):
    return lax.dot_general(a, b, (((ca,), (cb,)), ((), ())), preferred_element_type=F32)


def dot3(a, b, ca, cb):
    ah, al = split(a)
    bh, bl = split(b)
    return dot1(ah, bh, ca, cb) + (dot1(ah, bl, ca, cb) + dot1(al, bh, ca, cb))


ORDERS = ((0, 1, 2), (1, 2, 0), (2, 0, 1))


def coordinates():
    blk, rhs = lax.axis_index("blk"), lax.axis_index("rhs")
    x = (blk % 2) * 2 + rhs // 2
    return (x, blk // 8, (blk // 2) % 4), rhs % 2


def device_of(place, core):
    x, y, z = place
    return {"blk": (y * 4 + z) * 2 + x // 2, "rhs": (x % 2) * 2 + core}


def moved(place, axis, by):
    at = list(place)
    at[axis] = (at[axis] + by) % 4
    return tuple(at)


def all_sum_kernel(shares, x_ref, out_ref, from_core, *rest):
    parts = len(shares)
    received, acc = rest[: 3 * parts], rest[3 * parts : 5 * parts]
    send_sem, recv_sem = rest[5 * parts :]
    place, core = coordinates()
    half = x_ref.shape[0] // 2
    partner = device_of(place, 1 - core)
    peers = [device_of(moved(place, axis, by), core) for axis in range(3) for by in (1, 2, 3)]

    barrier = pltpu.get_barrier_semaphore()
    for peer in [partner] + peers:
        pl.semaphore_signal(barrier, inc=1, device_id=peer, device_id_type=MESH)
    pl.semaphore_wait(barrier, 10)

    counter = [0]

    def copy(src, dst, device):
        at = counter[0]
        counter[0] += 1
        made = pltpu.make_async_remote_copy(
            src_ref=src, dst_ref=dst, send_sem=send_sem.at[at], recv_sem=recv_sem.at[at],
            device_id=device, device_id_type=MESH,
        )
        made.start()
        return made

    offsets, total = [], 0
    for share in shares:
        offsets.append(total)
        total += 64 * share
    mine, other = core * half, (1 - core) * half

    first = [
        copy(x_ref.at[pl.ds(other + offset, 64 * share)], from_core.at[pl.ds(offset, 64 * share)], partner)
        for offset, share in zip(offsets, shares)
    ]
    pending = []
    for part, (offset, share) in enumerate(zip(offsets, shares)):
        first[part].wait_recv()
        rows = pl.ds(offset, 64 * share)
        from_core[rows] = from_core[rows] + x_ref[pl.ds(mine + offset, 64 * share)]

    sources = [from_core.at[pl.ds(offset, 64 * share)] for offset, share in zip(offsets, shares)]
    for stage in range(3):
        copies = []
        for part, share in enumerate(shares):
            axis = ORDERS[part][stage]
            size = share * 4 ** (2 - stage)
            block = []
            for by in (1, 2, 3):
                to = (place[axis] + by) % 4
                block.append(copy(
                    sources[part].at[pl.ds(to * size, size)],
                    received[3 * part + stage].at[by - 1],
                    device_of(moved(place, axis, by), core),
                ))
            copies.append(block)
        for part, share in enumerate(shares):
            axis = ORDERS[part][stage]
            size = share * 4 ** (2 - stage)
            for made in copies[part]:
                made.wait_recv()
            got = received[3 * part + stage]
            value = sources[part][pl.ds(place[axis] * size, size)] + got[0] + got[1] + got[2]
            if stage < 2:
                acc[2 * part + stage][...] = value
                sources[part] = acc[2 * part + stage]
            else:
                sources[part] = value
        pending += [made for block in copies for made in block]

    starts = []
    for part, share in enumerate(shares):
        at = mine + offsets[part]
        for stage in range(3):
            at = at + place[ORDERS[part][stage]] * share * 4 ** (2 - stage)
        starts.append(at)
        out_ref[pl.ds(at, share)] = sources[part]
    for stage in (2, 1, 0):
        copies = []
        for part, share in enumerate(shares):
            axis = ORDERS[part][stage]
            size = share * 4 ** (2 - stage)
            at = mine + offsets[part]
            for before in range(stage + 1):
                at = at + place[ORDERS[part][before]] * share * 4 ** (2 - before)
            rows = out_ref.at[pl.ds(at, size)]
            for by in (1, 2, 3):
                copies.append(copy(rows, rows, device_of(moved(place, axis, by), core)))
        for made in copies:
            made.wait_recv()
        pending += copies
    rows = out_ref.at[pl.ds(mine, half)]
    last = copy(rows, rows, partner)
    last.wait_recv()
    for made in first + pending + [last]:
        made.wait_send()


def all_sum(value, shares, collective_id):
    rows = value.shape[0]
    scratch = [pltpu.VMEM((rows // 2, 128), F32)]
    for share in shares:
        scratch += [pltpu.VMEM((3, share * 4 ** (2 - stage), 128), F32) for stage in range(3)]
    for share in shares:
        scratch += [pltpu.VMEM((share * 4 ** (2 - stage), 128), F32) for stage in range(2)]
    copies = 2 * 9 * len(shares) + len(shares) + 1
    return pl.pallas_call(
        functools.partial(all_sum_kernel, shares),
        out_shape=jax.ShapeDtypeStruct(value.shape, F32),
        in_specs=[VMEM_SPEC],
        out_specs=VMEM_SPEC,
        scratch_shapes=scratch + [pltpu.SemaphoreType.DMA((copies,)), pltpu.SemaphoreType.DMA((copies,))],
        compiler_params=pltpu.CompilerParams(collective_id=collective_id, has_side_effects=True),
        name=f"all_sum_{rows}",
    )(value)


def coeffs_kernel(basis_ref, image_ref, out_ref):
    ih, il = split(image_ref[...])
    for m in range(basis_ref.shape[0]):
        bh, bl = split(basis_ref[m])
        out_ref[m, 0] = dot1(bh, ih, 0, 0) + (dot1(bh, il, 0, 0) + dot1(bl, ih, 0, 0))


def local_coeffs(basis, image):
    count, rows, width = basis.shape
    groups = width // GROUP
    return pl.pallas_call(
        coeffs_kernel,
        grid=(groups,),
        out_shape=jax.ShapeDtypeStruct((count, groups, GROUP, GROUP), F32),
        in_specs=[
            pl.BlockSpec((count, rows, GROUP), lambda g: (0, 0, g)),
            pl.BlockSpec((rows, GROUP), lambda g: (0, g)),
        ],
        out_specs=pl.BlockSpec((count, 1, GROUP, GROUP), lambda g: (0, g, 0, 0)),
        name="local_coeffs",
    )(basis, image)


def residual_kernel(basis_ref, image_ref, coeffs_ref, residual_ref, gram_ref):
    value = image_ref[...]
    for m in range(basis_ref.shape[0]):
        value = value - dot3(basis_ref[m], coeffs_ref[m, 0], 1, 0)
    residual_ref[...] = value
    gram_ref[0] = dot3(value, value, 0, 0)


def local_residual(basis, image, coeffs):
    count, rows, width = basis.shape
    groups = width // GROUP
    return pl.pallas_call(
        residual_kernel,
        grid=(groups,),
        out_shape=(
            jax.ShapeDtypeStruct((rows, width), F32),
            jax.ShapeDtypeStruct((groups, GROUP, GROUP), F32),
        ),
        in_specs=[
            pl.BlockSpec((count, rows, GROUP), lambda g: (0, 0, g)),
            pl.BlockSpec((rows, GROUP), lambda g: (0, g)),
            pl.BlockSpec((count, 1, GROUP, GROUP), lambda g: (0, g, 0, 0)),
        ],
        out_specs=(
            pl.BlockSpec((rows, GROUP), lambda g: (0, g)),
            pl.BlockSpec((1, GROUP, GROUP), lambda g: (g, 0, 0)),
        ),
        name="local_residual",
    )(basis, image, coeffs)


STEP = 32


def factor_kernel(gram_ref, residual_ref, new_ref, factor_ref, a_ref, b_ref):
    groups = gram_ref.shape[0]
    a_ref[...] = gram_ref[...]
    shape = (GROUP, GROUP)
    row_of = lax.broadcasted_iota(jnp.int32, shape, 0)
    lane_of = lax.broadcasted_iota(jnp.int32, shape, 1)
    eye = jnp.where(row_of == lane_of, 1.0, 0.0).astype(F32)
    b_ref[...] = jnp.broadcast_to(eye[None], (groups,) + shape)
    lane = lax.broadcasted_iota(jnp.int32, (1, 8, GROUP), 2)
    sub = lax.broadcasted_iota(jnp.int32, (1, 8, GROUP), 1)
    for block in range(GROUP // STEP):
        s = block * STEP
        o = (s + 64) % GROUP
        tiles = []
        for t in range(STEP // 8):
            rows = a_ref[:, s + 8 * t : s + 8 * t + 8, :]
            ones = jnp.where(lane == o + 8 * t + sub, 1.0, 0.0).astype(F32)
            tiles.append(jnp.where((lane >= s) & (lane < s + STEP), rows, ones))
        for j in range(STEP):
            at, within = j // 8, j % 8
            row = tiles[at][:, within : within + 1, :]
            scaled = row / tiles[at][:, within : within + 1, s + j : s + j + 1]
            for t in range(at, STEP // 8):
                column = tiles[t][:, :, s + j : s + j + 1]
                if t == at:
                    column = jnp.where(sub > within, column, 0.0)
                tiles[t] = tiles[t] - column * scaled
        for t in range(STEP // 8):
            diagonal = jnp.sum(jnp.where(lane == s + 8 * t + sub, tiles[t], 0.0), axis=2, keepdims=True)
            tiles[t] = tiles[t] * (1.0 / jnp.sqrt(diagonal))
        panel = jnp.concatenate(tiles, axis=1)
        for g in range(groups):
            inverse = panel[g, :, o : o + STEP]
            wa = jnp.dot(inverse, a_ref[g, s : s + STEP, :], precision=HIGHEST, preferred_element_type=F32)
            wb = jnp.dot(inverse, b_ref[g, s : s + STEP, :], precision=HIGHEST, preferred_element_type=F32)
            a_ref[g, s : s + STEP, :] = wa
            b_ref[g, s : s + STEP, :] = wb
            if s + STEP < GROUP:
                below = slice(s + STEP, GROUP)
                left = wa.T[s + STEP :, :]
                a_ref[g, below, :] = a_ref[g, below, :] - jnp.dot(left, wa, precision=HIGHEST, preferred_element_type=F32)
                b_ref[g, below, :] = b_ref[g, below, :] - jnp.dot(left, wb, precision=HIGHEST, preferred_element_type=F32)
    for g in range(groups):
        factor_ref[g] = jnp.where(row_of >= lane_of, a_ref[g].T, 0.0)
        inverse = jnp.where(row_of >= lane_of, b_ref[g], 0.0)
        columns = slice(g * GROUP, (g + 1) * GROUP)
        new_ref[:, columns] = dot3(residual_ref[:, columns], inverse, 1, 1)


def factor_and_solve(gram, residual):
    return pl.pallas_call(
        factor_kernel,
        out_shape=(jax.ShapeDtypeStruct(residual.shape, F32), jax.ShapeDtypeStruct(gram.shape, F32)),
        in_specs=[VMEM_SPEC, VMEM_SPEC],
        out_specs=(VMEM_SPEC, VMEM_SPEC),
        scratch_shapes=[pltpu.VMEM(gram.shape, F32), pltpu.VMEM(gram.shape, F32)],
        name="factor_and_solve",
    )(gram, residual)


SLOTS = 7
SLOT_OFFSETS = (0, 1, -2, 2, -1, 3, -3)
SLOT_ORIGIN = (0, 1, 0, 0, 1, 1, 1)
CHUNKS = 4
PIECE = 256
BLOCK = 128


def apply_kernel(
    index_ref, present_ref, strips_ref, vector_ref, out_ref,
    high_ref, low_ref, window, stage_even, stage_odd, image, strip_sem, copy_sem, recv_sem, exit_recv, own_send, relay_send, entry_send,
    exit_send,
):
    blk, rhs = lax.axis_index("blk"), lax.axis_index("rhs")
    x_lo, core = rhs // 2, rhs % 2
    odd = blk % 2
    sign = 1 - 2 * odd

    def peer(t):
        return (x_lo + t // 2) % 2, (core + t % 2) % 2

    def quarter(at):
        return ((at[0] + odd) % 2) * 2 + at[1]

    def group_device(t):
        x, c = peer(t)
        return {"blk": blk, "rhs": x * 2 + c}

    ahead = {"blk": (blk + 32 + 2 * sign) % 32, "rhs": rhs}
    behind = {"blk": (blk + 32 - 2 * sign) % 32, "rhs": rhs}
    partner = {"blk": blk + sign, "rhs": (1 - x_lo) * 2 + core}
    columns = quarter((x_lo, core)) * (CHUNKS * GROUP)

    def piece(chunk, slot, t):
        x, c = peer(2 * SLOT_ORIGIN[slot] + t)
        return window.at[chunk, slot, pl.ds((x * 2 + c) * PIECE, PIECE)]

    def remote(src, dst, send, recv, device):
        return pltpu.make_async_remote_copy(
            src_ref=src, dst_ref=dst, send_sem=send, recv_sem=recv, device_id=device, device_id_type=MESH
        )

    def strip_copy(i, lane):
        return pltpu.make_async_copy(strips_ref.at[i], (stage_even, stage_odd)[lane], strip_sem.at[lane])

    def own_copy(chunk):
        cols = pl.ds(pl.multiple_of(columns + chunk * GROUP, GROUP), GROUP)
        return pltpu.make_async_copy(vector_ref.at[:, cols], piece(chunk, 0, 0), copy_sem.at[chunk])

    def entry_copy(chunk, t):
        cols = pl.ds(pl.multiple_of(quarter(peer(t)) * (CHUNKS * GROUP) + chunk * GROUP, GROUP), GROUP)
        return remote(
            vector_ref.at[:, cols], piece(chunk, 0, 0), entry_send.at[chunk, t - 1], recv_sem.at[chunk, 0, t],
            group_device(t),
        )

    def exit_copy(chunk, t):
        x, c = peer(t)
        cols = pl.ds(pl.multiple_of(columns + chunk * GROUP, GROUP), GROUP)
        return remote(
            image.at[chunk, pl.ds((x * 2 + c) * PIECE, PIECE)], out_ref.at[:, cols], exit_send.at[chunk, t - 1],
            exit_recv.at[chunk, t - 1], group_device(t),
        )

    def send_copy(chunk, t, way):
        slot, device = ((1, partner), (2, ahead), (3, behind))[way]
        x, c = peer(t)
        dst = window.at[chunk, slot, pl.ds((x * 2 + c) * PIECE, PIECE)]
        return remote(piece(chunk, 0, t), dst, own_send.at[chunk, t, way], recv_sem.at[chunk, slot, t], device)

    def relay_copy(chunk, t, way):
        source, slot, device = ((1, 5, behind), (3, 4, partner), (4, 6, ahead))[way]
        x, c = peer(2 * SLOT_ORIGIN[source] + t)
        dst = window.at[chunk, slot, pl.ds((x * 2 + c) * PIECE, PIECE)]
        return remote(piece(chunk, source, t), dst, relay_send.at[chunk, t, way], recv_sem.at[chunk, slot, t], device)

    def arrived(chunk, slot, t):
        at = piece(chunk, slot, t)
        remote(at, at, own_send.at[chunk, t, 0], recv_sem.at[chunk, slot, t], partner).wait_recv()

    def send_own(chunk, t):
        if t == 0:
            own_copy(chunk).wait()
        else:
            arrived(chunk, 0, t)
        for way in range(3):
            send_copy(chunk, t, way).start()

    def relay(chunk, t, way):
        arrived(chunk, (1, 3, 4)[way], t)
        relay_copy(chunk, t, way).start()

    def build(i, lane):
        stage = (stage_even, stage_odd)[lane]
        strip_copy(i, lane).wait()
        rows = slice(i * BLOCK, (i + 1) * BLOCK)

        def one_slot(slot, carry):
            for j in range(8):
                at = slot * 8 + j
                tile = stage[index_ref[i, at]] * present_ref[i, at]
                high, low = split(tile)
                high_ref[slot, rows, j * BLOCK : (j + 1) * BLOCK] = high
                low_ref[slot, rows, j * BLOCK : (j + 1) * BLOCK] = low
            return carry

        lax.fori_loop(0, SLOTS, one_slot, 0)

        if i + 2 < 8:
            strip_copy(i + 2, lane).start()

    def multiply(chunk, first, last):
        def one(step, carry):
            slot, k = step // 4, pl.multiple_of((step % 4) * PIECE, PIECE)
            high, low = split(window[chunk, slot, pl.ds(k, PIECE)])
            both = dot1(high_ref[slot, :, pl.ds(k, PIECE)], jnp.concatenate([high, low], axis=1), 1, 0)
            rest = dot1(low_ref[slot, :, pl.ds(k, PIECE)], high, 1, 0)
            image[chunk] = image[chunk] + (both[:, :GROUP] + (both[:, GROUP:] + rest))
            return carry

        lax.fori_loop(4 * first, 4 * last, one, 0)

    def finish(chunk):
        cols = pl.ds(pl.multiple_of(columns + chunk * GROUP, GROUP), GROUP)
        out_ref[:, cols] = image[chunk, pl.ds(pl.multiple_of(rhs * PIECE, PIECE), PIECE)]
        for t in (3, 2, 1):
            exit_copy(chunk, t).start()

    def tick(chunk, t, now, before, after):
        if now and t < 3:
            send_own(chunk, t + 1)
        elif now and after is True:
            send_own(chunk + 1, 0)
        elif now:

            @pl.when(after)
            def _():
                send_own(chunk + 1, 0)

        back = chunk - 1
        for way, lag in ((0, 1), (1, 1), (2, 2)):
            if t >= lag and now:
                relay(chunk, t - lag, way)
            elif t < lag and before:
                relay(back, t - lag + 4, way)
        if before:
            if t == 0:
                for u in range(4):
                    arrived(back, 2, u)
                multiply(back, 1, 3)
            if t == 1:
                multiply(back, 3, 4)
            if t == 2:
                for u in range(4):
                    arrived(back, 5, u)
                multiply(back, 4, 6)
            if t == 3:
                for u in range(4):
                    arrived(back, 6, u)
                multiply(back, 6, 7)
                finish(back)

    for i in range(2):
        strip_copy(i, i).start()
    for chunk in range(CHUNKS):
        own_copy(chunk).start()

    barrier = pltpu.get_barrier_semaphore()
    for device in [partner, ahead, behind] + [group_device(t) for t in (1, 2, 3)]:
        pl.semaphore_signal(barrier, inc=1, device_id=device, device_id_type=MESH)
    pl.semaphore_wait(barrier, 6)

    for chunk in range(CHUNKS):
        for t in (2, 3, 1):
            entry_copy(chunk, t).start()
    send_own(0, 0)
    image[...] = jnp.zeros_like(image)
    for t in range(4):
        tick(0, t, True, False, True)
        for i in (2 * t, 2 * t + 1):
            build(i, i % 2)
    multiply(0, 0, 1)

    def body(chunk, carry):
        for t in range(4):
            tick(chunk, t, True, True, chunk + 1 < CHUNKS)
        multiply(chunk, 0, 1)
        return carry

    lax.fori_loop(1, CHUNKS, body, 0)
    for t in range(4):
        tick(CHUNKS, t, False, True, False)

    def drain(chunk, carry):
        for t in (1, 2, 3):
            exit_copy(chunk, t).wait_recv()
            exit_copy(chunk, t).wait_send()
            entry_copy(chunk, t).wait_send()
        for t in range(4):
            for way in range(3):
                send_copy(chunk, t, way).wait_send()
                relay_copy(chunk, t, way).wait_send()
        return carry

    lax.fori_loop(0, CHUNKS, drain, 0)


def apply_near_field(strips, near_cols, vector_block):
    blocks, near = near_cols.shape
    total = blocks * lax.axis_size("blk")
    blk = lax.axis_index("blk")
    sign = 1 - 2 * (blk % 2)
    groups = blk + sign * jnp.array(SLOT_OFFSETS, jnp.int32)
    target = jnp.mod(groups[:, None] * blocks + jnp.arange(blocks, dtype=jnp.int32)[None], total).reshape(-1)
    match = near_cols[:, :, None] == target[None, None]
    index = jnp.sum(jnp.where(match, jnp.arange(near, dtype=jnp.int32)[None, :, None], 0), axis=1)
    present = jnp.sum(jnp.where(match, 1.0, 0.0), axis=1).astype(F32)
    rows, width = vector_block.shape
    smem = pl.BlockSpec(memory_space=pltpu.SMEM)
    anywhere = pl.BlockSpec(memory_space=pl.ANY)
    dma = pltpu.SemaphoreType.DMA
    size = blocks * BLOCK
    return pl.pallas_call(
        apply_kernel,
        out_shape=jax.ShapeDtypeStruct((rows, width), F32),
        in_specs=[smem, smem, anywhere, anywhere],
        out_specs=VMEM_SPEC,
        scratch_shapes=[
            pltpu.VMEM((SLOTS, size, size), BF16),
            pltpu.VMEM((SLOTS, size, size), BF16),
            pltpu.VMEM((CHUNKS, SLOTS, size, GROUP), F32),
            pltpu.VMEM((near, BLOCK, BLOCK), F32),
            pltpu.VMEM((near, BLOCK, BLOCK), F32),
            pltpu.VMEM((CHUNKS, size, GROUP), F32),
            dma((2,)), dma((CHUNKS,)), dma((CHUNKS, SLOTS, 4)), dma((CHUNKS, 3)),
            dma((CHUNKS, 4, 3)), dma((CHUNKS, 4, 3)), dma((CHUNKS, 3)), dma((CHUNKS, 3)),
        ],
        compiler_params=pltpu.CompilerParams(
            collective_id=3, has_side_effects=True, vmem_limit_bytes=64_000_000
        ),
        name="apply_near_field",
    )(index, present, strips, vector_block)


def local(strips, near_cols, vector_block, basis):
    image = apply_near_field(strips, near_cols, vector_block)
    partial_coeffs = local_coeffs(basis, image)
    flat = partial_coeffs.reshape(-1, GROUP)
    coeffs = all_sum(flat, (24, 24, 16), 1).reshape(partial_coeffs.shape)
    residual, partial_gram = local_residual(basis, image, coeffs)
    gram = all_sum(partial_gram.reshape(-1, GROUP), (8, 8), 2).reshape(partial_gram.shape)
    new_block, factor = factor_and_solve(gram, residual)
    return (new_block, coeffs, factor)


def solution(mesh):
    placed = (
        P("blk", None, None, None),
        P("blk", None),
        P(("blk", "rhs"), None),
        P(None, ("blk", "rhs"), None),
    )
    return jax.shard_map(
        local,
        mesh=mesh,
        in_specs=placed,
        out_specs=(P(("blk", "rhs"), None), P(), P()),
        check_vma=False,
    )
```

```python
import functools

import jax
import jax.numpy as jnp
from jax import lax
from jax.experimental import pallas as pl
from jax.experimental.pallas import tpu as pltpu
from jax.sharding import PartitionSpec as P

HOPS = 3
GROUP = 128
MESH = pl.DeviceIdType.MESH
HIGHEST = lax.Precision.HIGHEST
BF16, F32 = jnp.bfloat16, jnp.float32
VMEM_SPEC = pl.BlockSpec(memory_space=pltpu.VMEM)


def split(value):
    high = value.astype(BF16)
    low = (value - high.astype(F32)).astype(BF16)
    return high, low


def dot1(a, b, ca, cb):
    return lax.dot_general(a, b, (((ca,), (cb,)), ((), ())), preferred_element_type=F32)


def dot3(a, b, ca, cb):
    ah, al = split(a)
    bh, bl = split(b)
    return dot1(ah, bh, ca, cb) + (dot1(ah, bl, ca, cb) + dot1(al, bh, ca, cb))


ORDERS = ((0, 1, 2), (1, 2, 0), (2, 0, 1))


def coordinates():
    blk, rhs = lax.axis_index("blk"), lax.axis_index("rhs")
    x = (blk % 2) * 2 + rhs // 2
    return (x, blk // 8, (blk // 2) % 4), rhs % 2


def device_of(place, core):
    x, y, z = place
    return {"blk": (y * 4 + z) * 2 + x // 2, "rhs": (x % 2) * 2 + core}


def moved(place, axis, by):
    at = list(place)
    at[axis] = (at[axis] + by) % 4
    return tuple(at)


def all_sum_kernel(shares, x_ref, out_ref, from_core, *rest):
    parts = len(shares)
    received, acc = rest[: 3 * parts], rest[3 * parts : 5 * parts]
    send_sem, recv_sem = rest[5 * parts :]
    place, core = coordinates()
    half = x_ref.shape[0] // 2
    partner = device_of(place, 1 - core)
    peers = [device_of(moved(place, axis, by), core) for axis in range(3) for by in (1, 2, 3)]

    barrier = pltpu.get_barrier_semaphore()
    for peer in [partner] + peers:
        pl.semaphore_signal(barrier, inc=1, device_id=peer, device_id_type=MESH)
    pl.semaphore_wait(barrier, 10)

    counter = [0]

    def copy(src, dst, device):
        at = counter[0]
        counter[0] += 1
        made = pltpu.make_async_remote_copy(
            src_ref=src, dst_ref=dst, send_sem=send_sem.at[at], recv_sem=recv_sem.at[at],
            device_id=device, device_id_type=MESH,
        )
        made.start()
        return made

    offsets, total = [], 0
    for share in shares:
        offsets.append(total)
        total += 64 * share
    mine, other = core * half, (1 - core) * half

    first = [
        copy(x_ref.at[pl.ds(other + offset, 64 * share)], from_core.at[pl.ds(offset, 64 * share)], partner)
        for offset, share in zip(offsets, shares)
    ]
    pending = []
    for part, (offset, share) in enumerate(zip(offsets, shares)):
        first[part].wait_recv()
        rows = pl.ds(offset, 64 * share)
        from_core[rows] = from_core[rows] + x_ref[pl.ds(mine + offset, 64 * share)]

    sources = [from_core.at[pl.ds(offset, 64 * share)] for offset, share in zip(offsets, shares)]
    for stage in range(3):
        copies = []
        for part, share in enumerate(shares):
            axis = ORDERS[part][stage]
            size = share * 4 ** (2 - stage)
            block = []
            for by in (1, 2, 3):
                to = (place[axis] + by) % 4
                block.append(copy(
                    sources[part].at[pl.ds(to * size, size)],
                    received[3 * part + stage].at[by - 1],
                    device_of(moved(place, axis, by), core),
                ))
            copies.append(block)
        for part, share in enumerate(shares):
            axis = ORDERS[part][stage]
            size = share * 4 ** (2 - stage)
            for made in copies[part]:
                made.wait_recv()
            got = received[3 * part + stage]
            value = sources[part][pl.ds(place[axis] * size, size)] + got[0] + got[1] + got[2]
            if stage < 2:
                acc[2 * part + stage][...] = value
                sources[part] = acc[2 * part + stage]
            else:
                sources[part] = value
        pending += [made for block in copies for made in block]

    starts = []
    for part, share in enumerate(shares):
        at = mine + offsets[part]
        for stage in range(3):
            at = at + place[ORDERS[part][stage]] * share * 4 ** (2 - stage)
        starts.append(at)
        out_ref[pl.ds(at, share)] = sources[part]
    for stage in (2, 1, 0):
        copies = []
        for part, share in enumerate(shares):
            axis = ORDERS[part][stage]
            size = share * 4 ** (2 - stage)
            at = mine + offsets[part]
            for before in range(stage + 1):
                at = at + place[ORDERS[part][before]] * share * 4 ** (2 - before)
            rows = out_ref.at[pl.ds(at, size)]
            for by in (1, 2, 3):
                copies.append(copy(rows, rows, device_of(moved(place, axis, by), core)))
        for made in copies:
            made.wait_recv()
        pending += copies
    rows = out_ref.at[pl.ds(mine, half)]
    last = copy(rows, rows, partner)
    last.wait_recv()
    for made in first + pending + [last]:
        made.wait_send()


def all_sum(value, shares, collective_id):
    rows = value.shape[0]
    scratch = [pltpu.VMEM((rows // 2, 128), F32)]
    for share in shares:
        scratch += [pltpu.VMEM((3, share * 4 ** (2 - stage), 128), F32) for stage in range(3)]
    for share in shares:
        scratch += [pltpu.VMEM((share * 4 ** (2 - stage), 128), F32) for stage in range(2)]
    copies = 2 * 9 * len(shares) + len(shares) + 1
    return pl.pallas_call(
        functools.partial(all_sum_kernel, shares),
        out_shape=jax.ShapeDtypeStruct(value.shape, F32),
        in_specs=[VMEM_SPEC],
        out_specs=VMEM_SPEC,
        scratch_shapes=scratch + [pltpu.SemaphoreType.DMA((copies,)), pltpu.SemaphoreType.DMA((copies,))],
        compiler_params=pltpu.CompilerParams(collective_id=collective_id, has_side_effects=True),
        name=f"all_sum_{rows}",
    )(value)


PER_STEP = 4


def beside(high, low):
    return jnp.concatenate([high, low], axis=1)


def coeffs_kernel(basis_ref, image_ref, out_ref):
    for g in range(PER_STEP):
        columns = slice(g * GROUP, (g + 1) * GROUP)
        ih, il = split(image_ref[:, columns])
        bh, bl = split(jnp.concatenate([basis_ref[m, :, columns] for m in range(basis_ref.shape[0])], axis=1))
        both = dot1(bh, beside(ih, il), 0, 0)
        value = both[:, :GROUP] + (both[:, GROUP:] + dot1(bl, ih, 0, 0))
        for m in range(basis_ref.shape[0]):
            out_ref[m, g] = value[m * GROUP : (m + 1) * GROUP]


def local_coeffs(basis, image):
    count, rows, width = basis.shape
    groups = width // GROUP
    wide = PER_STEP * GROUP
    return pl.pallas_call(
        coeffs_kernel,
        grid=(groups // PER_STEP,),
        out_shape=jax.ShapeDtypeStruct((count, groups, GROUP, GROUP), F32),
        in_specs=[
            pl.BlockSpec((count, rows, wide), lambda g: (0, 0, g)),
            pl.BlockSpec((rows, wide), lambda g: (0, g)),
        ],
        out_specs=pl.BlockSpec((count, PER_STEP, GROUP, GROUP), lambda g: (0, g, 0, 0)),
        name="local_coeffs",
    )(basis, image)


def residual_kernel(basis_ref, image_ref, coeffs_ref, residual_ref, gram_ref, copied_ref):
    count = basis_ref.shape[0]
    copied_ref[...] = coeffs_ref[...]
    for g in range(PER_STEP):
        columns = slice(g * GROUP, (g + 1) * GROUP)
        bh, bl = split(jnp.concatenate([basis_ref[m, :, columns] for m in range(count)], axis=1))
        ch, cl = split(jnp.concatenate([coeffs_ref[m, g] for m in range(count)], axis=0))
        both = dot1(bh, beside(ch, cl), 1, 0)
        value = image_ref[:, columns] - (both[:, :GROUP] + (both[:, GROUP:] + dot1(bl, ch, 1, 0)))
        residual_ref[:, columns] = value
        rh, rl = split(value)
        square = dot1(rh, beside(rh, rl), 0, 0)
        cross = square[:, GROUP:]
        gram_ref[g] = square[:, :GROUP] + (cross + cross.T)


def local_residual(basis, image, coeffs):
    count, rows, width = basis.shape
    groups = width // GROUP
    wide = PER_STEP * GROUP
    return pl.pallas_call(
        residual_kernel,
        grid=(groups // PER_STEP,),
        out_shape=(
            jax.ShapeDtypeStruct((rows, width), F32),
            jax.ShapeDtypeStruct((groups, GROUP, GROUP), F32),
            jax.ShapeDtypeStruct(coeffs.shape, F32),
        ),
        in_specs=[
            pl.BlockSpec((count, rows, wide), lambda g: (0, 0, g)),
            pl.BlockSpec((rows, wide), lambda g: (0, g)),
            pl.BlockSpec((count, PER_STEP, GROUP, GROUP), lambda g: (0, g, 0, 0)),
        ],
        out_specs=(
            pl.BlockSpec((rows, wide), lambda g: (0, g)),
            pl.BlockSpec((PER_STEP, GROUP, GROUP), lambda g: (g, 0, 0)),
            pl.BlockSpec((count, PER_STEP, GROUP, GROUP), lambda g: (0, g, 0, 0)),
        ),
        name="local_residual",
    )(basis, image, coeffs)


STEP = 32


def factor_kernel(gram_ref, residual_ref, new_ref, factor_ref, a_ref, b_ref):
    groups = gram_ref.shape[0]
    a_ref[...] = gram_ref[...]
    shape = (GROUP, GROUP)
    row_of = lax.broadcasted_iota(jnp.int32, shape, 0)
    lane_of = lax.broadcasted_iota(jnp.int32, shape, 1)
    eye = jnp.where(row_of == lane_of, 1.0, 0.0).astype(F32)
    b_ref[...] = jnp.broadcast_to(eye[None], (groups,) + shape)
    lane = lax.broadcasted_iota(jnp.int32, (1, 8, GROUP), 2)
    sub = lax.broadcasted_iota(jnp.int32, (1, 8, GROUP), 1)
    for block in range(GROUP // STEP):
        s = block * STEP
        o = (s + 64) % GROUP
        tiles = []
        for t in range(STEP // 8):
            rows = a_ref[:, s + 8 * t : s + 8 * t + 8, :]
            ones = jnp.where(lane == o + 8 * t + sub, 1.0, 0.0).astype(F32)
            tiles.append(jnp.where((lane >= s) & (lane < s + STEP), rows, ones))
        for j in range(STEP):
            at, within = j // 8, j % 8
            row = tiles[at][:, within : within + 1, :]
            scaled = row / tiles[at][:, within : within + 1, s + j : s + j + 1]
            for t in range(at, STEP // 8):
                column = tiles[t][:, :, s + j : s + j + 1]
                if t == at:
                    column = jnp.where(sub > within, column, 0.0)
                tiles[t] = tiles[t] - column * scaled
        for t in range(STEP // 8):
            diagonal = jnp.sum(jnp.where(lane == s + 8 * t + sub, tiles[t], 0.0), axis=2, keepdims=True)
            tiles[t] = tiles[t] * (1.0 / jnp.sqrt(diagonal))
        panel = jnp.concatenate(tiles, axis=1)
        for g in range(groups):
            inverse = panel[g, :, o : o + STEP]
            wa = jnp.dot(inverse, a_ref[g, s : s + STEP, :], precision=HIGHEST, preferred_element_type=F32)
            wb = jnp.dot(inverse, b_ref[g, s : s + STEP, :], precision=HIGHEST, preferred_element_type=F32)
            a_ref[g, s : s + STEP, :] = wa
            b_ref[g, s : s + STEP, :] = wb
            if s + STEP < GROUP:
                below = slice(s + STEP, GROUP)
                left = wa.T[s + STEP :, :]
                a_ref[g, below, :] = a_ref[g, below, :] - jnp.dot(left, wa, precision=HIGHEST, preferred_element_type=F32)
                b_ref[g, below, :] = b_ref[g, below, :] - jnp.dot(left, wb, precision=HIGHEST, preferred_element_type=F32)
    for g in range(groups):
        factor_ref[g] = jnp.where(row_of >= lane_of, a_ref[g].T, 0.0)
        inverse = jnp.where(row_of >= lane_of, b_ref[g], 0.0)
        columns = slice(g * GROUP, (g + 1) * GROUP)
        nh, nl = split(inverse)
        weights = jnp.concatenate([beside(nh, nh), beside(nl, jnp.zeros_like(nl))], axis=0)
        both = dot1(beside(*split(residual_ref[:, columns])), weights, 1, 1)
        new_ref[:, columns] = both[:, :GROUP] + both[:, GROUP:]


def factor_and_solve(gram, residual):
    return pl.pallas_call(
        factor_kernel,
        out_shape=(jax.ShapeDtypeStruct(residual.shape, F32), jax.ShapeDtypeStruct(gram.shape, F32)),
        in_specs=[VMEM_SPEC, VMEM_SPEC],
        out_specs=(VMEM_SPEC, VMEM_SPEC),
        scratch_shapes=[pltpu.VMEM(gram.shape, F32), pltpu.VMEM(gram.shape, F32)],
        name="factor_and_solve",
    )(gram, residual)


SLOTS = 7
SLOT_OFFSETS = (0, 1, -2, 2, -1, 3, -3)
SLOT_ORIGIN = (0, 1, 0, 0, 1, 1, 1)
CHUNKS = 4
PIECE = 256
BLOCK = 128


def apply_kernel(
    index_ref, present_ref, strips_ref, vector_ref, out_ref,
    high_ref, low_ref, window, stage_even, stage_odd, image, strip_sem, copy_sem, recv_sem, exit_recv, own_send, relay_send, entry_send,
    exit_send,
):
    blk, rhs = lax.axis_index("blk"), lax.axis_index("rhs")
    x_lo, core = rhs // 2, rhs % 2
    odd = blk % 2
    sign = 1 - 2 * odd

    def peer(t):
        return (x_lo + t // 2) % 2, (core + t % 2) % 2

    def quarter(at):
        return ((at[0] + odd) % 2) * 2 + at[1]

    def group_device(t):
        x, c = peer(t)
        return {"blk": blk, "rhs": x * 2 + c}

    ahead = {"blk": (blk + 32 + 2 * sign) % 32, "rhs": rhs}
    behind = {"blk": (blk + 32 - 2 * sign) % 32, "rhs": rhs}
    partner = {"blk": blk + sign, "rhs": (1 - x_lo) * 2 + core}
    columns = quarter((x_lo, core)) * (CHUNKS * GROUP)

    def piece(chunk, slot, t):
        x, c = peer(2 * SLOT_ORIGIN[slot] + t)
        return window.at[chunk, slot, pl.ds((x * 2 + c) * PIECE, PIECE)]

    def remote(src, dst, send, recv, device):
        return pltpu.make_async_remote_copy(
            src_ref=src, dst_ref=dst, send_sem=send, recv_sem=recv, device_id=device, device_id_type=MESH
        )

    def strip_copy(i, lane):
        return pltpu.make_async_copy(strips_ref.at[i], (stage_even, stage_odd)[lane], strip_sem.at[lane])

    def own_copy(chunk):
        cols = pl.ds(pl.multiple_of(columns + chunk * GROUP, GROUP), GROUP)
        return pltpu.make_async_copy(vector_ref.at[:, cols], piece(chunk, 0, 0), copy_sem.at[chunk])

    def entry_copy(chunk, t):
        cols = pl.ds(pl.multiple_of(quarter(peer(t)) * (CHUNKS * GROUP) + chunk * GROUP, GROUP), GROUP)
        return remote(
            vector_ref.at[:, cols], piece(chunk, 0, 0), entry_send.at[chunk, t - 1], recv_sem.at[chunk, 0, t],
            group_device(t),
        )

    def exit_copy(chunk, t):
        x, c = peer(t)
        cols = pl.ds(pl.multiple_of(columns + chunk * GROUP, GROUP), GROUP)
        return remote(
            image.at[chunk, pl.ds((x * 2 + c) * PIECE, PIECE)], out_ref.at[:, cols], exit_send.at[chunk, t - 1],
            exit_recv.at[chunk, t - 1], group_device(t),
        )

    def send_copy(chunk, t, way):
        slot, device = ((1, partner), (2, ahead), (3, behind))[way]
        x, c = peer(t)
        dst = window.at[chunk, slot, pl.ds((x * 2 + c) * PIECE, PIECE)]
        return remote(piece(chunk, 0, t), dst, own_send.at[chunk, t, way], recv_sem.at[chunk, slot, t], device)

    def relay_copy(chunk, t, way):
        source, slot, device = ((1, 5, behind), (3, 4, partner), (4, 6, ahead))[way]
        x, c = peer(2 * SLOT_ORIGIN[source] + t)
        dst = window.at[chunk, slot, pl.ds((x * 2 + c) * PIECE, PIECE)]
        return remote(piece(chunk, source, t), dst, relay_send.at[chunk, t, way], recv_sem.at[chunk, slot, t], device)

    def arrived(chunk, slot, t):
        at = piece(chunk, slot, t)
        remote(at, at, own_send.at[chunk, t, 0], recv_sem.at[chunk, slot, t], partner).wait_recv()

    def send_own(chunk, t):
        if t == 0:
            own_copy(chunk).wait()
        else:
            arrived(chunk, 0, t)
        for way in range(3):
            send_copy(chunk, t, way).start()

    def relay(chunk, t, way):
        arrived(chunk, (1, 3, 4)[way], t)
        relay_copy(chunk, t, way).start()

    def build(i, lane):
        stage = (stage_even, stage_odd)[lane]
        strip_copy(i, lane).wait()
        rows = slice(i * BLOCK, (i + 1) * BLOCK)

        def one_slot(slot, carry):
            for j in range(8):
                at = slot * 8 + j
                tile = stage[index_ref[i, at]] * present_ref[i, at]
                high, low = split(tile)
                high_ref[slot, rows, j * BLOCK : (j + 1) * BLOCK] = high
                low_ref[slot, rows, j * BLOCK : (j + 1) * BLOCK] = low
            return carry

        lax.fori_loop(0, SLOTS, one_slot, 0)

        if i + 2 < 8:
            strip_copy(i + 2, lane).start()

    def multiply(chunk, first, last):
        def one(slot, carry):
            high, low = split(window[chunk, slot])
            both = dot1(high_ref[slot], beside(high, low), 1, 0)
            rest = dot1(low_ref[slot], high, 1, 0)
            image[chunk] = image[chunk] + (both[:, :GROUP] + (both[:, GROUP:] + rest))
            return carry

        lax.fori_loop(first, last, one, 0)

    def finish(chunk):
        cols = pl.ds(pl.multiple_of(columns + chunk * GROUP, GROUP), GROUP)
        out_ref[:, cols] = image[chunk, pl.ds(pl.multiple_of(rhs * PIECE, PIECE), PIECE)]
        for t in (3, 2, 1):
            exit_copy(chunk, t).start()

    def tick(chunk, t, now, before, after):
        if now and t < 3:
            send_own(chunk, t + 1)
        elif now and after is True:
            send_own(chunk + 1, 0)
        elif now:

            @pl.when(after)
            def _():
                send_own(chunk + 1, 0)

        back = chunk - 1
        for way, lag in ((0, 1), (1, 1), (2, 2)):
            if t >= lag and now:
                relay(chunk, t - lag, way)
            elif t < lag and before:
                relay(back, t - lag + 4, way)
        if before:
            if t == 0:
                for u in range(4):
                    arrived(back, 2, u)
                multiply(back, 1, 3)
            if t == 1:
                multiply(back, 3, 4)
            if t == 2:
                for u in range(4):
                    arrived(back, 5, u)
                multiply(back, 4, 6)
            if t == 3:
                for u in range(4):
                    arrived(back, 6, u)
                multiply(back, 6, 7)
                finish(back)

    for i in range(2):
        strip_copy(i, i).start()
    for chunk in range(CHUNKS):
        own_copy(chunk).start()

    barrier = pltpu.get_barrier_semaphore()
    for device in [partner, ahead, behind] + [group_device(t) for t in (1, 2, 3)]:
        pl.semaphore_signal(barrier, inc=1, device_id=device, device_id_type=MESH)
    pl.semaphore_wait(barrier, 6)

    for chunk in range(CHUNKS):
        for t in (2, 3, 1):
            entry_copy(chunk, t).start()
    send_own(0, 0)
    image[...] = jnp.zeros_like(image)
    for t in range(4):
        tick(0, t, True, False, True)
        for i in (2 * t, 2 * t + 1):
            build(i, i % 2)
    multiply(0, 0, 1)

    def body(chunk, carry):
        for t in range(4):
            tick(chunk, t, True, True, chunk + 1 < CHUNKS)
        multiply(chunk, 0, 1)
        return carry

    lax.fori_loop(1, CHUNKS, body, 0)
    for t in range(4):
        tick(CHUNKS, t, False, True, False)

    def drain(chunk, carry):
        for t in (1, 2, 3):
            exit_copy(chunk, t).wait_recv()
            exit_copy(chunk, t).wait_send()
            entry_copy(chunk, t).wait_send()
        for t in range(4):
            for way in range(3):
                send_copy(chunk, t, way).wait_send()
                relay_copy(chunk, t, way).wait_send()
        return carry

    lax.fori_loop(0, CHUNKS, drain, 0)


def apply_near_field(strips, near_cols, vector_block):
    blocks, near = near_cols.shape
    total = blocks * lax.axis_size("blk")
    blk = lax.axis_index("blk")
    sign = 1 - 2 * (blk % 2)
    groups = blk + sign * jnp.array(SLOT_OFFSETS, jnp.int32)
    target = jnp.mod(groups[:, None] * blocks + jnp.arange(blocks, dtype=jnp.int32)[None], total).reshape(-1)
    match = near_cols[:, :, None] == target[None, None]
    index = jnp.sum(jnp.where(match, jnp.arange(near, dtype=jnp.int32)[None, :, None], 0), axis=1)
    present = jnp.sum(jnp.where(match, 1.0, 0.0), axis=1).astype(F32)
    rows, width = vector_block.shape
    smem = pl.BlockSpec(memory_space=pltpu.SMEM)
    anywhere = pl.BlockSpec(memory_space=pl.ANY)
    dma = pltpu.SemaphoreType.DMA
    size = blocks * BLOCK
    return pl.pallas_call(
        apply_kernel,
        out_shape=jax.ShapeDtypeStruct((rows, width), F32),
        in_specs=[smem, smem, anywhere, anywhere],
        out_specs=VMEM_SPEC,
        scratch_shapes=[
            pltpu.VMEM((SLOTS, size, size), BF16),
            pltpu.VMEM((SLOTS, size, size), BF16),
            pltpu.VMEM((CHUNKS, SLOTS, size, GROUP), F32),
            pltpu.VMEM((near, BLOCK, BLOCK), F32),
            pltpu.VMEM((near, BLOCK, BLOCK), F32),
            pltpu.VMEM((CHUNKS, size, GROUP), F32),
            dma((2,)), dma((CHUNKS,)), dma((CHUNKS, SLOTS, 4)), dma((CHUNKS, 3)),
            dma((CHUNKS, 4, 3)), dma((CHUNKS, 4, 3)), dma((CHUNKS, 3)), dma((CHUNKS, 3)),
        ],
        compiler_params=pltpu.CompilerParams(
            collective_id=3, has_side_effects=True, vmem_limit_bytes=64_000_000
        ),
        name="apply_near_field",
    )(index, present, strips, vector_block)


def local(strips, near_cols, vector_block, basis):
    image = apply_near_field(strips, near_cols, vector_block)
    partial_coeffs = local_coeffs(basis, image)
    flat = partial_coeffs.reshape(-1, GROUP)
    coeffs = all_sum(flat, (24, 24, 16), 1).reshape(partial_coeffs.shape)
    residual, partial_gram, coeffs = local_residual(basis, image, coeffs)
    gram = all_sum(partial_gram.reshape(-1, GROUP), (8, 8), 2).reshape(partial_gram.shape)
    new_block, factor = factor_and_solve(gram, residual)
    return (new_block, coeffs, factor)


def solution(mesh):
    placed = (
        P("blk", None, None, None),
        P("blk", None),
        P(("blk", "rhs"), None),
        P(None, ("blk", "rhs"), None),
    )
    return jax.shard_map(
        local,
        mesh=mesh,
        in_specs=placed,
        out_specs=(P(("blk", "rhs"), None), P(), P()),
        check_vma=False,
    )
```

```python
import functools

import jax
import jax.numpy as jnp
from jax import lax
from jax.experimental import pallas as pl
from jax.experimental.pallas import tpu as pltpu
from jax.sharding import PartitionSpec as P

HOPS = 3
GROUP = 128
MESH = pl.DeviceIdType.MESH
HIGHEST = lax.Precision.HIGHEST
BF16, F32 = jnp.bfloat16, jnp.float32
VMEM_SPEC = pl.BlockSpec(memory_space=pltpu.VMEM)


def split(value):
    high = value.astype(BF16)
    low = (value - high.astype(F32)).astype(BF16)
    return high, low


def dot1(a, b, ca, cb):
    return lax.dot_general(a, b, (((ca,), (cb,)), ((), ())), preferred_element_type=F32)


ORDERS = ((0, 1, 2), (1, 2, 0), (2, 0, 1))


def coordinates():
    blk, rhs = lax.axis_index("blk"), lax.axis_index("rhs")
    x = (blk % 2) * 2 + rhs // 2
    return (x, blk // 8, (blk // 2) % 4), rhs % 2


def device_of(place, core):
    x, y, z = place
    return {"blk": (y * 4 + z) * 2 + x // 2, "rhs": (x % 2) * 2 + core}


def moved(place, axis, by):
    at = list(place)
    at[axis] = (at[axis] + by) % 4
    return tuple(at)


COEFF_SHARES = (24, 24, 16)
GRAM_SHARES = (8, 8)
HALF = 8


def beside(high, low):
    return jnp.concatenate([high, low], axis=1)


def orthogonalize_kernel(
    basis_ref, image_ref, coeffs_ref, residual_ref, gram_ref, basis_in, image_in, coeffs_part, gram_part, *rest
):
    coeff_count, gram_count = len(COEFF_SHARES), len(GRAM_SHARES)
    rest = list(rest)

    def take(count):
        taken = rest[:count]
        del rest[:count]
        return taken

    buffers = {}
    for key, count in (("coeffs", coeff_count), ("gram", gram_count)):
        buffers[key] = (take(1)[0], take(3 * count), take(2 * count))
    load_sem, send_sem, recv_sem = rest
    count = basis_ref.shape[0]
    depth = count * GROUP
    place, core = coordinates()
    partner = device_of(place, 1 - core)
    peers = [device_of(moved(place, axis, by), core) for axis in range(3) for by in (1, 2, 3)]
    own_first, other_first = core * HALF, (1 - core) * HALF

    def loads(g):
        columns = pl.ds(pl.multiple_of(g * GROUP, GROUP), GROUP)
        return (
            pltpu.make_async_copy(basis_ref.at[:, :, columns], basis_in.at[g], load_sem.at[0, g]),
            pltpu.make_async_copy(image_ref.at[:, columns], image_in.at[g], load_sem.at[1, g]),
        )

    def start_loads(i, first):
        for load in loads(first + i):
            load.start()
        return first

    lax.fori_loop(0, HALF, start_loads, other_first)
    lax.fori_loop(0, HALF, start_loads, own_first)

    barrier = pltpu.get_barrier_semaphore()
    for peer in [partner] + peers:
        pl.semaphore_signal(barrier, inc=1, device_id=peer, device_id_type=MESH)

    pending = []

    def copy(src, dst, device):
        at = len(pending)
        made = pltpu.make_async_remote_copy(
            src_ref=src, dst_ref=dst, send_sem=send_sem.at[at], recv_sem=recv_sem.at[at],
            device_id=device, device_id_type=MESH,
        )
        made.start()
        pending.append(made)
        return made

    def basis_halves(g):
        return split(jnp.concatenate([basis_in[g, m] for m in range(count)], axis=1))

    def local_coeffs(i, first):
        g = first + i
        for load in loads(g):
            load.wait()
        ih, il = split(image_in[g])
        bh, bl = basis_halves(g)
        both = dot1(bh, beside(ih, il), 0, 0)
        value = both[:, :GROUP] + (both[:, GROUP:] + dot1(bl, ih, 0, 0))
        coeffs_part[pl.ds(pl.multiple_of(g * depth, depth), depth)] = value
        return first

    def local_residual(i, first):
        g = first + i
        bh, bl = basis_halves(g)
        ch, cl = split(coeffs_ref[pl.ds(pl.multiple_of(g * depth, depth), depth)])
        both = dot1(bh, beside(ch, cl), 1, 0)
        value = image_in[g] - (both[:, :GROUP] + (both[:, GROUP:] + dot1(bl, ch, 1, 0)))
        residual_ref[:, pl.ds(pl.multiple_of(g * GROUP, GROUP), GROUP)] = value
        rh, rl = split(value)
        square = dot1(rh, beside(rh, rl), 0, 0)
        cross = square[:, GROUP:]
        gram_part[pl.ds(pl.multiple_of(g * GROUP, GROUP), GROUP)] = square[:, :GROUP] + (cross + cross.T)
        return first

    def bounds(shares):
        ends = [0]
        for share in shares:
            ends.append(ends[-1] + 64 * share)
        return ends

    def swap(key, shares, part_ref, part):
        ends = bounds(shares)
        size = ends[part + 1] - ends[part]
        start = (1 - core) * ends[-1] + ends[part]
        return copy(part_ref.at[pl.ds(start, size)], buffers[key][0].at[pl.ds(ends[part], size)], partner)

    def scatter(key, shares, source, part, stage):
        axis = ORDERS[part][stage]
        size = shares[part] * 4 ** (2 - stage)
        got = buffers[key][1][3 * part + stage]
        return [
            copy(
                source.at[pl.ds((place[axis] + by) % 4 * size, size)], got.at[by - 1],
                device_of(moved(place, axis, by), core),
            )
            for by in (1, 2, 3)
        ]

    def begin(key, shares, part_ref, part, swapped):
        ends = bounds(shares)
        size = ends[part + 1] - ends[part]
        mine = core * ends[-1] + ends[part]
        swapped.wait_recv()
        from_core = buffers[key][0]
        rows = pl.ds(ends[part], size)
        from_core[rows] = from_core[rows] + part_ref[pl.ds(mine, size)]
        source = from_core.at[rows]
        return source, scatter(key, shares, source, part, 0)

    def offset(shares, part, stages):
        ends = bounds(shares)
        at = core * ends[-1] + ends[part]
        for stage in range(stages):
            at = at + place[ORDERS[part][stage]] * (shares[part] * 4 ** (2 - stage))
        return at

    def gather(shares, out_ref, part, stage):
        axis = ORDERS[part][stage]
        size = shares[part] * 4 ** (2 - stage)
        rows = out_ref.at[pl.ds(offset(shares, part, stage + 1), size)]
        return [copy(rows, rows, device_of(moved(place, axis, by), core)) for by in (1, 2, 3)]

    def arrive(copies):
        for made in copies:
            made.wait_recv()

    def sum_up(key, shares, begun, out_ref):
        live = dict(enumerate(begun))
        for stage in range(3):
            for part, share in enumerate(shares):
                source, copies = live[part]
                arrive(copies)
                axis = ORDERS[part][stage]
                size = share * 4 ** (2 - stage)
                got = buffers[key][1][3 * part + stage]
                value = source[pl.ds(place[axis] * size, size)] + got[0] + got[1] + got[2]
                if stage < 2:
                    acc = buffers[key][2][2 * part + stage]
                    acc[...] = value
                    live[part] = (acc, scatter(key, shares, acc, part, stage + 1))
                else:
                    out_ref[pl.ds(offset(shares, part, 3), share)] = value
                    live[part] = gather(shares, out_ref, part, 2)
        for stage in (2, 1, 0):
            for part in range(len(shares)):
                arrive(live[part])
                if stage:
                    live[part] = gather(shares, out_ref, part, stage - 1)
                else:
                    yield part

    def give(shares, out_ref, part):
        ends = bounds(shares)
        rows = out_ref.at[pl.ds(core * ends[-1] + ends[part], ends[part + 1] - ends[part])]
        return copy(rows, rows, partner)

    spans = [(end // depth, last // depth) for end, last in zip(bounds(COEFF_SHARES), bounds(COEFF_SHARES)[1:])]
    swapped = []
    for part, (low, high) in enumerate(spans):
        lax.fori_loop(low, high, local_coeffs, other_first)
        if part == 0:
            pl.semaphore_wait(barrier, 10)
        swapped.append(swap("coeffs", COEFF_SHARES, coeffs_part, part))
    begun = []
    for part, (low, high) in enumerate(spans):
        lax.fori_loop(low, high, local_coeffs, own_first)
        begun.append(begin("coeffs", COEFF_SHARES, coeffs_part, part, swapped[part]))
    given = []
    for part in sum_up("coeffs", COEFF_SHARES, begun, coeffs_ref):
        given.append(give(COEFF_SHARES, coeffs_ref, part))
        lax.fori_loop(*spans[part], local_residual, own_first)

    swapped = []
    for part, (low, high) in enumerate(spans):
        given[part].wait_recv()
        lax.fori_loop(low, high, local_residual, other_first)
        if part:
            swapped.append(swap("gram", GRAM_SHARES, gram_part, part - 1))
    begun = [begin("gram", GRAM_SHARES, gram_part, part, swapped[part]) for part in range(gram_count)]
    given = [give(GRAM_SHARES, gram_ref, part) for part in sum_up("gram", GRAM_SHARES, begun, gram_ref)]
    arrive(given)
    for made in pending:
        made.wait_send()


def orthogonalize(basis, image):
    count, rows, width = basis.shape
    groups = width // GROUP
    scratch = [
        pltpu.VMEM((groups, count, rows, GROUP), F32),
        pltpu.VMEM((groups, rows, GROUP), F32),
        pltpu.VMEM((groups * count * GROUP, GROUP), F32),
        pltpu.VMEM((groups * GROUP, GROUP), F32),
    ]
    copies = 0
    for shares in (COEFF_SHARES, GRAM_SHARES):
        scratch.append(pltpu.VMEM((64 * sum(shares), GROUP), F32))
        for share in shares:
            scratch += [pltpu.VMEM((3, share * 4 ** (2 - stage), GROUP), F32) for stage in range(3)]
        for share in shares:
            scratch += [pltpu.VMEM((share * 4 ** (2 - stage), GROUP), F32) for stage in range(2)]
        copies += 20 * len(shares)
    dma = pltpu.SemaphoreType.DMA
    anywhere = pl.BlockSpec(memory_space=pl.ANY)
    return pl.pallas_call(
        orthogonalize_kernel,
        out_shape=(
            jax.ShapeDtypeStruct((groups * count * GROUP, GROUP), F32),
            jax.ShapeDtypeStruct((rows, width), F32),
            jax.ShapeDtypeStruct((groups * GROUP, GROUP), F32),
        ),
        in_specs=[anywhere, anywhere],
        out_specs=(VMEM_SPEC, VMEM_SPEC, VMEM_SPEC),
        scratch_shapes=scratch + [dma((2, groups)), dma((copies,)), dma((copies,))],
        compiler_params=pltpu.CompilerParams(
            collective_id=1, has_side_effects=True, vmem_limit_bytes=60_000_000
        ),
        name="orthogonalize",
    )(basis, image)


STEP = 32


def factor_kernel(gram_ref, residual_ref, flat_ref, new_ref, factor_ref, coeffs_ref, a_ref, b_ref, held, in_sem, out_sem):
    groups = gram_ref.shape[0]
    count = coeffs_ref.shape[0]
    fetch = pltpu.make_async_copy(flat_ref, held, in_sem)
    fetch.start()
    a_ref[...] = gram_ref[...]
    shape = (GROUP, GROUP)
    row_of = lax.broadcasted_iota(jnp.int32, shape, 0)
    lane_of = lax.broadcasted_iota(jnp.int32, shape, 1)
    eye = jnp.where(row_of == lane_of, 1.0, 0.0).astype(F32)
    b_ref[...] = jnp.broadcast_to(eye[None], (groups,) + shape)
    lane = lax.broadcasted_iota(jnp.int32, (1, 8, GROUP), 2)
    sub = lax.broadcasted_iota(jnp.int32, (1, 8, GROUP), 1)
    stores = [
        pltpu.make_async_copy(held.at[g], coeffs_ref.at[:, g], out_sem.at[g]) for g in range(groups)
    ]
    for block in range(GROUP // STEP):
        if block == 1:
            fetch.wait()
            for store in stores:
                store.start()
        s = block * STEP
        o = (s + 64) % GROUP
        tiles = []
        for t in range(STEP // 8):
            rows = a_ref[:, s + 8 * t : s + 8 * t + 8, :]
            ones = jnp.where(lane == o + 8 * t + sub, 1.0, 0.0).astype(F32)
            tiles.append(jnp.where((lane >= s) & (lane < s + STEP), rows, ones))
        for j in range(STEP):
            at, within = j // 8, j % 8
            row = tiles[at][:, within : within + 1, :]
            scaled = row / tiles[at][:, within : within + 1, s + j : s + j + 1]
            for t in range(at, STEP // 8):
                column = tiles[t][:, :, s + j : s + j + 1]
                if t == at:
                    column = jnp.where(sub > within, column, 0.0)
                tiles[t] = tiles[t] - column * scaled
        for t in range(STEP // 8):
            diagonal = jnp.sum(jnp.where(lane == s + 8 * t + sub, tiles[t], 0.0), axis=2, keepdims=True)
            tiles[t] = tiles[t] * (1.0 / jnp.sqrt(diagonal))
        panel = jnp.concatenate(tiles, axis=1)
        for g in range(groups):
            inverse = panel[g, :, o : o + STEP]
            wa = jnp.dot(inverse, a_ref[g, s : s + STEP, :], precision=HIGHEST, preferred_element_type=F32)
            wb = jnp.dot(inverse, b_ref[g, s : s + STEP, :], precision=HIGHEST, preferred_element_type=F32)
            a_ref[g, s : s + STEP, :] = wa
            b_ref[g, s : s + STEP, :] = wb
            if s + STEP < GROUP:
                below = slice(s + STEP, GROUP)
                left = wa.T[s + STEP :, :]
                a_ref[g, below, :] = a_ref[g, below, :] - jnp.dot(left, wa, precision=HIGHEST, preferred_element_type=F32)
                b_ref[g, below, :] = b_ref[g, below, :] - jnp.dot(left, wb, precision=HIGHEST, preferred_element_type=F32)
    for g in range(groups):
        factor_ref[g] = jnp.where(row_of >= lane_of, a_ref[g].T, 0.0)
        inverse = jnp.where(row_of >= lane_of, b_ref[g], 0.0)
        columns = slice(g * GROUP, (g + 1) * GROUP)
        nh, nl = split(inverse)
        weights = jnp.concatenate([beside(nh, nh), beside(nl, jnp.zeros_like(nl))], axis=0)
        both = dot1(beside(*split(residual_ref[:, columns])), weights, 1, 1)
        new_ref[:, columns] = both[:, :GROUP] + both[:, GROUP:]
    for store in stores:
        store.wait()


def factor_and_solve(gram, residual, flat_coeffs, count):
    groups = gram.shape[0]
    anywhere = pl.BlockSpec(memory_space=pl.ANY)
    shape = (groups, count, GROUP, GROUP)
    return pl.pallas_call(
        factor_kernel,
        out_shape=(
            jax.ShapeDtypeStruct(residual.shape, F32),
            jax.ShapeDtypeStruct(gram.shape, F32),
            jax.ShapeDtypeStruct((count, groups, GROUP, GROUP), F32),
        ),
        in_specs=[VMEM_SPEC, VMEM_SPEC, anywhere],
        out_specs=(VMEM_SPEC, VMEM_SPEC, anywhere),
        scratch_shapes=[
            pltpu.VMEM(gram.shape, F32), pltpu.VMEM(gram.shape, F32), pltpu.VMEM(shape, F32),
            pltpu.SemaphoreType.DMA(()), pltpu.SemaphoreType.DMA((groups,)),
        ],
        name="factor_and_solve",
    )(gram, residual, flat_coeffs.reshape(shape))


SLOTS = 7
SLOT_OFFSETS = (0, 1, -2, 2, -1, 3, -3)
SLOT_ORIGIN = (0, 1, 0, 0, 1, 1, 1)
CHUNKS = 4
PIECE = 256
BLOCK = 128


def apply_kernel(
    index_ref, present_ref, strips_ref, vector_ref, out_ref,
    high_ref, low_ref, window, stage_even, stage_odd, image, strip_sem, copy_sem, recv_sem, exit_recv, own_send, relay_send, entry_send,
    exit_send,
):
    blk, rhs = lax.axis_index("blk"), lax.axis_index("rhs")
    x_lo, core = rhs // 2, rhs % 2
    odd = blk % 2
    sign = 1 - 2 * odd

    def peer(t):
        return (x_lo + t // 2) % 2, (core + t % 2) % 2

    def quarter(at):
        return ((at[0] + odd) % 2) * 2 + at[1]

    def group_device(t):
        x, c = peer(t)
        return {"blk": blk, "rhs": x * 2 + c}

    ahead = {"blk": (blk + 32 + 2 * sign) % 32, "rhs": rhs}
    behind = {"blk": (blk + 32 - 2 * sign) % 32, "rhs": rhs}
    partner = {"blk": blk + sign, "rhs": (1 - x_lo) * 2 + core}
    columns = quarter((x_lo, core)) * (CHUNKS * GROUP)

    def piece(chunk, slot, t):
        x, c = peer(2 * SLOT_ORIGIN[slot] + t)
        return window.at[chunk, slot, pl.ds((x * 2 + c) * PIECE, PIECE)]

    def remote(src, dst, send, recv, device):
        return pltpu.make_async_remote_copy(
            src_ref=src, dst_ref=dst, send_sem=send, recv_sem=recv, device_id=device, device_id_type=MESH
        )

    def strip_copy(i, lane):
        return pltpu.make_async_copy(strips_ref.at[i], (stage_even, stage_odd)[lane], strip_sem.at[lane])

    def own_copy(chunk):
        cols = pl.ds(pl.multiple_of(columns + chunk * GROUP, GROUP), GROUP)
        return pltpu.make_async_copy(vector_ref.at[:, cols], piece(chunk, 0, 0), copy_sem.at[chunk])

    def entry_copy(chunk, t):
        cols = pl.ds(pl.multiple_of(quarter(peer(t)) * (CHUNKS * GROUP) + chunk * GROUP, GROUP), GROUP)
        return remote(
            vector_ref.at[:, cols], piece(chunk, 0, 0), entry_send.at[chunk, t - 1], recv_sem.at[chunk, 0, t],
            group_device(t),
        )

    def exit_copy(chunk, t):
        x, c = peer(t)
        cols = pl.ds(pl.multiple_of(columns + chunk * GROUP, GROUP), GROUP)
        return remote(
            image.at[chunk, pl.ds((x * 2 + c) * PIECE, PIECE)], out_ref.at[:, cols], exit_send.at[chunk, t - 1],
            exit_recv.at[chunk, t - 1], group_device(t),
        )

    def send_copy(chunk, t, way):
        slot, device = ((1, partner), (2, ahead), (3, behind))[way]
        x, c = peer(t)
        dst = window.at[chunk, slot, pl.ds((x * 2 + c) * PIECE, PIECE)]
        return remote(piece(chunk, 0, t), dst, own_send.at[chunk, t, way], recv_sem.at[chunk, slot, t], device)

    def relay_copy(chunk, t, way):
        source, slot, device = ((1, 5, behind), (3, 4, partner), (4, 6, ahead))[way]
        x, c = peer(2 * SLOT_ORIGIN[source] + t)
        dst = window.at[chunk, slot, pl.ds((x * 2 + c) * PIECE, PIECE)]
        return remote(piece(chunk, source, t), dst, relay_send.at[chunk, t, way], recv_sem.at[chunk, slot, t], device)

    def arrived(chunk, slot, t):
        at = piece(chunk, slot, t)
        remote(at, at, own_send.at[chunk, t, 0], recv_sem.at[chunk, slot, t], partner).wait_recv()

    def send_own(chunk, t):
        if t == 0:
            own_copy(chunk).wait()
        else:
            arrived(chunk, 0, t)
        for way in range(3):
            send_copy(chunk, t, way).start()

    def relay(chunk, t, way):
        arrived(chunk, (1, 3, 4)[way], t)
        relay_copy(chunk, t, way).start()

    def build(i, lane):
        stage = (stage_even, stage_odd)[lane]
        strip_copy(i, lane).wait()
        rows = slice(i * BLOCK, (i + 1) * BLOCK)

        def one_slot(slot, carry):
            for j in range(8):
                at = slot * 8 + j
                tile = stage[index_ref[i, at]] * present_ref[i, at]
                high, low = split(tile)
                high_ref[slot, rows, j * BLOCK : (j + 1) * BLOCK] = high
                low_ref[slot, rows, j * BLOCK : (j + 1) * BLOCK] = low
            return carry

        lax.fori_loop(0, SLOTS, one_slot, 0)

        if i + 2 < 8:
            strip_copy(i + 2, lane).start()

    def multiply(chunk, first, last):
        def one(slot, carry):
            high, low = split(window[chunk, slot])
            both = dot1(high_ref[slot], beside(high, low), 1, 0)
            rest = dot1(low_ref[slot], high, 1, 0)
            image[chunk] = image[chunk] + (both[:, :GROUP] + (both[:, GROUP:] + rest))
            return carry

        lax.fori_loop(first, last, one, 0)

    def finish(chunk):
        cols = pl.ds(pl.multiple_of(columns + chunk * GROUP, GROUP), GROUP)
        out_ref[:, cols] = image[chunk, pl.ds(pl.multiple_of(rhs * PIECE, PIECE), PIECE)]
        for t in (3, 2, 1):
            exit_copy(chunk, t).start()

    def tick(chunk, t, first):
        now = True if first else chunk < CHUNKS
        back = chunk - 1

        def when(condition, action):
            if condition is True:
                action()
            else:
                pl.when(condition)(action)

        if t < 3:
            when(now, lambda: send_own(chunk, t + 1))
        else:
            when(True if first else chunk + 1 < CHUNKS, lambda: send_own(chunk + 1, 0))
        for way, lag in ((0, 1), (1, 1), (2, 2)):
            if t >= lag:
                when(now, functools.partial(relay, chunk, t - lag, way))
            elif not first:
                relay(back, t - lag + 4, way)
        if not first:
            for slot in ((2,), (), (5,), (6,))[t]:
                for u in range(4):
                    arrived(back, slot, u)
            multiply(back, (1, 3, 4, 6)[t], (3, 4, 6, 7)[t])
            if t == 3:
                finish(back)

    for i in range(2):
        strip_copy(i, i).start()
    for chunk in range(CHUNKS):
        own_copy(chunk).start()

    barrier = pltpu.get_barrier_semaphore()
    for device in [partner, ahead, behind] + [group_device(t) for t in (1, 2, 3)]:
        pl.semaphore_signal(barrier, inc=1, device_id=device, device_id_type=MESH)
    pl.semaphore_wait(barrier, 6)

    for chunk in range(CHUNKS):
        for t in (2, 3, 1):
            entry_copy(chunk, t).start()
    send_own(0, 0)
    image[...] = jnp.zeros_like(image)
    for t in range(4):
        tick(0, t, True)
        for i in (2 * t, 2 * t + 1):
            build(i, i % 2)
    multiply(0, 0, 1)

    def body(chunk, carry):
        for t in range(4):
            tick(chunk, t, False)

        @pl.when(chunk < CHUNKS)
        def _():
            multiply(chunk, 0, 1)

        return carry

    lax.fori_loop(1, CHUNKS + 1, body, 0)

    def drain(chunk, carry):
        for t in (1, 2, 3):
            exit_copy(chunk, t).wait_recv()
            exit_copy(chunk, t).wait_send()
            entry_copy(chunk, t).wait_send()
        for t in range(4):
            for way in range(3):
                send_copy(chunk, t, way).wait_send()
                relay_copy(chunk, t, way).wait_send()
        return carry

    lax.fori_loop(0, CHUNKS, drain, 0)


def apply_near_field(strips, near_cols, vector_block):
    blocks, near = near_cols.shape
    total = blocks * lax.axis_size("blk")
    blk = lax.axis_index("blk")
    sign = 1 - 2 * (blk % 2)
    groups = blk + sign * jnp.array(SLOT_OFFSETS, jnp.int32)
    target = jnp.mod(groups[:, None] * blocks + jnp.arange(blocks, dtype=jnp.int32)[None], total).reshape(-1)
    match = near_cols[:, :, None] == target[None, None]
    index = jnp.sum(jnp.where(match, jnp.arange(near, dtype=jnp.int32)[None, :, None], 0), axis=1)
    present = jnp.sum(jnp.where(match, 1.0, 0.0), axis=1).astype(F32)
    rows, width = vector_block.shape
    smem = pl.BlockSpec(memory_space=pltpu.SMEM)
    anywhere = pl.BlockSpec(memory_space=pl.ANY)
    dma = pltpu.SemaphoreType.DMA
    size = blocks * BLOCK
    return pl.pallas_call(
        apply_kernel,
        out_shape=jax.ShapeDtypeStruct((rows, width), F32),
        in_specs=[smem, smem, anywhere, anywhere],
        out_specs=VMEM_SPEC,
        scratch_shapes=[
            pltpu.VMEM((SLOTS, size, size), BF16),
            pltpu.VMEM((SLOTS, size, size), BF16),
            pltpu.VMEM((CHUNKS, SLOTS, size, GROUP), F32),
            pltpu.VMEM((near, BLOCK, BLOCK), F32),
            pltpu.VMEM((near, BLOCK, BLOCK), F32),
            pltpu.VMEM((CHUNKS, size, GROUP), F32),
            dma((2,)), dma((CHUNKS,)), dma((CHUNKS, SLOTS, 4)), dma((CHUNKS, 3)),
            dma((CHUNKS, 4, 3)), dma((CHUNKS, 4, 3)), dma((CHUNKS, 3)), dma((CHUNKS, 3)),
        ],
        compiler_params=pltpu.CompilerParams(
            collective_id=3, has_side_effects=True, vmem_limit_bytes=64_000_000
        ),
        name="apply_near_field",
    )(index, present, strips, vector_block)


def local(strips, near_cols, vector_block, basis):
    image = apply_near_field(strips, near_cols, vector_block)
    flat_coeffs, residual, gram = orthogonalize(basis, image)
    gram = gram.reshape(-1, GROUP, GROUP)
    new_block, factor, coeffs = factor_and_solve(gram, residual, flat_coeffs, basis.shape[0])
    return (new_block, coeffs, factor)


def solution(mesh):
    placed = (
        P("blk", None, None, None),
        P("blk", None),
        P(("blk", "rhs"), None),
        P(None, ("blk", "rhs"), None),
    )
    return jax.shard_map(
        local,
        mesh=mesh,
        in_specs=placed,
        out_specs=(P(("blk", "rhs"), None), P(), P()),
        check_vma=False,
    )
```

```python
import functools

import jax
import jax.numpy as jnp
from jax import lax
from jax.experimental import pallas as pl
from jax.experimental.pallas import tpu as pltpu
from jax.sharding import PartitionSpec as P

HOPS = 3
GROUP = 128
MESH = pl.DeviceIdType.MESH
BF16, F32 = jnp.bfloat16, jnp.float32
VMEM_SPEC = pl.BlockSpec(memory_space=pltpu.VMEM)


def split(value):
    high = value.astype(BF16)
    low = (value - high.astype(F32)).astype(BF16)
    return high, low


def dot1(a, b, ca, cb):
    return lax.dot_general(a, b, (((ca,), (cb,)), ((), ())), preferred_element_type=F32)


ORDERS = ((0, 1, 2), (1, 2, 0), (2, 0, 1))


def coordinates():
    blk, rhs = lax.axis_index("blk"), lax.axis_index("rhs")
    x = (blk % 2) * 2 + rhs // 2
    return (x, blk // 8, (blk // 2) % 4), rhs % 2


def device_of(place, core):
    x, y, z = place
    return {"blk": (y * 4 + z) * 2 + x // 2, "rhs": (x % 2) * 2 + core}


def moved(place, axis, by):
    at = list(place)
    at[axis] = (at[axis] + by) % 4
    return tuple(at)


COEFF_SHARES = (24, 24, 16)
GRAM_SHARES = (8, 8)
HALF = 8


def beside(high, low):
    return jnp.concatenate([high, low], axis=1)


def orthogonalize_kernel(
    basis_ref, image_ref, coeffs_ref, residual_ref, gram_ref, basis_in, image_in, coeffs_part, gram_part, *rest
):
    coeff_count, gram_count = len(COEFF_SHARES), len(GRAM_SHARES)
    rest = list(rest)

    def take(count):
        taken = rest[:count]
        del rest[:count]
        return taken

    buffers = {}
    for key, count in (("coeffs", coeff_count), ("gram", gram_count)):
        buffers[key] = (take(1)[0], take(3 * count), take(2 * count))
    load_sem, send_sem, recv_sem = rest
    count = basis_ref.shape[0]
    depth = count * GROUP
    place, core = coordinates()
    partner = device_of(place, 1 - core)
    peers = [device_of(moved(place, axis, by), core) for axis in range(3) for by in (1, 2, 3)]
    own_first, other_first = core * HALF, (1 - core) * HALF

    def loads(g):
        columns = pl.ds(pl.multiple_of(g * GROUP, GROUP), GROUP)
        return (
            pltpu.make_async_copy(basis_ref.at[:, :, columns], basis_in.at[g], load_sem.at[0, g]),
            pltpu.make_async_copy(image_ref.at[:, columns], image_in.at[g], load_sem.at[1, g]),
        )

    def start_loads(i, first):
        for load in loads(first + i):
            load.start()
        return first

    lax.fori_loop(0, HALF, start_loads, other_first)
    lax.fori_loop(0, HALF, start_loads, own_first)

    barrier = pltpu.get_barrier_semaphore()
    for peer in [partner] + peers:
        pl.semaphore_signal(barrier, inc=1, device_id=peer, device_id_type=MESH)

    pending = []

    def copy(src, dst, device):
        at = len(pending)
        made = pltpu.make_async_remote_copy(
            src_ref=src, dst_ref=dst, send_sem=send_sem.at[at], recv_sem=recv_sem.at[at],
            device_id=device, device_id_type=MESH,
        )
        made.start()
        pending.append(made)
        return made

    def basis_halves(g):
        return split(jnp.concatenate([basis_in[g, m] for m in range(count)], axis=1))

    def local_coeffs(i, first):
        g = first + i
        for load in loads(g):
            load.wait()
        ih, il = split(image_in[g])
        bh, bl = basis_halves(g)
        both = dot1(bh, beside(ih, il), 0, 0)
        value = both[:, :GROUP] + (both[:, GROUP:] + dot1(bl, ih, 0, 0))
        coeffs_part[pl.ds(pl.multiple_of(g * depth, depth), depth)] = value
        return first

    def local_residual(i, first):
        g = first + i
        bh, bl = basis_halves(g)
        ch, cl = split(coeffs_ref[pl.ds(pl.multiple_of(g * depth, depth), depth)])
        both = dot1(bh, beside(ch, cl), 1, 0)
        value = image_in[g] - (both[:, :GROUP] + (both[:, GROUP:] + dot1(bl, ch, 1, 0)))
        residual_ref[:, pl.ds(pl.multiple_of(g * GROUP, GROUP), GROUP)] = value
        rh, rl = split(value)
        square = dot1(rh, beside(rh, rl), 0, 0)
        cross = square[:, GROUP:]
        gram_part[pl.ds(pl.multiple_of(g * GROUP, GROUP), GROUP)] = square[:, :GROUP] + (cross + cross.T)
        return first

    def bounds(shares):
        ends = [0]
        for share in shares:
            ends.append(ends[-1] + 64 * share)
        return ends

    def swap(key, shares, part_ref, part):
        ends = bounds(shares)
        size = ends[part + 1] - ends[part]
        start = (1 - core) * ends[-1] + ends[part]
        return copy(part_ref.at[pl.ds(start, size)], buffers[key][0].at[pl.ds(ends[part], size)], partner)

    def scatter(key, shares, source, part, stage):
        axis = ORDERS[part][stage]
        size = shares[part] * 4 ** (2 - stage)
        got = buffers[key][1][3 * part + stage]
        return [
            copy(
                source.at[pl.ds((place[axis] + by) % 4 * size, size)], got.at[by - 1],
                device_of(moved(place, axis, by), core),
            )
            for by in (1, 2, 3)
        ]

    def begin(key, shares, part_ref, part, swapped):
        ends = bounds(shares)
        size = ends[part + 1] - ends[part]
        mine = core * ends[-1] + ends[part]
        swapped.wait_recv()
        from_core = buffers[key][0]
        rows = pl.ds(ends[part], size)
        from_core[rows] = from_core[rows] + part_ref[pl.ds(mine, size)]
        source = from_core.at[rows]
        return source, scatter(key, shares, source, part, 0)

    def offset(shares, part, stages):
        ends = bounds(shares)
        at = core * ends[-1] + ends[part]
        for stage in range(stages):
            at = at + place[ORDERS[part][stage]] * (shares[part] * 4 ** (2 - stage))
        return at

    def gather(shares, out_ref, part, stage):
        axis = ORDERS[part][stage]
        size = shares[part] * 4 ** (2 - stage)
        rows = out_ref.at[pl.ds(offset(shares, part, stage + 1), size)]
        return [copy(rows, rows, device_of(moved(place, axis, by), core)) for by in (1, 2, 3)]

    def arrive(copies):
        for made in copies:
            made.wait_recv()

    def sum_up(key, shares, begun, out_ref):
        live = dict(enumerate(begun))
        for stage in range(3):
            for part, share in enumerate(shares):
                source, copies = live[part]
                arrive(copies)
                axis = ORDERS[part][stage]
                size = share * 4 ** (2 - stage)
                got = buffers[key][1][3 * part + stage]
                value = source[pl.ds(place[axis] * size, size)] + got[0] + got[1] + got[2]
                if stage < 2:
                    acc = buffers[key][2][2 * part + stage]
                    acc[...] = value
                    live[part] = (acc, scatter(key, shares, acc, part, stage + 1))
                else:
                    out_ref[pl.ds(offset(shares, part, 3), share)] = value
                    live[part] = gather(shares, out_ref, part, 2)
        for stage in (2, 1, 0):
            for part in range(len(shares)):
                arrive(live[part])
                if stage:
                    live[part] = gather(shares, out_ref, part, stage - 1)
                else:
                    yield part

    def give(shares, out_ref, part):
        ends = bounds(shares)
        rows = out_ref.at[pl.ds(core * ends[-1] + ends[part], ends[part + 1] - ends[part])]
        return copy(rows, rows, partner)

    spans = [(end // depth, last // depth) for end, last in zip(bounds(COEFF_SHARES), bounds(COEFF_SHARES)[1:])]
    swapped = []
    for part, (low, high) in enumerate(spans):
        lax.fori_loop(low, high, local_coeffs, other_first)
        if part == 0:
            pl.semaphore_wait(barrier, 10)
        swapped.append(swap("coeffs", COEFF_SHARES, coeffs_part, part))
    begun = []
    for part, (low, high) in enumerate(spans):
        lax.fori_loop(low, high, local_coeffs, own_first)
        begun.append(begin("coeffs", COEFF_SHARES, coeffs_part, part, swapped[part]))
    given = []
    for part in sum_up("coeffs", COEFF_SHARES, begun, coeffs_ref):
        given.append(give(COEFF_SHARES, coeffs_ref, part))
        lax.fori_loop(*spans[part], local_residual, own_first)

    swapped = []
    for part, (low, high) in enumerate(spans):
        given[part].wait_recv()
        lax.fori_loop(low, high, local_residual, other_first)
        if part:
            swapped.append(swap("gram", GRAM_SHARES, gram_part, part - 1))
    begun = [begin("gram", GRAM_SHARES, gram_part, part, swapped[part]) for part in range(gram_count)]
    given = [give(GRAM_SHARES, gram_ref, part) for part in sum_up("gram", GRAM_SHARES, begun, gram_ref)]
    arrive(given)
    for made in pending:
        made.wait_send()


def orthogonalize(basis, image):
    count, rows, width = basis.shape
    groups = width // GROUP
    scratch = [
        pltpu.VMEM((groups, count, rows, GROUP), F32),
        pltpu.VMEM((groups, rows, GROUP), F32),
        pltpu.VMEM((groups * count * GROUP, GROUP), F32),
        pltpu.VMEM((groups * GROUP, GROUP), F32),
    ]
    copies = 0
    for shares in (COEFF_SHARES, GRAM_SHARES):
        scratch.append(pltpu.VMEM((64 * sum(shares), GROUP), F32))
        for share in shares:
            scratch += [pltpu.VMEM((3, share * 4 ** (2 - stage), GROUP), F32) for stage in range(3)]
        for share in shares:
            scratch += [pltpu.VMEM((share * 4 ** (2 - stage), GROUP), F32) for stage in range(2)]
        copies += 20 * len(shares)
    dma = pltpu.SemaphoreType.DMA
    anywhere = pl.BlockSpec(memory_space=pl.ANY)
    return pl.pallas_call(
        orthogonalize_kernel,
        out_shape=(
            jax.ShapeDtypeStruct((groups * count * GROUP, GROUP), F32),
            jax.ShapeDtypeStruct((rows, width), F32),
            jax.ShapeDtypeStruct((groups * GROUP, GROUP), F32),
        ),
        in_specs=[anywhere, anywhere],
        out_specs=(VMEM_SPEC, VMEM_SPEC, VMEM_SPEC),
        scratch_shapes=scratch + [dma((2, groups)), dma((copies,)), dma((copies,))],
        compiler_params=pltpu.CompilerParams(
            collective_id=1, has_side_effects=True, vmem_limit_bytes=60_000_000
        ),
        name="orthogonalize",
    )(basis, image)


STEP = 32
PIVOTS = 2


def factor_kernel(gram_ref, residual_ref, flat_ref, new_ref, factor_ref, coeffs_ref, work_ref, held, in_sem, out_sem):
    groups = gram_ref.shape[0]
    fetch = pltpu.make_async_copy(flat_ref, held, in_sem)
    fetch.start()
    shape = (GROUP, GROUP)
    row_of = lax.broadcasted_iota(jnp.int32, shape, 0)
    lane_of = lax.broadcasted_iota(jnp.int32, shape, 1)
    eye = jnp.where(row_of == lane_of, 1.0, 0.0).astype(F32)
    for g in range(groups):
        work_ref[g, :, :GROUP] = gram_ref[g]
        work_ref[g, :, GROUP:] = eye
    lane = lax.broadcasted_iota(jnp.int32, (8, GROUP), 1)
    sub = lax.broadcasted_iota(jnp.int32, (8, GROUP), 0)
    stores = [
        pltpu.make_async_copy(held.at[g], coeffs_ref.at[:, g], out_sem.at[g]) for g in range(groups)
    ]
    count = STEP // 8
    for block in range(GROUP // STEP):
        if block == 1:
            fetch.wait()
            for store in stores:
                store.start()
        s = block * STEP
        o = (s + 64) % GROUP
        ones = [jnp.where(lane == o + 8 * t + sub, 1.0, 0.0).astype(F32) for t in range(count)]
        inside = (lane >= s) & (lane < s + STEP)
        panels = [
            [jnp.where(inside, work_ref[g, s + 8 * t : s + 8 * t + 8, :GROUP], ones[t]) for t in range(count)]
            for g in range(groups)
        ]
        for first in range(0, STEP, PIVOTS):
            at, within = first // 8, first % 8
            for tiles in panels:
                columns = {
                    t: [
                        jnp.broadcast_to(tiles[t][:, s + first + q : s + first + q + 1], (8, GROUP))
                        for q in range(PIVOTS)
                    ]
                    for t in range(at, count)
                }
                for q in range(PIVOTS):
                    pivot = slice(within + q, within + q + 1)
                    inverse = 1.0 / columns[at][q][pivot]
                    scaled = tiles[at][pivot] * inverse
                    later = [columns[at][p][pivot] * inverse for p in range(q + 1, PIVOTS)]
                    for t in range(at, count):
                        column = columns[t][q]
                        if t == at:
                            column = jnp.where(sub > within + q, column, 0.0)
                        tiles[t] = tiles[t] - column * scaled
                        for p, value in zip(range(q + 1, PIVOTS), later):
                            columns[t][p] = columns[t][p] - column * value
        for g, tiles in enumerate(panels):
            for t in range(count):
                diagonal = jnp.sum(jnp.where(lane == s + 8 * t + sub, tiles[t], 0.0), axis=1, keepdims=True)
                tiles[t] = tiles[t] * (1.0 / jnp.sqrt(diagonal))
            inverse = jnp.concatenate(tiles, axis=0)[:, o : o + STEP]
            high = inverse.astype(BF16).astype(F32)
            left = jnp.concatenate([high, inverse - high, high], axis=1).astype(BF16)
            wh, wl = split(work_ref[g, s : s + STEP])
            rows = dot1(left, jnp.concatenate([wh, wh, wl], axis=0), 1, 0)
            work_ref[g, s : s + STEP] = rows
            if s + STEP < GROUP:
                rh, rl = split(rows)
                ah, al = rh[:, :GROUP], rl[:, :GROUP]
                update = dot1(jnp.concatenate([ah, al, ah], axis=0), jnp.concatenate([rh, rh, rl], axis=0), 0, 0)
                below = slice(s + STEP, GROUP)
                work_ref[g, below] = work_ref[g, below] - update[s + STEP :]
    for g in range(groups):
        factor_ref[g] = jnp.where(row_of >= lane_of, work_ref[g, :, :GROUP].T, 0.0)
        inverse = jnp.where(row_of >= lane_of, work_ref[g, :, GROUP:], 0.0)
        columns = slice(g * GROUP, (g + 1) * GROUP)
        nh, nl = split(inverse)
        weights = jnp.concatenate([beside(nh, nh), beside(nl, jnp.zeros_like(nl))], axis=0)
        both = dot1(beside(*split(residual_ref[:, columns])), weights, 1, 1)
        new_ref[:, columns] = both[:, :GROUP] + both[:, GROUP:]
    for store in stores:
        store.wait()


def factor_and_solve(gram, residual, flat_coeffs, count):
    groups = gram.shape[0]
    anywhere = pl.BlockSpec(memory_space=pl.ANY)
    shape = (groups, count, GROUP, GROUP)
    return pl.pallas_call(
        factor_kernel,
        out_shape=(
            jax.ShapeDtypeStruct(residual.shape, F32),
            jax.ShapeDtypeStruct(gram.shape, F32),
            jax.ShapeDtypeStruct((count, groups, GROUP, GROUP), F32),
        ),
        in_specs=[VMEM_SPEC, VMEM_SPEC, anywhere],
        out_specs=(VMEM_SPEC, VMEM_SPEC, anywhere),
        scratch_shapes=[
            pltpu.VMEM((groups, GROUP, 2 * GROUP), F32), pltpu.VMEM(shape, F32),
            pltpu.SemaphoreType.DMA(()), pltpu.SemaphoreType.DMA((groups,)),
        ],
        name="factor_and_solve",
    )(gram, residual, flat_coeffs.reshape(shape))


SLOTS = 7
SLOT_OFFSETS = (0, 1, -2, 2, -1, 3, -3)
SLOT_ORIGIN = (0, 1, 0, 0, 1, 1, 1)
CHUNKS = 4
ROWS = 256
PIECE = 128
TICKS = 8
AHEAD = 2
BLOCK = 128
NEAR = 25


def apply_kernel(
    index_ref, strips_ref, vector_ref, out_ref,
    high_ref, low_ref, window, stage_even, stage_odd, image, strip_sem, copy_sem, entry_recv, recv_sem, exit_recv, own_send, relay_send, entry_send,
    exit_send,
):
    blk, rhs = lax.axis_index("blk"), lax.axis_index("rhs")
    x_lo, core = rhs // 2, rhs % 2
    odd = blk % 2
    sign = 1 - 2 * odd

    def peer(t):
        return (x_lo + t // 2) % 2, (core + t % 2) % 2

    def quarter(at):
        return ((at[0] + odd) % 2) * 2 + at[1]

    def group_device(t):
        x, c = peer(t)
        return {"blk": blk, "rhs": x * 2 + c}

    ahead = {"blk": (blk + 32 + 2 * sign) % 32, "rhs": rhs}
    behind = {"blk": (blk + 32 - 2 * sign) % 32, "rhs": rhs}
    partner = {"blk": blk + sign, "rhs": (1 - x_lo) * 2 + core}
    columns = quarter((x_lo, core)) * (CHUNKS * GROUP)

    def entry_rows(chunk, n):
        x, c = peer(n)
        return window.at[chunk, 0, pl.ds((x * 2 + c) * ROWS, ROWS)]

    def piece(chunk, slot, t, source=None):
        x, c = peer(2 * SLOT_ORIGIN[slot if source is None else source] + t // 2)
        return window.at[chunk, slot, pl.ds((x * 2 + c) * ROWS + t % 2 * PIECE, PIECE)]

    def remote(src, dst, send, recv, device):
        return pltpu.make_async_remote_copy(
            src_ref=src, dst_ref=dst, send_sem=send, recv_sem=recv, device_id=device, device_id_type=MESH
        )

    def strip_copy(i, lane):
        stage = (stage_even, stage_odd)[lane]
        return pltpu.make_async_copy(strips_ref.at[i], stage.at[pl.ds(0, NEAR)], strip_sem.at[lane])

    def own_copy(chunk):
        cols = pl.ds(pl.multiple_of(columns + chunk * GROUP, GROUP), GROUP)
        return pltpu.make_async_copy(vector_ref.at[:, cols], entry_rows(chunk, 0), copy_sem.at[chunk])

    def entry_copy(chunk, t):
        cols = pl.ds(pl.multiple_of(quarter(peer(t)) * (CHUNKS * GROUP) + chunk * GROUP, GROUP), GROUP)
        return remote(
            vector_ref.at[:, cols], entry_rows(chunk, 0), entry_send.at[chunk, t - 1], entry_recv.at[chunk, t - 1],
            group_device(t),
        )

    def exit_copy(chunk, t):
        x, c = peer(t)
        cols = pl.ds(pl.multiple_of(columns + chunk * GROUP, GROUP), GROUP)
        return remote(
            image.at[chunk, pl.ds((x * 2 + c) * ROWS, ROWS)], out_ref.at[:, cols], exit_send.at[chunk, t - 1],
            exit_recv.at[chunk, t - 1], group_device(t),
        )

    def send_copy(chunk, t, way):
        slot, device = ((1, partner), (2, ahead), (3, behind))[way]
        return remote(
            piece(chunk, 0, t), piece(chunk, slot, t, 0), own_send.at[chunk, t, way], recv_sem.at[chunk, slot, t], device
        )

    def relay_copy(chunk, t, way):
        source, slot, device = ((1, 5, behind), (3, 4, partner), (4, 6, ahead))[way]
        return remote(
            piece(chunk, source, t), piece(chunk, slot, t, source), relay_send.at[chunk, t, way],
            recv_sem.at[chunk, slot, t], device,
        )

    def arrived(chunk, slot, t):
        at = piece(chunk, slot, t)
        remote(at, at, own_send.at[chunk, t, 0], recv_sem.at[chunk, slot, t], partner).wait_recv()

    def send_own(chunk, t):
        if t == 0:
            own_copy(chunk).wait()
        elif t % 2 == 0:
            at = entry_rows(chunk, t // 2)
            remote(at, at, entry_send.at[chunk, 0], entry_recv.at[chunk, t // 2 - 1], partner).wait_recv()
        for way in range(3):
            send_copy(chunk, t, way).start()

    def relay(chunk, t, way):
        arrived(chunk, (1, 3, 4)[way], t)
        relay_copy(chunk, t, way).start()

    def build(i, lane):
        stage = (stage_even, stage_odd)[lane]
        strip_copy(i, lane).wait()
        rows = slice(i * BLOCK, (i + 1) * BLOCK)

        def one_slot(slot, carry):
            for j in range(8):
                at = slot * 8 + j
                high, low = split(stage[index_ref[i, at]])
                high_ref[slot, rows, j * BLOCK : (j + 1) * BLOCK] = high
                low_ref[slot, rows, j * BLOCK : (j + 1) * BLOCK] = low
            return carry

        lax.fori_loop(0, SLOTS, one_slot, 0)

        if i + 2 < 8:
            strip_copy(i + 2, lane).start()

    def multiply(chunk, slot):
        high, low = split(window[chunk, slot])
        both = dot1(high_ref[slot], beside(high, low), 1, 0)
        rest = dot1(low_ref[slot], high, 1, 0)
        image[chunk] = image[chunk] + (both[:, :GROUP] + (both[:, GROUP:] + rest))

    def finish(chunk):
        cols = pl.ds(pl.multiple_of(columns + chunk * GROUP, GROUP), GROUP)
        out_ref[:, cols] = image[chunk, pl.ds(pl.multiple_of(rhs * ROWS, ROWS), ROWS)]
        for t in (3, 2, 1):
            exit_copy(chunk, t).start()

    def tick(chunk, t, first):
        now = True if first else chunk < CHUNKS
        back = chunk - 1

        def when(condition, action):
            if condition is True:
                action()
            else:
                pl.when(condition)(action)

        if t + AHEAD < TICKS:
            when(now, lambda: send_own(chunk, t + AHEAD))
        else:
            when(True if first else chunk + 1 < CHUNKS, lambda: send_own(chunk + 1, t + AHEAD - TICKS))
        for way, lag in ((0, 1), (1, 1), (2, 2)):
            if t >= lag:
                when(now, functools.partial(relay, chunk, t - lag, way))
            elif not first:
                relay(back, t - lag + TICKS, way)
        if t == TICKS - 1:
            when(now, lambda: multiply(chunk, 0))
        elif t and not first:
            if t in (2, 5, 6):
                for u in range(TICKS):
                    arrived(back, t, u)
            multiply(back, t)
            if t == SLOTS - 1:
                finish(back)

    for i in range(2):
        strip_copy(i, i).start()
    for chunk in range(CHUNKS):
        own_copy(chunk).start()

    barrier = pltpu.get_barrier_semaphore()
    for device in [partner, ahead, behind] + [group_device(t) for t in (1, 2, 3)]:
        pl.semaphore_signal(barrier, inc=1, device_id=device, device_id_type=MESH)
    pl.semaphore_wait(barrier, 6)

    for chunk in range(CHUNKS):
        for t in (2, 3, 1):
            entry_copy(chunk, t).start()
    for t in range(AHEAD):
        send_own(0, t)
    image[...] = jnp.zeros_like(image)
    for stage in (stage_even, stage_odd):
        stage[NEAR] = jnp.zeros_like(stage[NEAR])
    for t in range(TICKS):
        if t == TICKS - 1:
            build(t, t % 2)
        tick(0, t, True)
        if t < TICKS - 1:
            build(t, t % 2)

    def body(chunk, carry):
        for t in range(TICKS):
            tick(chunk, t, False)
        return carry

    lax.fori_loop(1, CHUNKS + 1, body, 0)

    def drain(chunk, carry):
        for t in (1, 2, 3):
            exit_copy(chunk, t).wait_recv()
            exit_copy(chunk, t).wait_send()
            entry_copy(chunk, t).wait_send()
        for t in range(TICKS):
            for way in range(3):
                send_copy(chunk, t, way).wait_send()
                relay_copy(chunk, t, way).wait_send()
        return carry

    lax.fori_loop(0, CHUNKS, drain, 0)


def place_kernel(total, near_ref, index_ref):
    blocks = near_ref.shape[0]
    blk = lax.axis_index("blk")
    sign = 1 - 2 * (blk % 2)
    at = lax.broadcasted_iota(jnp.int32, index_ref.shape, 1)
    offset = jnp.zeros(index_ref.shape, jnp.int32)
    for slot, by in enumerate(SLOT_OFFSETS):
        offset = jnp.where((at >= slot * blocks) & (at < (slot + 1) * blocks), by * sign * blocks + at - slot * blocks, offset)
    offset = jnp.where(offset < 0, offset + total, offset)
    relative = near_ref[...] - blk * blocks
    relative = jnp.where(relative < 0, relative + total, relative)
    index = jnp.full(index_ref.shape, NEAR, jnp.int32)
    for k in range(NEAR):
        index = jnp.where(relative[:, k : k + 1] == offset, k, index)
    index_ref[...] = index


def apply_near_field(strips, near_cols, vector_block):
    blocks, near = near_cols.shape
    total = blocks * lax.axis_size("blk")
    index = pl.pallas_call(
        functools.partial(place_kernel, total),
        out_shape=jax.ShapeDtypeStruct((blocks, SLOTS * blocks), jnp.int32),
        in_specs=[VMEM_SPEC],
        out_specs=VMEM_SPEC,
        name="place_strips",
    )(near_cols)
    rows, width = vector_block.shape
    smem = pl.BlockSpec(memory_space=pltpu.SMEM)
    anywhere = pl.BlockSpec(memory_space=pl.ANY)
    dma = pltpu.SemaphoreType.DMA
    size = blocks * BLOCK
    return pl.pallas_call(
        apply_kernel,
        out_shape=jax.ShapeDtypeStruct((rows, width), F32),
        in_specs=[smem, anywhere, anywhere],
        out_specs=VMEM_SPEC,
        scratch_shapes=[
            pltpu.VMEM((SLOTS, size, size), BF16),
            pltpu.VMEM((SLOTS, size, size), BF16),
            pltpu.VMEM((CHUNKS, SLOTS, size, GROUP), F32),
            pltpu.VMEM((near + 1, BLOCK, BLOCK), F32),
            pltpu.VMEM((near + 1, BLOCK, BLOCK), F32),
            pltpu.VMEM((CHUNKS, size, GROUP), F32),
            dma((2,)), dma((CHUNKS,)), dma((CHUNKS, 3)), dma((CHUNKS, SLOTS, TICKS)), dma((CHUNKS, 3)),
            dma((CHUNKS, TICKS, 3)), dma((CHUNKS, TICKS, 3)), dma((CHUNKS, 3)), dma((CHUNKS, 3)),
        ],
        compiler_params=pltpu.CompilerParams(
            collective_id=3, has_side_effects=True, vmem_limit_bytes=64_000_000
        ),
        name="apply_near_field",
    )(index, strips, vector_block)


def local(strips, near_cols, vector_block, basis):
    image = apply_near_field(strips, near_cols, vector_block)
    flat_coeffs, residual, gram = orthogonalize(basis, image)
    gram = gram.reshape(-1, GROUP, GROUP)
    new_block, factor, coeffs = factor_and_solve(gram, residual, flat_coeffs, basis.shape[0])
    return (new_block, coeffs, factor)


def solution(mesh):
    placed = (
        P("blk", None, None, None),
        P("blk", None),
        P(("blk", "rhs"), None),
        P(None, ("blk", "rhs"), None),
    )
    return jax.shard_map(
        local,
        mesh=mesh,
        in_specs=placed,
        out_specs=(P(("blk", "rhs"), None), P(), P()),
        check_vma=False,
    )
```

```python
import functools

import jax
import jax.numpy as jnp
from jax import lax
from jax.experimental import pallas as pl
from jax.experimental.pallas import tpu as pltpu
from jax.sharding import PartitionSpec as P

HOPS = 3
GROUP = 128
MESH = pl.DeviceIdType.MESH
BF16, F32 = jnp.bfloat16, jnp.float32
VMEM_SPEC = pl.BlockSpec(memory_space=pltpu.VMEM)


def split(value):
    high = value.astype(BF16)
    low = (value - high.astype(F32)).astype(BF16)
    return high, low


def dot1(a, b, ca, cb):
    return lax.dot_general(a, b, (((ca,), (cb,)), ((), ())), preferred_element_type=F32)


ORDERS = ((0, 1, 2), (1, 2, 0), (2, 0, 1))


def coordinates():
    blk, rhs = lax.axis_index("blk"), lax.axis_index("rhs")
    x = (blk % 2) * 2 + rhs // 2
    return (x, blk // 8, (blk // 2) % 4), rhs % 2


def device_of(place, core):
    x, y, z = place
    return {"blk": (y * 4 + z) * 2 + x // 2, "rhs": (x % 2) * 2 + core}


def moved(place, axis, by):
    at = list(place)
    at[axis] = (at[axis] + by) % 4
    return tuple(at)


COEFF_SHARES = (24, 24, 16)
GRAM_SHARES = (8, 8)
HALF = 8


def beside(high, low):
    return jnp.concatenate([high, low], axis=1)


def orthogonalize_kernel(
    basis_ref, image_ref, coeffs_ref, residual_ref, gram_ref, basis_in, image_in, coeffs_part, gram_part, *rest
):
    coeff_count, gram_count = len(COEFF_SHARES), len(GRAM_SHARES)
    rest = list(rest)

    def take(count):
        taken = rest[:count]
        del rest[:count]
        return taken

    buffers = {}
    for key, count in (("coeffs", coeff_count), ("gram", gram_count)):
        buffers[key] = (take(1)[0], take(3 * count), take(2 * count))
    load_sem, send_sem, recv_sem = rest
    count = basis_ref.shape[0]
    depth = count * GROUP
    place, core = coordinates()
    partner = device_of(place, 1 - core)
    peers = [device_of(moved(place, axis, by), core) for axis in range(3) for by in (1, 2, 3)]
    own_first, other_first = core * HALF, (1 - core) * HALF

    def loads(g):
        columns = pl.ds(pl.multiple_of(g * GROUP, GROUP), GROUP)
        return (
            pltpu.make_async_copy(basis_ref.at[:, :, columns], basis_in.at[g], load_sem.at[0, g]),
            pltpu.make_async_copy(image_ref.at[:, columns], image_in.at[g], load_sem.at[1, g]),
        )

    def start_loads(i, first):
        for load in loads(first + i):
            load.start()
        return first

    lax.fori_loop(0, HALF, start_loads, other_first)
    lax.fori_loop(0, HALF, start_loads, own_first)

    barrier = pltpu.get_barrier_semaphore()
    for peer in [partner] + peers:
        pl.semaphore_signal(barrier, inc=1, device_id=peer, device_id_type=MESH)

    pending = []

    def copy(src, dst, device):
        at = len(pending)
        made = pltpu.make_async_remote_copy(
            src_ref=src, dst_ref=dst, send_sem=send_sem.at[at], recv_sem=recv_sem.at[at],
            device_id=device, device_id_type=MESH,
        )
        made.start()
        pending.append(made)
        return made

    def basis_halves(g):
        return split(jnp.concatenate([basis_in[g, m] for m in range(count)], axis=1))

    def local_coeffs(i, first):
        g = first + i
        for load in loads(g):
            load.wait()
        ih, il = split(image_in[g])
        bh, bl = basis_halves(g)
        both = dot1(bh, beside(ih, il), 0, 0)
        value = both[:, :GROUP] + (both[:, GROUP:] + dot1(bl, ih, 0, 0))
        coeffs_part[pl.ds(pl.multiple_of(g * depth, depth), depth)] = value
        return first

    def local_residual(i, first):
        g = first + i
        bh, bl = basis_halves(g)
        ch, cl = split(coeffs_ref[pl.ds(pl.multiple_of(g * depth, depth), depth)])
        both = dot1(bh, beside(ch, cl), 1, 0)
        value = image_in[g] - (both[:, :GROUP] + (both[:, GROUP:] + dot1(bl, ch, 1, 0)))
        residual_ref[:, pl.ds(pl.multiple_of(g * GROUP, GROUP), GROUP)] = value
        rh, rl = split(value)
        square = dot1(rh, beside(rh, rl), 0, 0)
        cross = square[:, GROUP:]
        gram_part[pl.ds(pl.multiple_of(g * GROUP, GROUP), GROUP)] = square[:, :GROUP] + (cross + cross.T)
        return first

    def bounds(shares):
        ends = [0]
        for share in shares:
            ends.append(ends[-1] + 64 * share)
        return ends

    def swap(key, shares, part_ref, part):
        ends = bounds(shares)
        size = ends[part + 1] - ends[part]
        start = (1 - core) * ends[-1] + ends[part]
        return copy(part_ref.at[pl.ds(start, size)], buffers[key][0].at[pl.ds(ends[part], size)], partner)

    def scatter(key, shares, source, part, stage):
        axis = ORDERS[part][stage]
        size = shares[part] * 4 ** (2 - stage)
        got = buffers[key][1][3 * part + stage]
        return [
            copy(
                source.at[pl.ds((place[axis] + by) % 4 * size, size)], got.at[by - 1],
                device_of(moved(place, axis, by), core),
            )
            for by in (1, 2, 3)
        ]

    def begin(key, shares, part_ref, part, swapped):
        ends = bounds(shares)
        size = ends[part + 1] - ends[part]
        mine = core * ends[-1] + ends[part]
        swapped.wait_recv()
        from_core = buffers[key][0]
        rows = pl.ds(ends[part], size)
        from_core[rows] = from_core[rows] + part_ref[pl.ds(mine, size)]
        source = from_core.at[rows]
        return source, scatter(key, shares, source, part, 0)

    def offset(shares, part, stages):
        ends = bounds(shares)
        at = core * ends[-1] + ends[part]
        for stage in range(stages):
            at = at + place[ORDERS[part][stage]] * (shares[part] * 4 ** (2 - stage))
        return at

    def gather(shares, out_ref, part, stage):
        axis = ORDERS[part][stage]
        size = shares[part] * 4 ** (2 - stage)
        rows = out_ref.at[pl.ds(offset(shares, part, stage + 1), size)]
        return [copy(rows, rows, device_of(moved(place, axis, by), core)) for by in (1, 2, 3)]

    def arrive(copies):
        for made in copies:
            made.wait_recv()

    def sum_up(key, shares, begun, out_ref):
        live = dict(enumerate(begun))
        for stage in range(3):
            for part, share in enumerate(shares):
                source, copies = live[part]
                arrive(copies)
                axis = ORDERS[part][stage]
                size = share * 4 ** (2 - stage)
                got = buffers[key][1][3 * part + stage]
                value = source[pl.ds(place[axis] * size, size)] + got[0] + got[1] + got[2]
                if stage < 2:
                    acc = buffers[key][2][2 * part + stage]
                    acc[...] = value
                    live[part] = (acc, scatter(key, shares, acc, part, stage + 1))
                else:
                    out_ref[pl.ds(offset(shares, part, 3), share)] = value
                    live[part] = gather(shares, out_ref, part, 2)
        for stage in (2, 1, 0):
            for part in range(len(shares)):
                arrive(live[part])
                if stage:
                    live[part] = gather(shares, out_ref, part, stage - 1)
                else:
                    yield part

    def give(shares, out_ref, part):
        ends = bounds(shares)
        rows = out_ref.at[pl.ds(core * ends[-1] + ends[part], ends[part + 1] - ends[part])]
        return copy(rows, rows, partner)

    spans = [(end // depth, last // depth) for end, last in zip(bounds(COEFF_SHARES), bounds(COEFF_SHARES)[1:])]
    swapped = []
    for part, (low, high) in enumerate(spans):
        lax.fori_loop(low, high, local_coeffs, other_first)
        if part == 0:
            pl.semaphore_wait(barrier, 10)
        swapped.append(swap("coeffs", COEFF_SHARES, coeffs_part, part))
    begun = []
    for part, (low, high) in enumerate(spans):
        lax.fori_loop(low, high, local_coeffs, own_first)
        begun.append(begin("coeffs", COEFF_SHARES, coeffs_part, part, swapped[part]))
    given = []
    for part in sum_up("coeffs", COEFF_SHARES, begun, coeffs_ref):
        given.append(give(COEFF_SHARES, coeffs_ref, part))
        lax.fori_loop(*spans[part], local_residual, own_first)

    swapped = []
    for part, (low, high) in enumerate(spans):
        given[part].wait_recv()
        lax.fori_loop(low, high, local_residual, other_first)
        if part:
            swapped.append(swap("gram", GRAM_SHARES, gram_part, part - 1))
    begun = [begin("gram", GRAM_SHARES, gram_part, part, swapped[part]) for part in range(gram_count)]
    given = [give(GRAM_SHARES, gram_ref, part) for part in sum_up("gram", GRAM_SHARES, begun, gram_ref)]
    arrive(given)
    for made in pending:
        made.wait_send()


def orthogonalize(basis, image):
    count, rows, width = basis.shape
    groups = width // GROUP
    scratch = [
        pltpu.VMEM((groups, count, rows, GROUP), F32),
        pltpu.VMEM((groups, rows, GROUP), F32),
        pltpu.VMEM((groups * count * GROUP, GROUP), F32),
        pltpu.VMEM((groups * GROUP, GROUP), F32),
    ]
    copies = 0
    for shares in (COEFF_SHARES, GRAM_SHARES):
        scratch.append(pltpu.VMEM((64 * sum(shares), GROUP), F32))
        for share in shares:
            scratch += [pltpu.VMEM((3, share * 4 ** (2 - stage), GROUP), F32) for stage in range(3)]
        for share in shares:
            scratch += [pltpu.VMEM((share * 4 ** (2 - stage), GROUP), F32) for stage in range(2)]
        copies += 20 * len(shares)
    dma = pltpu.SemaphoreType.DMA
    anywhere = pl.BlockSpec(memory_space=pl.ANY)
    return pl.pallas_call(
        orthogonalize_kernel,
        out_shape=(
            jax.ShapeDtypeStruct((groups * count * GROUP, GROUP), F32),
            jax.ShapeDtypeStruct((rows, width), F32),
            jax.ShapeDtypeStruct((groups * GROUP, GROUP), F32),
        ),
        in_specs=[anywhere, anywhere],
        out_specs=(VMEM_SPEC, VMEM_SPEC, VMEM_SPEC),
        scratch_shapes=scratch + [dma((2, groups)), dma((copies,)), dma((copies,))],
        compiler_params=pltpu.CompilerParams(
            collective_id=1, has_side_effects=True, vmem_limit_bytes=60_000_000
        ),
        name="orthogonalize",
    )(basis, image)


STEP = 32
PIVOTS = 2


def factor_kernel(gram_ref, residual_ref, flat_ref, new_ref, factor_ref, coeffs_ref, work_ref, held, in_sem, out_sem):
    groups = gram_ref.shape[0]
    fetch = pltpu.make_async_copy(flat_ref, held, in_sem)
    fetch.start()
    shape = (GROUP, GROUP)
    row_of = lax.broadcasted_iota(jnp.int32, shape, 0)
    lane_of = lax.broadcasted_iota(jnp.int32, shape, 1)
    eye = jnp.where(row_of == lane_of, 1.0, 0.0).astype(F32)
    for g in range(groups):
        work_ref[g, :, :GROUP] = gram_ref[g]
        work_ref[g, :, GROUP:] = eye
    lane = lax.broadcasted_iota(jnp.int32, (8, GROUP), 1)
    sub = lax.broadcasted_iota(jnp.int32, (8, GROUP), 0)
    stores = [
        pltpu.make_async_copy(held.at[g], coeffs_ref.at[:, g], out_sem.at[g]) for g in range(groups)
    ]
    count = STEP // 8
    for block in range(GROUP // STEP):
        if block == 1:
            fetch.wait()
            for store in stores:
                store.start()
        s = block * STEP
        o = (s + 64) % GROUP
        ones = [jnp.where(lane == o + 8 * t + sub, 1.0, 0.0).astype(F32) for t in range(count)]
        inside = (lane >= s) & (lane < s + STEP)
        panels = [
            [jnp.where(inside, work_ref[g, s + 8 * t : s + 8 * t + 8, :GROUP], ones[t]) for t in range(count)]
            for g in range(groups)
        ]
        for first in range(0, STEP, PIVOTS):
            at, within = first // 8, first % 8
            for tiles in panels:
                columns = {
                    t: [
                        jnp.broadcast_to(tiles[t][:, s + first + q : s + first + q + 1], (8, GROUP))
                        for q in range(PIVOTS)
                    ]
                    for t in range(at, count)
                }
                for q in range(PIVOTS):
                    pivot = slice(within + q, within + q + 1)
                    inverse = 1.0 / columns[at][q][pivot]
                    scaled = tiles[at][pivot] * inverse
                    later = [columns[at][p][pivot] * inverse for p in range(q + 1, PIVOTS)]
                    for t in range(at, count):
                        column = columns[t][q]
                        if t == at:
                            column = jnp.where(sub > within + q, column, 0.0)
                        tiles[t] = tiles[t] - column * scaled
                        for p, value in zip(range(q + 1, PIVOTS), later):
                            columns[t][p] = columns[t][p] - column * value
        for g, tiles in enumerate(panels):
            for t in range(count):
                diagonal = jnp.sum(jnp.where(lane == s + 8 * t + sub, tiles[t], 0.0), axis=1, keepdims=True)
                tiles[t] = tiles[t] * (1.0 / jnp.sqrt(diagonal))
            inverse = jnp.concatenate(tiles, axis=0)[:, o : o + STEP]
            high = inverse.astype(BF16).astype(F32)
            left = jnp.concatenate([high, inverse - high, high], axis=1).astype(BF16)
            wh, wl = split(work_ref[g, s : s + STEP])
            rows = dot1(left, jnp.concatenate([wh, wh, wl], axis=0), 1, 0)
            work_ref[g, s : s + STEP] = rows
            if s + STEP < GROUP:
                rh, rl = split(rows)
                ah, al = rh[:, :GROUP], rl[:, :GROUP]
                update = dot1(jnp.concatenate([ah, al, ah], axis=0), jnp.concatenate([rh, rh, rl], axis=0), 0, 0)
                below = slice(s + STEP, GROUP)
                work_ref[g, below] = work_ref[g, below] - update[s + STEP :]
    for g in range(groups):
        factor_ref[g] = jnp.where(row_of >= lane_of, work_ref[g, :, :GROUP].T, 0.0)
        inverse = jnp.where(row_of >= lane_of, work_ref[g, :, GROUP:], 0.0)
        columns = slice(g * GROUP, (g + 1) * GROUP)
        nh, nl = split(inverse)
        weights = jnp.concatenate([beside(nh, nh), beside(nl, jnp.zeros_like(nl))], axis=0)
        both = dot1(beside(*split(residual_ref[:, columns])), weights, 1, 1)
        new_ref[:, columns] = both[:, :GROUP] + both[:, GROUP:]
    for store in stores:
        store.wait()


def factor_and_solve(gram, residual, flat_coeffs, count):
    groups = gram.shape[0]
    anywhere = pl.BlockSpec(memory_space=pl.ANY)
    shape = (groups, count, GROUP, GROUP)
    return pl.pallas_call(
        factor_kernel,
        out_shape=(
            jax.ShapeDtypeStruct(residual.shape, F32),
            jax.ShapeDtypeStruct(gram.shape, F32),
            jax.ShapeDtypeStruct((count, groups, GROUP, GROUP), F32),
        ),
        in_specs=[VMEM_SPEC, VMEM_SPEC, anywhere],
        out_specs=(VMEM_SPEC, VMEM_SPEC, anywhere),
        scratch_shapes=[
            pltpu.VMEM((groups, GROUP, 2 * GROUP), F32), pltpu.VMEM(shape, F32),
            pltpu.SemaphoreType.DMA(()), pltpu.SemaphoreType.DMA((groups,)),
        ],
        name="factor_and_solve",
    )(gram, residual, flat_coeffs.reshape(shape))


SLOTS = 7
SLOT_OFFSETS = (0, 1, -2, 2, -1, 3, -3)
SLOT_ORIGIN = (0, 1, 0, 0, 1, 1, 1)
CHUNKS = 4
ROWS = 256
PIECE = 256
TICKS = 4
AHEAD = 1
PLAN = ((1, 2), (3,), (4, 5), (6,))
BLOCK = 128
NEAR = 25


def apply_kernel(
    index_ref, strips_ref, vector_ref, out_ref,
    high_ref, low_ref, window, stage_even, stage_odd, image, strip_sem, copy_sem, entry_recv, recv_sem, exit_recv, own_send, relay_send, entry_send,
    exit_send,
):
    blk, rhs = lax.axis_index("blk"), lax.axis_index("rhs")
    x_lo, core = rhs // 2, rhs % 2
    odd = blk % 2
    sign = 1 - 2 * odd

    def peer(t):
        return (x_lo + t // 2) % 2, (core + t % 2) % 2

    def quarter(at):
        return ((at[0] + odd) % 2) * 2 + at[1]

    def group_device(t):
        x, c = peer(t)
        return {"blk": blk, "rhs": x * 2 + c}

    ahead = {"blk": (blk + 32 + 2 * sign) % 32, "rhs": rhs}
    behind = {"blk": (blk + 32 - 2 * sign) % 32, "rhs": rhs}
    partner = {"blk": blk + sign, "rhs": (1 - x_lo) * 2 + core}
    columns = quarter((x_lo, core)) * (CHUNKS * GROUP)

    def entry_rows(chunk, n):
        x, c = peer(n)
        return window.at[chunk, 0, pl.ds((x * 2 + c) * ROWS, ROWS)]

    def piece(chunk, slot, t, source=None):
        x, c = peer(2 * SLOT_ORIGIN[slot if source is None else source] + t)
        return window.at[chunk, slot, pl.ds((x * 2 + c) * PIECE, PIECE)]

    def remote(src, dst, send, recv, device):
        return pltpu.make_async_remote_copy(
            src_ref=src, dst_ref=dst, send_sem=send, recv_sem=recv, device_id=device, device_id_type=MESH
        )

    def strip_copy(i, lane):
        stage = (stage_even, stage_odd)[lane]
        return pltpu.make_async_copy(strips_ref.at[i], stage.at[pl.ds(0, NEAR)], strip_sem.at[lane])

    def own_copy(chunk):
        cols = pl.ds(pl.multiple_of(columns + chunk * GROUP, GROUP), GROUP)
        return pltpu.make_async_copy(vector_ref.at[:, cols], entry_rows(chunk, 0), copy_sem.at[chunk])

    def entry_copy(chunk, t):
        cols = pl.ds(pl.multiple_of(quarter(peer(t)) * (CHUNKS * GROUP) + chunk * GROUP, GROUP), GROUP)
        return remote(
            vector_ref.at[:, cols], entry_rows(chunk, 0), entry_send.at[chunk, t - 1], entry_recv.at[chunk, t - 1],
            group_device(t),
        )

    def exit_copy(chunk, t):
        x, c = peer(t)
        cols = pl.ds(pl.multiple_of(columns + chunk * GROUP, GROUP), GROUP)
        return remote(
            image.at[chunk, pl.ds((x * 2 + c) * ROWS, ROWS)], out_ref.at[:, cols], exit_send.at[chunk, t - 1],
            exit_recv.at[chunk, t - 1], group_device(t),
        )

    def send_copy(chunk, t, way):
        slot, device = ((1, partner), (2, ahead), (3, behind))[way]
        return remote(
            piece(chunk, 0, t), piece(chunk, slot, t, 0), own_send.at[chunk, t, way], recv_sem.at[chunk, slot, t], device
        )

    def relay_copy(chunk, t, way):
        source, slot, device = ((1, 5, behind), (3, 4, partner), (4, 6, ahead))[way]
        return remote(
            piece(chunk, source, t), piece(chunk, slot, t, source), relay_send.at[chunk, t, way],
            recv_sem.at[chunk, slot, t], device,
        )

    def arrived(chunk, slot, t):
        at = piece(chunk, slot, t)
        remote(at, at, own_send.at[chunk, t, 0], recv_sem.at[chunk, slot, t], partner).wait_recv()

    def send_own(chunk, t):
        if t == 0:
            own_copy(chunk).wait()
        else:
            at = entry_rows(chunk, t)
            remote(at, at, entry_send.at[chunk, 0], entry_recv.at[chunk, t - 1], partner).wait_recv()
        for way in range(3):
            send_copy(chunk, t, way).start()

    def relay(chunk, t, way):
        arrived(chunk, (1, 3, 4)[way], t)
        relay_copy(chunk, t, way).start()

    def build(i, lane):
        stage = (stage_even, stage_odd)[lane]
        strip_copy(i, lane).wait()
        rows = slice(i * BLOCK, (i + 1) * BLOCK)

        def one_slot(slot, carry):
            for j in range(8):
                at = slot * 8 + j
                high, low = split(stage[index_ref[i, at]])
                high_ref[slot, rows, j * BLOCK : (j + 1) * BLOCK] = high
                low_ref[slot, rows, j * BLOCK : (j + 1) * BLOCK] = low
            return carry

        lax.fori_loop(0, SLOTS, one_slot, 0)

        if i + 2 < 8:
            strip_copy(i + 2, lane).start()

    def multiply(chunk, slot):
        high, low = split(window[chunk, slot])
        both = dot1(high_ref[slot], beside(high, low), 1, 0)
        rest = dot1(low_ref[slot], high, 1, 0)
        image[chunk] = image[chunk] + (both[:, :GROUP] + (both[:, GROUP:] + rest))

    def finish(chunk):
        cols = pl.ds(pl.multiple_of(columns + chunk * GROUP, GROUP), GROUP)
        out_ref[:, cols] = image[chunk, pl.ds(pl.multiple_of(rhs * ROWS, ROWS), ROWS)]
        for t in (3, 2, 1):
            exit_copy(chunk, t).start()

    def tick(chunk, t, first):
        now = True if first else chunk < CHUNKS
        back = chunk - 1

        def when(condition, action):
            if condition is True:
                action()
            else:
                pl.when(condition)(action)

        if t + AHEAD < TICKS:
            when(now, lambda: send_own(chunk, t + AHEAD))
        else:
            when(True if first else chunk + 1 < CHUNKS, lambda: send_own(chunk + 1, t + AHEAD - TICKS))
        for way, lag in ((0, 1), (1, 1), (2, 2)):
            if t >= lag:
                when(now, functools.partial(relay, chunk, t - lag, way))
            elif not first:
                relay(back, t - lag + TICKS, way)
        if not first:
            for slot in PLAN[t]:
                if slot in (2, 5, 6):
                    for u in range(TICKS):
                        arrived(back, slot, u)
                multiply(back, slot)
                if slot == SLOTS - 1:
                    finish(back)
        if t == TICKS - 1:
            when(now, lambda: multiply(chunk, 0))

    for i in range(2):
        strip_copy(i, i).start()
    for chunk in range(CHUNKS):
        own_copy(chunk).start()

    barrier = pltpu.get_barrier_semaphore()
    for device in [partner, ahead, behind] + [group_device(t) for t in (1, 2, 3)]:
        pl.semaphore_signal(barrier, inc=1, device_id=device, device_id_type=MESH)
    pl.semaphore_wait(barrier, 6)

    for chunk in range(CHUNKS):
        for t in (2, 3, 1):
            entry_copy(chunk, t).start()
    for t in range(AHEAD):
        send_own(0, t)
    image[...] = jnp.zeros_like(image)
    for stage in (stage_even, stage_odd):
        stage[NEAR] = jnp.zeros_like(stage[NEAR])
    for t in range(TICKS):
        rows = range(t * 8 // TICKS, (t + 1) * 8 // TICKS)
        if t == TICKS - 1:
            for i in rows:
                build(i, i % 2)
        tick(0, t, True)
        if t < TICKS - 1:
            for i in rows:
                build(i, i % 2)

    def body(chunk, carry):
        for t in range(TICKS):
            tick(chunk, t, False)
        return carry

    lax.fori_loop(1, CHUNKS + 1, body, 0)

    def drain(chunk, carry):
        for t in (1, 2, 3):
            exit_copy(chunk, t).wait_recv()
            exit_copy(chunk, t).wait_send()
            entry_copy(chunk, t).wait_send()
        for t in range(TICKS):
            for way in range(3):
                send_copy(chunk, t, way).wait_send()
                relay_copy(chunk, t, way).wait_send()
        return carry

    lax.fori_loop(0, CHUNKS, drain, 0)


def place_kernel(total, near_ref, index_ref):
    blocks = near_ref.shape[0]
    blk = lax.axis_index("blk")
    sign = 1 - 2 * (blk % 2)
    at = lax.broadcasted_iota(jnp.int32, index_ref.shape, 1)
    offset = jnp.zeros(index_ref.shape, jnp.int32)
    for slot, by in enumerate(SLOT_OFFSETS):
        offset = jnp.where((at >= slot * blocks) & (at < (slot + 1) * blocks), by * sign * blocks + at - slot * blocks, offset)
    offset = jnp.where(offset < 0, offset + total, offset)
    relative = near_ref[...] - blk * blocks
    relative = jnp.where(relative < 0, relative + total, relative)
    index = jnp.full(index_ref.shape, NEAR, jnp.int32)
    for k in range(NEAR):
        index = jnp.where(relative[:, k : k + 1] == offset, k, index)
    index_ref[...] = index


def apply_near_field(strips, near_cols, vector_block):
    blocks, near = near_cols.shape
    total = blocks * lax.axis_size("blk")
    index = pl.pallas_call(
        functools.partial(place_kernel, total),
        out_shape=jax.ShapeDtypeStruct((blocks, SLOTS * blocks), jnp.int32),
        in_specs=[VMEM_SPEC],
        out_specs=VMEM_SPEC,
        name="place_strips",
    )(near_cols)
    rows, width = vector_block.shape
    smem = pl.BlockSpec(memory_space=pltpu.SMEM)
    anywhere = pl.BlockSpec(memory_space=pl.ANY)
    dma = pltpu.SemaphoreType.DMA
    size = blocks * BLOCK
    return pl.pallas_call(
        apply_kernel,
        out_shape=jax.ShapeDtypeStruct((rows, width), F32),
        in_specs=[smem, anywhere, anywhere],
        out_specs=VMEM_SPEC,
        scratch_shapes=[
            pltpu.VMEM((SLOTS, size, size), BF16),
            pltpu.VMEM((SLOTS, size, size), BF16),
            pltpu.VMEM((CHUNKS, SLOTS, size, GROUP), F32),
            pltpu.VMEM((near + 1, BLOCK, BLOCK), F32),
            pltpu.VMEM((near + 1, BLOCK, BLOCK), F32),
            pltpu.VMEM((CHUNKS, size, GROUP), F32),
            dma((2,)), dma((CHUNKS,)), dma((CHUNKS, 3)), dma((CHUNKS, SLOTS, TICKS)), dma((CHUNKS, 3)),
            dma((CHUNKS, TICKS, 3)), dma((CHUNKS, TICKS, 3)), dma((CHUNKS, 3)), dma((CHUNKS, 3)),
        ],
        compiler_params=pltpu.CompilerParams(
            collective_id=3, has_side_effects=True, vmem_limit_bytes=64_000_000
        ),
        name="apply_near_field",
    )(index, strips, vector_block)


def local(strips, near_cols, vector_block, basis):
    image = apply_near_field(strips, near_cols, vector_block)
    flat_coeffs, residual, gram = orthogonalize(basis, image)
    gram = gram.reshape(-1, GROUP, GROUP)
    new_block, factor, coeffs = factor_and_solve(gram, residual, flat_coeffs, basis.shape[0])
    return (new_block, coeffs, factor)


def solution(mesh):
    placed = (
        P("blk", None, None, None),
        P("blk", None),
        P(("blk", "rhs"), None),
        P(None, ("blk", "rhs"), None),
    )
    return jax.shard_map(
        local,
        mesh=mesh,
        in_specs=placed,
        out_specs=(P(("blk", "rhs"), None), P(), P()),
        check_vma=False,
    )
```

```python
import functools

import jax
import jax.numpy as jnp
from jax import lax
from jax.experimental import pallas as pl
from jax.experimental.pallas import tpu as pltpu
from jax.sharding import PartitionSpec as P

HOPS = 3
GROUP = 128
MESH = pl.DeviceIdType.MESH
BF16, F32 = jnp.bfloat16, jnp.float32
VMEM_SPEC = pl.BlockSpec(memory_space=pltpu.VMEM)


def split(value):
    high = value.astype(BF16)
    low = (value - high.astype(F32)).astype(BF16)
    return high, low


def dot1(a, b, ca, cb):
    return lax.dot_general(a, b, (((ca,), (cb,)), ((), ())), preferred_element_type=F32)


ORDERS = ((0, 1, 2), (1, 2, 0), (2, 0, 1))


def coordinates():
    blk, rhs = lax.axis_index("blk"), lax.axis_index("rhs")
    x = (blk % 2) * 2 + rhs // 2
    return (x, blk // 8, (blk // 2) % 4), rhs % 2


def device_of(place, core):
    x, y, z = place
    return {"blk": (y * 4 + z) * 2 + x // 2, "rhs": (x % 2) * 2 + core}


def moved(place, axis, by):
    at = list(place)
    at[axis] = (at[axis] + by) % 4
    return tuple(at)


COEFF_SHARES = (24, 24, 16)
GRAM_SHARES = (8, 8)
HALF = 8


def beside(high, low):
    return jnp.concatenate([high, low], axis=1)


def orthogonalize_kernel(
    basis_ref, image_ref, coeffs_ref, residual_ref, gram_ref, basis_in, image_in, coeffs_part, gram_part, *rest
):
    coeff_count, gram_count = len(COEFF_SHARES), len(GRAM_SHARES)
    rest = list(rest)

    def take(count):
        taken = rest[:count]
        del rest[:count]
        return taken

    buffers = {}
    for key, count in (("coeffs", coeff_count), ("gram", gram_count)):
        buffers[key] = (take(1)[0], take(3 * count), take(2 * count))
    load_sem, send_sem, recv_sem = rest
    count = basis_ref.shape[0]
    depth = count * GROUP
    place, core = coordinates()
    partner = device_of(place, 1 - core)
    peers = [device_of(moved(place, axis, by), core) for axis in range(3) for by in (1, 2, 3)]
    own_first, other_first = core * HALF, (1 - core) * HALF

    def loads(g):
        columns = pl.ds(pl.multiple_of(g * GROUP, GROUP), GROUP)
        return (
            pltpu.make_async_copy(basis_ref.at[:, :, columns], basis_in.at[g], load_sem.at[0, g]),
            pltpu.make_async_copy(image_ref.at[:, columns], image_in.at[g], load_sem.at[1, g]),
        )

    def start_loads(i, first):
        for load in loads(first + i):
            load.start()
        return first

    lax.fori_loop(0, HALF, start_loads, other_first)
    lax.fori_loop(0, HALF, start_loads, own_first)

    barrier = pltpu.get_barrier_semaphore()
    for peer in [partner] + peers:
        pl.semaphore_signal(barrier, inc=1, device_id=peer, device_id_type=MESH)

    pending = []

    def copy(src, dst, device):
        at = len(pending)
        made = pltpu.make_async_remote_copy(
            src_ref=src, dst_ref=dst, send_sem=send_sem.at[at], recv_sem=recv_sem.at[at],
            device_id=device, device_id_type=MESH,
        )
        made.start()
        pending.append(made)
        return made

    def basis_halves(g):
        return split(jnp.concatenate([basis_in[g, m] for m in range(count)], axis=1))

    def local_coeffs(i, first):
        g = first + i
        for load in loads(g):
            load.wait()
        ih, il = split(image_in[g])
        bh, bl = basis_halves(g)
        both = dot1(bh, beside(ih, il), 0, 0)
        value = both[:, :GROUP] + (both[:, GROUP:] + dot1(bl, ih, 0, 0))
        coeffs_part[pl.ds(pl.multiple_of(g * depth, depth), depth)] = value
        return first

    def local_residual(i, first):
        g = first + i
        bh, bl = basis_halves(g)
        ch, cl = split(coeffs_ref[pl.ds(pl.multiple_of(g * depth, depth), depth)])
        both = dot1(bh, beside(ch, cl), 1, 0)
        value = image_in[g] - (both[:, :GROUP] + (both[:, GROUP:] + dot1(bl, ch, 1, 0)))
        residual_ref[:, pl.ds(pl.multiple_of(g * GROUP, GROUP), GROUP)] = value
        rh, rl = split(value)
        square = dot1(rh, beside(rh, rl), 0, 0)
        cross = square[:, GROUP:]
        gram_part[pl.ds(pl.multiple_of(g * GROUP, GROUP), GROUP)] = square[:, :GROUP] + (cross + cross.T)
        return first

    def bounds(shares):
        ends = [0]
        for share in shares:
            ends.append(ends[-1] + 64 * share)
        return ends

    def swap(key, shares, part_ref, part):
        ends = bounds(shares)
        size = ends[part + 1] - ends[part]
        start = (1 - core) * ends[-1] + ends[part]
        return copy(part_ref.at[pl.ds(start, size)], buffers[key][0].at[pl.ds(ends[part], size)], partner)

    def scatter(key, shares, source, part, stage):
        axis = ORDERS[part][stage]
        size = shares[part] * 4 ** (2 - stage)
        got = buffers[key][1][3 * part + stage]
        return [
            copy(
                source.at[pl.ds((place[axis] + by) % 4 * size, size)], got.at[by - 1],
                device_of(moved(place, axis, by), core),
            )
            for by in (1, 2, 3)
        ]

    def begin(key, shares, part_ref, part, swapped):
        ends = bounds(shares)
        size = ends[part + 1] - ends[part]
        mine = core * ends[-1] + ends[part]
        swapped.wait_recv()
        from_core = buffers[key][0]
        rows = pl.ds(ends[part], size)
        from_core[rows] = from_core[rows] + part_ref[pl.ds(mine, size)]
        source = from_core.at[rows]
        return source, scatter(key, shares, source, part, 0)

    def offset(shares, part, stages):
        ends = bounds(shares)
        at = core * ends[-1] + ends[part]
        for stage in range(stages):
            at = at + place[ORDERS[part][stage]] * (shares[part] * 4 ** (2 - stage))
        return at

    def gather(shares, out_ref, part, stage):
        axis = ORDERS[part][stage]
        size = shares[part] * 4 ** (2 - stage)
        rows = out_ref.at[pl.ds(offset(shares, part, stage + 1), size)]
        return [copy(rows, rows, device_of(moved(place, axis, by), core)) for by in (1, 2, 3)]

    def arrive(copies):
        for made in copies:
            made.wait_recv()

    def sum_up(key, shares, begun, out_ref):
        live = dict(enumerate(begun))
        for stage in range(3):
            for part, share in enumerate(shares):
                source, copies = live[part]
                arrive(copies)
                axis = ORDERS[part][stage]
                size = share * 4 ** (2 - stage)
                got = buffers[key][1][3 * part + stage]
                value = source[pl.ds(place[axis] * size, size)] + got[0] + got[1] + got[2]
                if stage < 2:
                    acc = buffers[key][2][2 * part + stage]
                    acc[...] = value
                    live[part] = (acc, scatter(key, shares, acc, part, stage + 1))
                else:
                    out_ref[pl.ds(offset(shares, part, 3), share)] = value
                    live[part] = gather(shares, out_ref, part, 2)
        for stage in (2, 1, 0):
            for part in range(len(shares)):
                arrive(live[part])
                if stage:
                    live[part] = gather(shares, out_ref, part, stage - 1)
                else:
                    yield part

    def give(shares, out_ref, part):
        ends = bounds(shares)
        rows = out_ref.at[pl.ds(core * ends[-1] + ends[part], ends[part + 1] - ends[part])]
        return copy(rows, rows, partner)

    spans = [(end // depth, last // depth) for end, last in zip(bounds(COEFF_SHARES), bounds(COEFF_SHARES)[1:])]
    swapped = []
    for part, (low, high) in enumerate(spans):
        lax.fori_loop(low, high, local_coeffs, other_first, unroll=True)
        if part == 0:
            pl.semaphore_wait(barrier, 10)
        swapped.append(swap("coeffs", COEFF_SHARES, coeffs_part, part))
    begun = []
    for part, (low, high) in enumerate(spans):
        lax.fori_loop(low, high, local_coeffs, own_first, unroll=True)
        begun.append(begin("coeffs", COEFF_SHARES, coeffs_part, part, swapped[part]))
    given = []
    for part in sum_up("coeffs", COEFF_SHARES, begun, coeffs_ref):
        given.append(give(COEFF_SHARES, coeffs_ref, part))
        lax.fori_loop(*spans[part], local_residual, own_first, unroll=True)

    swapped = []
    for part, (low, high) in enumerate(spans):
        given[part].wait_recv()
        lax.fori_loop(low, high, local_residual, other_first, unroll=True)
        if part:
            swapped.append(swap("gram", GRAM_SHARES, gram_part, part - 1))
    begun = [begin("gram", GRAM_SHARES, gram_part, part, swapped[part]) for part in range(gram_count)]
    given = [give(GRAM_SHARES, gram_ref, part) for part in sum_up("gram", GRAM_SHARES, begun, gram_ref)]
    arrive(given)
    for made in pending:
        made.wait_send()


def orthogonalize(basis, image):
    count, rows, width = basis.shape
    groups = width // GROUP
    scratch = [
        pltpu.VMEM((groups, count, rows, GROUP), F32),
        pltpu.VMEM((groups, rows, GROUP), F32),
        pltpu.VMEM((groups * count * GROUP, GROUP), F32),
        pltpu.VMEM((groups * GROUP, GROUP), F32),
    ]
    copies = 0
    for shares in (COEFF_SHARES, GRAM_SHARES):
        scratch.append(pltpu.VMEM((64 * sum(shares), GROUP), F32))
        for share in shares:
            scratch += [pltpu.VMEM((3, share * 4 ** (2 - stage), GROUP), F32) for stage in range(3)]
        for share in shares:
            scratch += [pltpu.VMEM((share * 4 ** (2 - stage), GROUP), F32) for stage in range(2)]
        copies += 20 * len(shares)
    dma = pltpu.SemaphoreType.DMA
    anywhere = pl.BlockSpec(memory_space=pl.ANY)
    return pl.pallas_call(
        orthogonalize_kernel,
        out_shape=(
            jax.ShapeDtypeStruct((groups * count * GROUP, GROUP), F32),
            jax.ShapeDtypeStruct((rows, width), F32),
            jax.ShapeDtypeStruct((groups * GROUP, GROUP), F32),
        ),
        in_specs=[anywhere, anywhere],
        out_specs=(VMEM_SPEC, VMEM_SPEC, VMEM_SPEC),
        scratch_shapes=scratch + [dma((2, groups)), dma((copies,)), dma((copies,))],
        compiler_params=pltpu.CompilerParams(
            collective_id=1, has_side_effects=True, vmem_limit_bytes=60_000_000
        ),
        name="orthogonalize",
    )(basis, image)


STEP = 32
PIVOTS = 2


def factor_kernel(gram_ref, residual_ref, flat_ref, new_ref, factor_ref, coeffs_ref, work_ref, held, residual, new, in_sem, out_sem):
    groups = gram_ref.shape[0]
    fetch = pltpu.make_async_copy(flat_ref, held, in_sem.at[0])
    fetch.start()
    bring = pltpu.make_async_copy(residual_ref, residual, in_sem.at[1])
    bring.start()
    shape = (GROUP, GROUP)
    row_of = lax.broadcasted_iota(jnp.int32, shape, 0)
    lane_of = lax.broadcasted_iota(jnp.int32, shape, 1)
    eye = jnp.where(row_of == lane_of, 1.0, 0.0).astype(F32)
    for g in range(groups):
        work_ref[g, :, :GROUP] = gram_ref[g]
        work_ref[g, :, GROUP:] = eye
    lane = lax.broadcasted_iota(jnp.int32, (8, GROUP), 1)
    sub = lax.broadcasted_iota(jnp.int32, (8, GROUP), 0)
    stores = [
        pltpu.make_async_copy(held.at[g], coeffs_ref.at[:, g], out_sem.at[0, g]) for g in range(groups)
    ]
    count = STEP // 8
    for block in range(GROUP // STEP):
        if block == 1:
            fetch.wait()
            for store in stores:
                store.start()
        s = block * STEP
        o = (s + 64) % GROUP
        ones = [jnp.where(lane == o + 8 * t + sub, 1.0, 0.0).astype(F32) for t in range(count)]
        inside = (lane >= s) & (lane < s + STEP)
        panels = [
            [jnp.where(inside, work_ref[g, s + 8 * t : s + 8 * t + 8, :GROUP], ones[t]) for t in range(count)]
            for g in range(groups)
        ]
        for first in range(0, STEP, PIVOTS):
            at, within = first // 8, first % 8
            for tiles in panels:
                columns = {
                    t: [
                        jnp.broadcast_to(tiles[t][:, s + first + q : s + first + q + 1], (8, GROUP))
                        for q in range(PIVOTS)
                    ]
                    for t in range(at, count)
                }
                for q in range(PIVOTS):
                    pivot = slice(within + q, within + q + 1)
                    inverse = 1.0 / columns[at][q][pivot]
                    scaled = tiles[at][pivot] * inverse
                    later = [columns[at][p][pivot] * inverse for p in range(q + 1, PIVOTS)]
                    for t in range(at, count):
                        column = columns[t][q]
                        if t == at:
                            column = jnp.where(sub > within + q, column, 0.0)
                        tiles[t] = tiles[t] - column * scaled
                        for p, value in zip(range(q + 1, PIVOTS), later):
                            columns[t][p] = columns[t][p] - column * value
        for g, tiles in enumerate(panels):
            for t in range(count):
                diagonal = jnp.sum(jnp.where(lane == s + 8 * t + sub, tiles[t], 0.0), axis=1, keepdims=True)
                tiles[t] = tiles[t] * (1.0 / jnp.sqrt(diagonal))
            inverse = jnp.concatenate(tiles, axis=0)[:, o : o + STEP]
            high = inverse.astype(BF16).astype(F32)
            left = jnp.concatenate([high, inverse - high, high], axis=1).astype(BF16)
            wh, wl = split(work_ref[g, s : s + STEP])
            rows = dot1(left, jnp.concatenate([wh, wh, wl], axis=0), 1, 0)
            work_ref[g, s : s + STEP] = rows
            if s + STEP < GROUP:
                rh, rl = split(rows)
                ah, al = rh[:, :GROUP], rl[:, :GROUP]
                update = dot1(jnp.concatenate([ah, al, ah], axis=0), jnp.concatenate([rh, rh, rl], axis=0), 0, 0)
                below = slice(s + STEP, GROUP)
                work_ref[g, below] = work_ref[g, below] - update[s + STEP :]
    bring.wait()
    for g in range(groups):
        factor_ref[g] = jnp.where(row_of >= lane_of, work_ref[g, :, :GROUP].T, 0.0)
        inverse = jnp.where(row_of >= lane_of, work_ref[g, :, GROUP:], 0.0)
        columns = slice(g * GROUP, (g + 1) * GROUP)
        nh, nl = split(inverse)
        weights = jnp.concatenate([beside(nh, nh), beside(nl, jnp.zeros_like(nl))], axis=0)
        both = dot1(beside(*split(residual[:, columns])), weights, 1, 1)
        new[g] = both[:, :GROUP] + both[:, GROUP:]
        store = pltpu.make_async_copy(new.at[g], new_ref.at[:, columns], out_sem.at[1, g])
        store.start()
        stores.append(store)
    for store in stores:
        store.wait()


def factor_and_solve(gram, residual, flat_coeffs, count):
    groups = gram.shape[0]
    anywhere = pl.BlockSpec(memory_space=pl.ANY)
    shape = (groups, count, GROUP, GROUP)
    return pl.pallas_call(
        factor_kernel,
        out_shape=(
            jax.ShapeDtypeStruct(residual.shape, F32),
            jax.ShapeDtypeStruct(gram.shape, F32),
            jax.ShapeDtypeStruct((count, groups, GROUP, GROUP), F32),
        ),
        in_specs=[VMEM_SPEC, anywhere, anywhere],
        out_specs=(anywhere, VMEM_SPEC, anywhere),
        scratch_shapes=[
            pltpu.VMEM((groups, GROUP, 2 * GROUP), F32), pltpu.VMEM(shape, F32),
            pltpu.VMEM(residual.shape, F32), pltpu.VMEM((groups, residual.shape[0], GROUP), F32),
            pltpu.SemaphoreType.DMA((2,)), pltpu.SemaphoreType.DMA((2, groups)),
        ],
        name="factor_and_solve",
    )(gram, residual, flat_coeffs.reshape(shape))


SLOTS = 7
SLOT_OFFSETS = (0, 1, -2, 2, -1, 3, -3)
SLOT_ORIGIN = (0, 1, 0, 0, 1, 1, 1)
CHUNKS = 4
ROWS = 256
PIECE = 256
TICKS = 4
AHEAD = 1
PLAN = ((1, 2), (3,), (4, 5), (6,))
BLOCK = 128
NEAR = 25


def apply_kernel(
    index_ref, strips_ref, vector_ref, out_ref,
    high_ref, low_ref, window, stage_even, stage_odd, image, strip_sem, copy_sem, entry_recv, recv_sem, exit_recv, own_send, relay_send, entry_send,
    exit_send,
):
    blk, rhs = lax.axis_index("blk"), lax.axis_index("rhs")
    x_lo, core = rhs // 2, rhs % 2
    odd = blk % 2
    sign = 1 - 2 * odd

    def peer(t):
        return (x_lo + t // 2) % 2, (core + t % 2) % 2

    def quarter(at):
        return ((at[0] + odd) % 2) * 2 + at[1]

    def group_device(t):
        x, c = peer(t)
        return {"blk": blk, "rhs": x * 2 + c}

    ahead = {"blk": (blk + 32 + 2 * sign) % 32, "rhs": rhs}
    behind = {"blk": (blk + 32 - 2 * sign) % 32, "rhs": rhs}
    partner = {"blk": blk + sign, "rhs": (1 - x_lo) * 2 + core}
    columns = quarter((x_lo, core)) * (CHUNKS * GROUP)

    def entry_rows(chunk, n):
        x, c = peer(n)
        return window.at[chunk, 0, pl.ds((x * 2 + c) * ROWS, ROWS)]

    def piece(chunk, slot, t, source=None):
        x, c = peer(2 * SLOT_ORIGIN[slot if source is None else source] + t)
        return window.at[chunk, slot, pl.ds((x * 2 + c) * PIECE, PIECE)]

    def remote(src, dst, send, recv, device):
        return pltpu.make_async_remote_copy(
            src_ref=src, dst_ref=dst, send_sem=send, recv_sem=recv, device_id=device, device_id_type=MESH
        )

    def strip_copy(i, lane):
        stage = (stage_even, stage_odd)[lane]
        return pltpu.make_async_copy(strips_ref.at[i], stage.at[pl.ds(0, NEAR)], strip_sem.at[lane])

    def own_copy(chunk):
        cols = pl.ds(pl.multiple_of(columns + chunk * GROUP, GROUP), GROUP)
        return pltpu.make_async_copy(vector_ref.at[:, cols], entry_rows(chunk, 0), copy_sem.at[chunk])

    def entry_copy(chunk, t):
        cols = pl.ds(pl.multiple_of(quarter(peer(t)) * (CHUNKS * GROUP) + chunk * GROUP, GROUP), GROUP)
        return remote(
            vector_ref.at[:, cols], entry_rows(chunk, 0), entry_send.at[chunk, t - 1], entry_recv.at[chunk, t - 1],
            group_device(t),
        )

    def exit_copy(chunk, t):
        x, c = peer(t)
        cols = pl.ds(pl.multiple_of(columns + chunk * GROUP, GROUP), GROUP)
        return remote(
            image.at[chunk, pl.ds((x * 2 + c) * ROWS, ROWS)], out_ref.at[:, cols], exit_send.at[chunk, t - 1],
            exit_recv.at[chunk, t - 1], group_device(t),
        )

    def send_copy(chunk, t, way):
        slot, device = ((1, partner), (2, ahead), (3, behind))[way]
        return remote(
            piece(chunk, 0, t), piece(chunk, slot, t, 0), own_send.at[chunk, t, way], recv_sem.at[chunk, slot, t], device
        )

    def relay_copy(chunk, t, way):
        source, slot, device = ((1, 5, behind), (3, 4, partner), (4, 6, ahead))[way]
        return remote(
            piece(chunk, source, t), piece(chunk, slot, t, source), relay_send.at[chunk, t, way],
            recv_sem.at[chunk, slot, t], device,
        )

    def arrived(chunk, slot, t):
        at = piece(chunk, slot, t)
        remote(at, at, own_send.at[chunk, t, 0], recv_sem.at[chunk, slot, t], partner).wait_recv()

    def send_own(chunk, t):
        if t == 0:
            own_copy(chunk).wait()
        else:
            at = entry_rows(chunk, t)
            remote(at, at, entry_send.at[chunk, 0], entry_recv.at[chunk, t - 1], partner).wait_recv()
        for way in range(3):
            send_copy(chunk, t, way).start()

    def relay(chunk, t, way):
        arrived(chunk, (1, 3, 4)[way], t)
        relay_copy(chunk, t, way).start()

    def build(i, lane):
        stage = (stage_even, stage_odd)[lane]
        strip_copy(i, lane).wait()
        rows = slice(i * BLOCK, (i + 1) * BLOCK)

        def one_slot(slot, carry):
            for j in range(8):
                at = slot * 8 + j
                high, low = split(stage[index_ref[i, at]])
                high_ref[slot, rows, j * BLOCK : (j + 1) * BLOCK] = high
                low_ref[slot, rows, j * BLOCK : (j + 1) * BLOCK] = low
            return carry

        lax.fori_loop(0, SLOTS, one_slot, 0)

        if i + 2 < 8:
            strip_copy(i + 2, lane).start()

    def multiply(chunk, slot):
        high, low = split(window[chunk, slot])
        both = dot1(high_ref[slot], beside(high, low), 1, 0)
        rest = dot1(low_ref[slot], high, 1, 0)
        image[chunk] = image[chunk] + (both[:, :GROUP] + (both[:, GROUP:] + rest))

    def finish(chunk):
        cols = pl.ds(pl.multiple_of(columns + chunk * GROUP, GROUP), GROUP)
        out_ref[:, cols] = image[chunk, pl.ds(pl.multiple_of(rhs * ROWS, ROWS), ROWS)]
        for t in (3, 2, 1):
            exit_copy(chunk, t).start()

    def tick(chunk, t, first):
        now = True if first else chunk < CHUNKS
        back = chunk - 1

        def when(condition, action):
            if condition is True:
                action()
            else:
                pl.when(condition)(action)

        if t + AHEAD < TICKS:
            when(now, lambda: send_own(chunk, t + AHEAD))
        else:
            when(True if first else chunk + 1 < CHUNKS, lambda: send_own(chunk + 1, t + AHEAD - TICKS))
        for way, lag in ((0, 1), (1, 1), (2, 2)):
            if t >= lag:
                when(now, functools.partial(relay, chunk, t - lag, way))
            elif not first:
                relay(back, t - lag + TICKS, way)
        if not first:
            for slot in PLAN[t]:
                if slot in (2, 5, 6):
                    for u in range(TICKS):
                        arrived(back, slot, u)
                multiply(back, slot)
                if slot == SLOTS - 1:
                    finish(back)
        if t == TICKS - 1:
            when(now, lambda: multiply(chunk, 0))

    for i in range(2):
        strip_copy(i, i).start()
    for chunk in range(CHUNKS):
        own_copy(chunk).start()

    barrier = pltpu.get_barrier_semaphore()
    for device in [partner, ahead, behind] + [group_device(t) for t in (1, 2, 3)]:
        pl.semaphore_signal(barrier, inc=1, device_id=device, device_id_type=MESH)
    pl.semaphore_wait(barrier, 6)

    for chunk in range(CHUNKS):
        for t in (2, 3, 1):
            entry_copy(chunk, t).start()
    for t in range(AHEAD):
        send_own(0, t)
    image[...] = jnp.zeros_like(image)
    for stage in (stage_even, stage_odd):
        stage[NEAR] = jnp.zeros_like(stage[NEAR])
    for t in range(TICKS):
        rows = range(t * 8 // TICKS, (t + 1) * 8 // TICKS)
        if t == TICKS - 1:
            for i in rows:
                build(i, i % 2)
        tick(0, t, True)
        if t < TICKS - 1:
            for i in rows:
                build(i, i % 2)

    def body(chunk, carry):
        for t in range(TICKS):
            tick(chunk, t, False)
        return carry

    lax.fori_loop(1, CHUNKS + 1, body, 0)

    def drain(chunk, carry):
        for t in (1, 2, 3):
            exit_copy(chunk, t).wait_recv()
            exit_copy(chunk, t).wait_send()
            entry_copy(chunk, t).wait_send()
        for t in range(TICKS):
            for way in range(3):
                send_copy(chunk, t, way).wait_send()
                relay_copy(chunk, t, way).wait_send()
        return carry

    lax.fori_loop(0, CHUNKS, drain, 0)


def place_kernel(total, near_ref, index_ref):
    blocks = near_ref.shape[0]
    blk = lax.axis_index("blk")
    sign = 1 - 2 * (blk % 2)
    at = lax.broadcasted_iota(jnp.int32, index_ref.shape, 1)
    offset = jnp.zeros(index_ref.shape, jnp.int32)
    for slot, by in enumerate(SLOT_OFFSETS):
        offset = jnp.where((at >= slot * blocks) & (at < (slot + 1) * blocks), by * sign * blocks + at - slot * blocks, offset)
    offset = jnp.where(offset < 0, offset + total, offset)
    relative = near_ref[...] - blk * blocks
    relative = jnp.where(relative < 0, relative + total, relative)
    index = jnp.full(index_ref.shape, NEAR, jnp.int32)
    for k in range(NEAR):
        index = jnp.where(relative[:, k : k + 1] == offset, k, index)
    index_ref[...] = index


def apply_near_field(strips, near_cols, vector_block):
    blocks, near = near_cols.shape
    total = blocks * lax.axis_size("blk")
    index = pl.pallas_call(
        functools.partial(place_kernel, total),
        out_shape=jax.ShapeDtypeStruct((blocks, SLOTS * blocks), jnp.int32),
        in_specs=[VMEM_SPEC],
        out_specs=VMEM_SPEC,
        name="place_strips",
    )(near_cols)
    rows, width = vector_block.shape
    smem = pl.BlockSpec(memory_space=pltpu.SMEM)
    anywhere = pl.BlockSpec(memory_space=pl.ANY)
    dma = pltpu.SemaphoreType.DMA
    size = blocks * BLOCK
    return pl.pallas_call(
        apply_kernel,
        out_shape=jax.ShapeDtypeStruct((rows, width), F32),
        in_specs=[smem, anywhere, anywhere],
        out_specs=VMEM_SPEC,
        scratch_shapes=[
            pltpu.VMEM((SLOTS, size, size), BF16),
            pltpu.VMEM((SLOTS, size, size), BF16),
            pltpu.VMEM((CHUNKS, SLOTS, size, GROUP), F32),
            pltpu.VMEM((near + 1, BLOCK, BLOCK), F32),
            pltpu.VMEM((near + 1, BLOCK, BLOCK), F32),
            pltpu.VMEM((CHUNKS, size, GROUP), F32),
            dma((2,)), dma((CHUNKS,)), dma((CHUNKS, 3)), dma((CHUNKS, SLOTS, TICKS)), dma((CHUNKS, 3)),
            dma((CHUNKS, TICKS, 3)), dma((CHUNKS, TICKS, 3)), dma((CHUNKS, 3)), dma((CHUNKS, 3)),
        ],
        compiler_params=pltpu.CompilerParams(
            collective_id=3, has_side_effects=True, vmem_limit_bytes=64_000_000
        ),
        name="apply_near_field",
    )(index, strips, vector_block)


def local(strips, near_cols, vector_block, basis):
    image = apply_near_field(strips, near_cols, vector_block)
    flat_coeffs, residual, gram = orthogonalize(basis, image)
    gram = gram.reshape(-1, GROUP, GROUP)
    new_block, factor, coeffs = factor_and_solve(gram, residual, flat_coeffs, basis.shape[0])
    return (new_block, coeffs, factor)


def solution(mesh):
    placed = (
        P("blk", None, None, None),
        P("blk", None),
        P(("blk", "rhs"), None),
        P(None, ("blk", "rhs"), None),
    )
    return jax.shard_map(
        local,
        mesh=mesh,
        in_specs=placed,
        out_specs=(P(("blk", "rhs"), None), P(), P()),
        check_vma=False,
    )
```

```python
import functools

import jax
import jax.numpy as jnp
from jax import lax
from jax.experimental import pallas as pl
from jax.experimental.pallas import tpu as pltpu
from jax.sharding import PartitionSpec as P

HOPS = 3
GROUP = 128
MESH = pl.DeviceIdType.MESH
BF16, F32 = jnp.bfloat16, jnp.float32
VMEM_SPEC = pl.BlockSpec(memory_space=pltpu.VMEM)


def split(value):
    high = value.astype(BF16)
    low = (value - high.astype(F32)).astype(BF16)
    return high, low


def dot1(a, b, ca, cb):
    return lax.dot_general(a, b, (((ca,), (cb,)), ((), ())), preferred_element_type=F32)


ORDERS = ((0, 1, 2), (1, 2, 0), (2, 0, 1))


def coordinates():
    blk, rhs = lax.axis_index("blk"), lax.axis_index("rhs")
    x = (blk % 2) * 2 + rhs // 2
    return (x, blk // 8, (blk // 2) % 4), rhs % 2


def device_of(place, core):
    x, y, z = place
    return {"blk": (y * 4 + z) * 2 + x // 2, "rhs": (x % 2) * 2 + core}


def moved(place, axis, by):
    at = list(place)
    at[axis] = (at[axis] + by) % 4
    return tuple(at)


COEFF_SHARES = (24, 24, 16)
GRAM_SHARES = (8, 8)
HALF = 8


def beside(high, low):
    return jnp.concatenate([high, low], axis=1)


def orthogonalize_kernel(
    basis_ref, image_ref, coeffs_ref, residual_ref, gram_ref, basis_in, image_in, coeffs_part, gram_part, *rest
):
    coeff_count, gram_count = len(COEFF_SHARES), len(GRAM_SHARES)
    rest = list(rest)

    def take(count):
        taken = rest[:count]
        del rest[:count]
        return taken

    buffers = {}
    for key, count in (("coeffs", coeff_count), ("gram", gram_count)):
        buffers[key] = (take(1)[0], take(3 * count), take(2 * count))
    load_sem, send_sem, recv_sem = rest
    count = basis_ref.shape[0]
    depth = count * GROUP
    place, core = coordinates()
    partner = device_of(place, 1 - core)
    peers = [device_of(moved(place, axis, by), core) for axis in range(3) for by in (1, 2, 3)]
    own_first, other_first = core * HALF, (1 - core) * HALF

    def loads(g):
        columns = pl.ds(pl.multiple_of(g * GROUP, GROUP), GROUP)
        return (
            pltpu.make_async_copy(basis_ref.at[:, :, columns], basis_in.at[g], load_sem.at[0, g]),
            pltpu.make_async_copy(image_ref.at[:, columns], image_in.at[g], load_sem.at[1, g]),
        )

    def start_loads(i, first):
        for load in loads(first + i):
            load.start()
        return first

    lax.fori_loop(0, HALF, start_loads, other_first)
    lax.fori_loop(0, HALF, start_loads, own_first)

    barrier = pltpu.get_barrier_semaphore()
    for peer in [partner] + peers:
        pl.semaphore_signal(barrier, inc=1, device_id=peer, device_id_type=MESH)

    pending = []

    def copy(src, dst, device):
        at = len(pending)
        made = pltpu.make_async_remote_copy(
            src_ref=src, dst_ref=dst, send_sem=send_sem.at[at], recv_sem=recv_sem.at[at],
            device_id=device, device_id_type=MESH,
        )
        made.start()
        pending.append(made)
        return made

    def basis_halves(g):
        return split(jnp.concatenate([basis_in[g, m] for m in range(count)], axis=1))

    def local_coeffs(i, first):
        g = first + i
        for load in loads(g):
            load.wait()
        ih, il = split(image_in[g])
        bh, bl = basis_halves(g)
        both = dot1(bh, beside(ih, il), 0, 0)
        value = both[:, :GROUP] + (both[:, GROUP:] + dot1(bl, ih, 0, 0))
        coeffs_part[pl.ds(pl.multiple_of(g * depth, depth), depth)] = value
        return first

    def local_residual(i, first):
        g = first + i
        bh, bl = basis_halves(g)
        ch, cl = split(coeffs_ref[pl.ds(pl.multiple_of(g * depth, depth), depth)])
        both = dot1(bh, beside(ch, cl), 1, 0)
        value = image_in[g] - (both[:, :GROUP] + (both[:, GROUP:] + dot1(bl, ch, 1, 0)))
        residual_ref[:, pl.ds(pl.multiple_of(g * GROUP, GROUP), GROUP)] = value
        rh, rl = split(value)
        square = dot1(rh, beside(rh, rl), 0, 0)
        cross = square[:, GROUP:]
        gram_part[pl.ds(pl.multiple_of(g * GROUP, GROUP), GROUP)] = square[:, :GROUP] + (cross + cross.T)
        return first

    def bounds(shares):
        ends = [0]
        for share in shares:
            ends.append(ends[-1] + 64 * share)
        return ends

    def swap(key, shares, part_ref, part):
        ends = bounds(shares)
        size = ends[part + 1] - ends[part]
        start = (1 - core) * ends[-1] + ends[part]
        return copy(part_ref.at[pl.ds(start, size)], buffers[key][0].at[pl.ds(ends[part], size)], partner)

    def scatter(key, shares, source, part, stage):
        axis = ORDERS[part][stage]
        size = shares[part] * 4 ** (2 - stage)
        got = buffers[key][1][3 * part + stage]
        return [
            copy(
                source.at[pl.ds((place[axis] + by) % 4 * size, size)], got.at[by - 1],
                device_of(moved(place, axis, by), core),
            )
            for by in (1, 2, 3)
        ]

    def begin(key, shares, part_ref, part, swapped):
        ends = bounds(shares)
        size = ends[part + 1] - ends[part]
        mine = core * ends[-1] + ends[part]
        swapped.wait_recv()
        from_core = buffers[key][0]
        rows = pl.ds(ends[part], size)
        from_core[rows] = from_core[rows] + part_ref[pl.ds(mine, size)]
        source = from_core.at[rows]
        return source, scatter(key, shares, source, part, 0)

    def offset(shares, part, stages):
        ends = bounds(shares)
        at = core * ends[-1] + ends[part]
        for stage in range(stages):
            at = at + place[ORDERS[part][stage]] * (shares[part] * 4 ** (2 - stage))
        return at

    def gather(shares, out_ref, part, stage):
        axis = ORDERS[part][stage]
        size = shares[part] * 4 ** (2 - stage)
        rows = out_ref.at[pl.ds(offset(shares, part, stage + 1), size)]
        return [copy(rows, rows, device_of(moved(place, axis, by), core)) for by in (1, 2, 3)]

    def arrive(copies):
        for made in copies:
            made.wait_recv()

    def sum_up(key, shares, begun, out_ref):
        live = dict(enumerate(begun))
        for stage in range(3):
            for part, share in enumerate(shares):
                source, copies = live[part]
                arrive(copies)
                axis = ORDERS[part][stage]
                size = share * 4 ** (2 - stage)
                got = buffers[key][1][3 * part + stage]
                value = source[pl.ds(place[axis] * size, size)] + got[0] + got[1] + got[2]
                if stage < 2:
                    acc = buffers[key][2][2 * part + stage]
                    acc[...] = value
                    live[part] = (acc, scatter(key, shares, acc, part, stage + 1))
                else:
                    out_ref[pl.ds(offset(shares, part, 3), share)] = value
                    live[part] = gather(shares, out_ref, part, 2)
        for stage in (2, 1, 0):
            for part in range(len(shares)):
                arrive(live[part])
                if stage:
                    live[part] = gather(shares, out_ref, part, stage - 1)
                else:
                    yield part

    def give(shares, out_ref, part):
        ends = bounds(shares)
        rows = out_ref.at[pl.ds(core * ends[-1] + ends[part], ends[part + 1] - ends[part])]
        return copy(rows, rows, partner)

    spans = [(end // depth, last // depth) for end, last in zip(bounds(COEFF_SHARES), bounds(COEFF_SHARES)[1:])]
    swapped = []
    for part, (low, high) in enumerate(spans):
        lax.fori_loop(low, high, local_coeffs, other_first, unroll=True)
        if part == 0:
            pl.semaphore_wait(barrier, 10)
        swapped.append(swap("coeffs", COEFF_SHARES, coeffs_part, part))
    begun = []
    for part, (low, high) in enumerate(spans):
        lax.fori_loop(low, high, local_coeffs, own_first, unroll=True)
        begun.append(begin("coeffs", COEFF_SHARES, coeffs_part, part, swapped[part]))
    given = []
    for part in sum_up("coeffs", COEFF_SHARES, begun, coeffs_ref):
        given.append(give(COEFF_SHARES, coeffs_ref, part))
        lax.fori_loop(*spans[part], local_residual, own_first, unroll=True)

    swapped = []
    for part, (low, high) in enumerate(spans):
        given[part].wait_recv()
        lax.fori_loop(low, high, local_residual, other_first, unroll=True)
        if part:
            swapped.append(swap("gram", GRAM_SHARES, gram_part, part - 1))
    begun = [begin("gram", GRAM_SHARES, gram_part, part, swapped[part]) for part in range(gram_count)]
    given = [give(GRAM_SHARES, gram_ref, part) for part in sum_up("gram", GRAM_SHARES, begun, gram_ref)]
    arrive(given)
    for made in pending:
        made.wait_send()


def orthogonalize(basis, image):
    count, rows, width = basis.shape
    groups = width // GROUP
    scratch = [
        pltpu.VMEM((groups, count, rows, GROUP), F32),
        pltpu.VMEM((groups, rows, GROUP), F32),
        pltpu.VMEM((groups * count * GROUP, GROUP), F32),
        pltpu.VMEM((groups * GROUP, GROUP), F32),
    ]
    copies = 0
    for shares in (COEFF_SHARES, GRAM_SHARES):
        scratch.append(pltpu.VMEM((64 * sum(shares), GROUP), F32))
        for share in shares:
            scratch += [pltpu.VMEM((3, share * 4 ** (2 - stage), GROUP), F32) for stage in range(3)]
        for share in shares:
            scratch += [pltpu.VMEM((share * 4 ** (2 - stage), GROUP), F32) for stage in range(2)]
        copies += 20 * len(shares)
    dma = pltpu.SemaphoreType.DMA
    anywhere = pl.BlockSpec(memory_space=pl.ANY)
    return pl.pallas_call(
        orthogonalize_kernel,
        out_shape=(
            jax.ShapeDtypeStruct((groups * count * GROUP, GROUP), F32),
            jax.ShapeDtypeStruct((rows, width), F32),
            jax.ShapeDtypeStruct((groups * GROUP, GROUP), F32),
        ),
        in_specs=[anywhere, anywhere],
        out_specs=(VMEM_SPEC, VMEM_SPEC, VMEM_SPEC),
        scratch_shapes=scratch + [dma((2, groups)), dma((copies,)), dma((copies,))],
        compiler_params=pltpu.CompilerParams(
            collective_id=1, has_side_effects=True, vmem_limit_bytes=60_000_000
        ),
        name="orthogonalize",
    )(basis, image)


STEP = 32
PIVOTS = 2


def factor_kernel(gram_ref, residual_ref, flat_ref, new_ref, factor_ref, coeffs_ref, work_ref, held, residual, new, factor, in_sem, out_sem):
    groups = gram_ref.shape[0]
    fetch = pltpu.make_async_copy(flat_ref, held, in_sem.at[0])
    fetch.start()
    bring = pltpu.make_async_copy(residual_ref, residual, in_sem.at[1])
    bring.start()
    shape = (GROUP, GROUP)
    row_of = lax.broadcasted_iota(jnp.int32, shape, 0)
    lane_of = lax.broadcasted_iota(jnp.int32, shape, 1)
    eye = jnp.where(row_of == lane_of, 1.0, 0.0).astype(F32)
    for g in range(groups):
        work_ref[g, :, :GROUP] = gram_ref[g]
        work_ref[g, :, GROUP:] = eye
    lane = lax.broadcasted_iota(jnp.int32, (8, GROUP), 1)
    sub = lax.broadcasted_iota(jnp.int32, (8, GROUP), 0)
    stores = [
        pltpu.make_async_copy(held.at[g], coeffs_ref.at[:, g], out_sem.at[0, g]) for g in range(groups)
    ]
    count = STEP // 8
    for block in range(GROUP // STEP):
        if block == 1:
            fetch.wait()
            for store in stores:
                store.start()
        s = block * STEP
        o = (s + 64) % GROUP
        ones = [jnp.where(lane == o + 8 * t + sub, 1.0, 0.0).astype(F32) for t in range(count)]
        inside = (lane >= s) & (lane < s + STEP)
        panels = [
            [jnp.where(inside, work_ref[g, s + 8 * t : s + 8 * t + 8, :GROUP], ones[t]) for t in range(count)]
            for g in range(groups)
        ]
        for first in range(0, STEP, PIVOTS):
            at, within = first // 8, first % 8
            for tiles in panels:
                columns = {
                    t: [
                        jnp.broadcast_to(tiles[t][:, s + first + q : s + first + q + 1], (8, GROUP))
                        for q in range(PIVOTS)
                    ]
                    for t in range(at, count)
                }
                for q in range(PIVOTS):
                    pivot = slice(within + q, within + q + 1)
                    inverse = 1.0 / columns[at][q][pivot]
                    scaled = tiles[at][pivot] * inverse
                    later = [columns[at][p][pivot] * inverse for p in range(q + 1, PIVOTS)]
                    for t in range(at, count):
                        column = columns[t][q]
                        if t == at:
                            column = jnp.where(sub > within + q, column, 0.0)
                        tiles[t] = tiles[t] - column * scaled
                        for p, value in zip(range(q + 1, PIVOTS), later):
                            columns[t][p] = columns[t][p] - column * value
        for g, tiles in enumerate(panels):
            for t in range(count):
                diagonal = jnp.sum(jnp.where(lane == s + 8 * t + sub, tiles[t], 0.0), axis=1, keepdims=True)
                tiles[t] = tiles[t] * (1.0 / jnp.sqrt(diagonal))
            inverse = jnp.concatenate(tiles, axis=0)[:, o : o + STEP]
            high = inverse.astype(BF16).astype(F32)
            left = jnp.concatenate([high, inverse - high, high], axis=1).astype(BF16)
            wh, wl = split(work_ref[g, s : s + STEP])
            rows = dot1(left, jnp.concatenate([wh, wh, wl], axis=0), 1, 0)
            work_ref[g, s : s + STEP] = rows
            if s + STEP < GROUP:
                rh, rl = split(rows)
                ah, al = rh[:, :GROUP], rl[:, :GROUP]
                update = dot1(jnp.concatenate([ah, al, ah], axis=0), jnp.concatenate([rh, rh, rl], axis=0), 0, 0)
                below = slice(s + STEP, GROUP)
                work_ref[g, below] = work_ref[g, below] - update[s + STEP :]
    bring.wait()
    for g in range(groups):
        factor[g] = jnp.where(row_of >= lane_of, work_ref[g, :, :GROUP].T, 0.0)
        store = pltpu.make_async_copy(factor.at[g], factor_ref.at[g], out_sem.at[2, g])
        store.start()
        stores.append(store)
        inverse = jnp.where(row_of >= lane_of, work_ref[g, :, GROUP:], 0.0)
        columns = slice(g * GROUP, (g + 1) * GROUP)
        nh, nl = split(inverse)
        weights = jnp.concatenate([beside(nh, nh), beside(nl, jnp.zeros_like(nl))], axis=0)
        both = dot1(beside(*split(residual[:, columns])), weights, 1, 1)
        new[g] = both[:, :GROUP] + both[:, GROUP:]
        store = pltpu.make_async_copy(new.at[g], new_ref.at[:, columns], out_sem.at[1, g])
        store.start()
        stores.append(store)
    for store in stores:
        store.wait()


def factor_and_solve(gram, residual, flat_coeffs, count):
    groups = gram.shape[0]
    anywhere = pl.BlockSpec(memory_space=pl.ANY)
    shape = (groups, count, GROUP, GROUP)
    return pl.pallas_call(
        factor_kernel,
        out_shape=(
            jax.ShapeDtypeStruct(residual.shape, F32),
            jax.ShapeDtypeStruct(gram.shape, F32),
            jax.ShapeDtypeStruct((count, groups, GROUP, GROUP), F32),
        ),
        in_specs=[VMEM_SPEC, anywhere, anywhere],
        out_specs=(anywhere, anywhere, anywhere),
        scratch_shapes=[
            pltpu.VMEM((groups, GROUP, 2 * GROUP), F32), pltpu.VMEM(shape, F32),
            pltpu.VMEM(residual.shape, F32), pltpu.VMEM((groups, residual.shape[0], GROUP), F32),
            pltpu.VMEM(gram.shape, F32), pltpu.SemaphoreType.DMA((2,)), pltpu.SemaphoreType.DMA((3, groups)),
        ],
        name="factor_and_solve",
    )(gram, residual, flat_coeffs.reshape(shape))


SLOTS = 7
SLOT_OFFSETS = (0, 1, -2, 2, -1, 3, -3)
SLOT_ORIGIN = (0, 1, 0, 0, 1, 1, 1)
CHUNKS = 4
ROWS = 256
PIECE = 256
TICKS = 4
AHEAD = 1
PLAN = ((1, 2), (3,), (4, 5), (6,))
BLOCK = 128
NEAR = 25


def place_strips(near_ref, index_ref, blk, sign):
    blocks = near_ref.shape[0]
    total = 32 * blocks
    at = lax.broadcasted_iota(jnp.int32, index_ref.shape, 1)
    offset = jnp.zeros(index_ref.shape, jnp.int32)
    for slot, by in enumerate(SLOT_OFFSETS):
        here = (at >= slot * blocks) & (at < (slot + 1) * blocks)
        offset = jnp.where(here, by * sign * blocks + at - slot * blocks, offset)
    offset = jnp.where(offset < 0, offset + total, offset)
    relative = near_ref[...] - blk * blocks
    relative = jnp.where(relative < 0, relative + total, relative)
    index = jnp.full(index_ref.shape, NEAR, jnp.int32)
    for k in range(NEAR):
        index = jnp.where(relative[:, k : k + 1] == offset, k, index)
    index_ref[...] = index


def apply_kernel(
    near_ref, strips_ref, vector_ref, out_ref,
    high_ref, low_ref, window, stage_even, stage_odd, image, index_held, index_ref, index_sem, strip_sem, copy_sem, entry_recv, recv_sem, exit_recv, own_send, relay_send, entry_send,
    exit_send,
):
    blk, rhs = lax.axis_index("blk"), lax.axis_index("rhs")
    x_lo, core = rhs // 2, rhs % 2
    odd = blk % 2
    sign = 1 - 2 * odd

    def peer(t):
        return (x_lo + t // 2) % 2, (core + t % 2) % 2

    def quarter(at):
        return ((at[0] + odd) % 2) * 2 + at[1]

    def group_device(t):
        x, c = peer(t)
        return {"blk": blk, "rhs": x * 2 + c}

    ahead = {"blk": (blk + 32 + 2 * sign) % 32, "rhs": rhs}
    behind = {"blk": (blk + 32 - 2 * sign) % 32, "rhs": rhs}
    partner = {"blk": blk + sign, "rhs": (1 - x_lo) * 2 + core}
    columns = quarter((x_lo, core)) * (CHUNKS * GROUP)

    def entry_rows(chunk, n):
        x, c = peer(n)
        return window.at[chunk, 0, pl.ds((x * 2 + c) * ROWS, ROWS)]

    def piece(chunk, slot, t, source=None):
        x, c = peer(2 * SLOT_ORIGIN[slot if source is None else source] + t)
        return window.at[chunk, slot, pl.ds((x * 2 + c) * PIECE, PIECE)]

    def remote(src, dst, send, recv, device):
        return pltpu.make_async_remote_copy(
            src_ref=src, dst_ref=dst, send_sem=send, recv_sem=recv, device_id=device, device_id_type=MESH
        )

    def strip_copy(i, lane):
        stage = (stage_even, stage_odd)[lane]
        return pltpu.make_async_copy(strips_ref.at[i], stage.at[pl.ds(0, NEAR)], strip_sem.at[lane])

    def own_copy(chunk):
        cols = pl.ds(pl.multiple_of(columns + chunk * GROUP, GROUP), GROUP)
        return pltpu.make_async_copy(vector_ref.at[:, cols], entry_rows(chunk, 0), copy_sem.at[chunk])

    def entry_copy(chunk, t):
        cols = pl.ds(pl.multiple_of(quarter(peer(t)) * (CHUNKS * GROUP) + chunk * GROUP, GROUP), GROUP)
        return remote(
            vector_ref.at[:, cols], entry_rows(chunk, 0), entry_send.at[chunk, t - 1], entry_recv.at[chunk, t - 1],
            group_device(t),
        )

    def exit_copy(chunk, t):
        x, c = peer(t)
        cols = pl.ds(pl.multiple_of(columns + chunk * GROUP, GROUP), GROUP)
        return remote(
            image.at[chunk, pl.ds((x * 2 + c) * ROWS, ROWS)], out_ref.at[:, cols], exit_send.at[chunk, t - 1],
            exit_recv.at[chunk, t - 1], group_device(t),
        )

    def send_copy(chunk, t, way):
        slot, device = ((1, partner), (2, ahead), (3, behind))[way]
        return remote(
            piece(chunk, 0, t), piece(chunk, slot, t, 0), own_send.at[chunk, t, way], recv_sem.at[chunk, slot, t], device
        )

    def relay_copy(chunk, t, way):
        source, slot, device = ((1, 5, behind), (3, 4, partner), (4, 6, ahead))[way]
        return remote(
            piece(chunk, source, t), piece(chunk, slot, t, source), relay_send.at[chunk, t, way],
            recv_sem.at[chunk, slot, t], device,
        )

    def arrived(chunk, slot, t):
        at = piece(chunk, slot, t)
        remote(at, at, own_send.at[chunk, t, 0], recv_sem.at[chunk, slot, t], partner).wait_recv()

    def send_own(chunk, t):
        if t == 0:
            own_copy(chunk).wait()
        else:
            at = entry_rows(chunk, t)
            remote(at, at, entry_send.at[chunk, 0], entry_recv.at[chunk, t - 1], partner).wait_recv()
        for way in range(3):
            send_copy(chunk, t, way).start()

    def relay(chunk, t, way):
        arrived(chunk, (1, 3, 4)[way], t)
        relay_copy(chunk, t, way).start()

    def build(i, lane):
        stage = (stage_even, stage_odd)[lane]
        strip_copy(i, lane).wait()
        rows = slice(i * BLOCK, (i + 1) * BLOCK)

        def one_slot(slot, carry):
            for j in range(8):
                at = slot * 8 + j
                high, low = split(stage[index_ref[i, at]])
                high_ref[slot, rows, j * BLOCK : (j + 1) * BLOCK] = high
                low_ref[slot, rows, j * BLOCK : (j + 1) * BLOCK] = low
            return carry

        lax.fori_loop(0, SLOTS, one_slot, 0)

        if i + 2 < 8:
            strip_copy(i + 2, lane).start()

    def multiply(chunk, slot):
        high, low = split(window[chunk, slot])
        both = dot1(high_ref[slot], beside(high, low), 1, 0)
        rest = dot1(low_ref[slot], high, 1, 0)
        image[chunk] = image[chunk] + (both[:, :GROUP] + (both[:, GROUP:] + rest))

    def finish(chunk):
        cols = pl.ds(pl.multiple_of(columns + chunk * GROUP, GROUP), GROUP)
        slot = SLOTS - 1
        high, low = split(window[chunk, slot])
        halves = beside(high, low)
        for t in (3, 2, 1, 0):
            x, c = peer(t)
            rows = pl.ds(pl.multiple_of((x * 2 + c) * ROWS, ROWS), ROWS)
            both = dot1(high_ref[slot, rows], halves, 1, 0)
            rest = dot1(low_ref[slot, rows], high, 1, 0)
            value = image[chunk, rows] + (both[:, :GROUP] + (both[:, GROUP:] + rest))
            if t:
                image[chunk, rows] = value
                exit_copy(chunk, t).start()
            else:
                out_ref[:, cols] = value

    def tick(chunk, t, first):
        now = True if first else chunk < CHUNKS
        back = chunk - 1

        def when(condition, action):
            if condition is True:
                action()
            else:
                pl.when(condition)(action)

        if t + AHEAD < TICKS:
            when(now, lambda: send_own(chunk, t + AHEAD))
        else:
            when(True if first else chunk + 1 < CHUNKS, lambda: send_own(chunk + 1, t + AHEAD - TICKS))
        for way, lag in ((0, 1), (1, 1), (2, 2)):
            if t >= lag:
                when(now, functools.partial(relay, chunk, t - lag, way))
            elif not first:
                relay(back, t - lag + TICKS, way)
        if not first:
            for slot in PLAN[t]:
                if slot in (2, 5, 6):
                    for u in range(TICKS):
                        arrived(back, slot, u)
                if slot == SLOTS - 1:
                    finish(back)
                else:
                    multiply(back, slot)
        if t == TICKS - 1:
            when(now, lambda: multiply(chunk, 0))

    for i in range(2):
        strip_copy(i, i).start()
    for chunk in range(CHUNKS):
        own_copy(chunk).start()

    barrier = pltpu.get_barrier_semaphore()
    for device in [partner, ahead, behind] + [group_device(t) for t in (1, 2, 3)]:
        pl.semaphore_signal(barrier, inc=1, device_id=device, device_id_type=MESH)
    place_strips(near_ref, index_held, blk, sign)
    table = pltpu.make_async_copy(index_held, index_ref, index_sem)
    table.start()
    pl.semaphore_wait(barrier, 6)

    for chunk in range(CHUNKS):
        for t in (2, 3, 1):
            entry_copy(chunk, t).start()
    for t in range(AHEAD):
        send_own(0, t)
    image[...] = jnp.zeros_like(image)
    for stage in (stage_even, stage_odd):
        stage[NEAR] = jnp.zeros_like(stage[NEAR])
    table.wait()
    for t in range(TICKS):
        rows = range(t * 8 // TICKS, (t + 1) * 8 // TICKS)
        if t == TICKS - 1:
            for i in rows:
                build(i, i % 2)
        tick(0, t, True)
        if t < TICKS - 1:
            for i in rows:
                build(i, i % 2)

    def body(chunk, carry):
        for t in range(TICKS):
            tick(chunk, t, False)
        return carry

    lax.fori_loop(1, CHUNKS + 1, body, 0)

    def drain(chunk, carry):
        for t in (1, 2, 3):
            exit_copy(chunk, t).wait_recv()
            exit_copy(chunk, t).wait_send()
            entry_copy(chunk, t).wait_send()
        for t in range(TICKS):
            for way in range(3):
                send_copy(chunk, t, way).wait_send()
                relay_copy(chunk, t, way).wait_send()
        return carry

    lax.fori_loop(0, CHUNKS, drain, 0)


def apply_near_field(strips, near_cols, vector_block):
    blocks, near = near_cols.shape
    rows, width = vector_block.shape
    anywhere = pl.BlockSpec(memory_space=pl.ANY)
    dma = pltpu.SemaphoreType.DMA
    size = blocks * BLOCK
    return pl.pallas_call(
        apply_kernel,
        out_shape=jax.ShapeDtypeStruct((rows, width), F32),
        in_specs=[VMEM_SPEC, anywhere, anywhere],
        out_specs=VMEM_SPEC,
        scratch_shapes=[
            pltpu.VMEM((SLOTS, size, size), BF16),
            pltpu.VMEM((SLOTS, size, size), BF16),
            pltpu.VMEM((CHUNKS, SLOTS, size, GROUP), F32),
            pltpu.VMEM((near + 1, BLOCK, BLOCK), F32),
            pltpu.VMEM((near + 1, BLOCK, BLOCK), F32),
            pltpu.VMEM((CHUNKS, size, GROUP), F32),
            pltpu.VMEM((blocks, 128), jnp.int32),
            pltpu.SMEM((blocks, 128), jnp.int32),
            dma(()), dma((2,)), dma((CHUNKS,)), dma((CHUNKS, 3)), dma((CHUNKS, SLOTS, TICKS)), dma((CHUNKS, 3)),
            dma((CHUNKS, TICKS, 3)), dma((CHUNKS, TICKS, 3)), dma((CHUNKS, 3)), dma((CHUNKS, 3)),
        ],
        compiler_params=pltpu.CompilerParams(
            collective_id=3, has_side_effects=True, vmem_limit_bytes=64_000_000
        ),
        name="apply_near_field",
    )(near_cols, strips, vector_block)


def local(strips, near_cols, vector_block, basis):
    image = apply_near_field(strips, near_cols, vector_block)
    flat_coeffs, residual, gram = orthogonalize(basis, image)
    gram = gram.reshape(-1, GROUP, GROUP)
    new_block, factor, coeffs = factor_and_solve(gram, residual, flat_coeffs, basis.shape[0])
    return (new_block, coeffs, factor)


def solution(mesh):
    placed = (
        P("blk", None, None, None),
        P("blk", None),
        P(("blk", "rhs"), None),
        P(None, ("blk", "rhs"), None),
    )
    return jax.shard_map(
        local,
        mesh=mesh,
        in_specs=placed,
        out_specs=(P(("blk", "rhs"), None), P(), P()),
        check_vma=False,
    )
```

```python
import functools

import jax
import jax.numpy as jnp
from jax import lax
from jax.experimental import pallas as pl
from jax.experimental.pallas import tpu as pltpu
from jax.sharding import PartitionSpec as P

HOPS = 3
GROUP = 128
MESH = pl.DeviceIdType.MESH
BF16, F32 = jnp.bfloat16, jnp.float32
VMEM_SPEC = pl.BlockSpec(memory_space=pltpu.VMEM)


def split(value):
    high = value.astype(BF16)
    low = (value - high.astype(F32)).astype(BF16)
    return high, low


def dot1(a, b, ca, cb):
    return lax.dot_general(a, b, (((ca,), (cb,)), ((), ())), preferred_element_type=F32)


ORDERS = ((0, 1, 2), (1, 2, 0), (2, 0, 1))


def coordinates():
    blk, rhs = lax.axis_index("blk"), lax.axis_index("rhs")
    x = (blk % 2) * 2 + rhs // 2
    return (x, blk // 8, (blk // 2) % 4), rhs % 2


def device_of(place, core):
    x, y, z = place
    return {"blk": (y * 4 + z) * 2 + x // 2, "rhs": (x % 2) * 2 + core}


def moved(place, axis, by):
    at = list(place)
    at[axis] = (at[axis] + by) % 4
    return tuple(at)


COEFF_SHARES = (24, 24, 16)
GRAM_SHARES = (8, 8)
HALF = 8


def beside(high, low):
    return jnp.concatenate([high, low], axis=1)


def orthogonalize_kernel(
    basis_ref, image_ref, coeffs_ref, residual_ref, gram_ref, basis_in, image_in, coeffs_part, gram_part, *rest
):
    coeff_count, gram_count = len(COEFF_SHARES), len(GRAM_SHARES)
    rest = list(rest)

    def take(count):
        taken = rest[:count]
        del rest[:count]
        return taken

    buffers = {}
    for key, count in (("coeffs", coeff_count), ("gram", gram_count)):
        buffers[key] = (take(1)[0], take(3 * count), take(2 * count))
    load_sem, send_sem, recv_sem = rest
    count = basis_ref.shape[0]
    depth = count * GROUP
    place, core = coordinates()
    partner = device_of(place, 1 - core)
    peers = [device_of(moved(place, axis, by), core) for axis in range(3) for by in (1, 2, 3)]
    own_first, other_first = core * HALF, (1 - core) * HALF

    def loads(g):
        columns = pl.ds(pl.multiple_of(g * GROUP, GROUP), GROUP)
        return (
            pltpu.make_async_copy(basis_ref.at[:, :, columns], basis_in.at[g], load_sem.at[0, g]),
            pltpu.make_async_copy(image_ref.at[:, columns], image_in.at[g], load_sem.at[1, g]),
        )

    def start_loads(i, first):
        for load in loads(first + i):
            load.start()
        return first

    lax.fori_loop(0, HALF, start_loads, other_first)
    lax.fori_loop(0, HALF, start_loads, own_first)

    barrier = pltpu.get_barrier_semaphore()
    for peer in [partner] + peers:
        pl.semaphore_signal(barrier, inc=1, device_id=peer, device_id_type=MESH)

    pending = []

    def copy(src, dst, device):
        at = len(pending)
        made = pltpu.make_async_remote_copy(
            src_ref=src, dst_ref=dst, send_sem=send_sem.at[at], recv_sem=recv_sem.at[at],
            device_id=device, device_id_type=MESH,
        )
        made.start()
        pending.append(made)
        return made

    def basis_halves(g):
        return split(jnp.concatenate([basis_in[g, m] for m in range(count)], axis=1))

    def local_coeffs(i, first):
        g = first + i
        for load in loads(g):
            load.wait()
        ih, il = split(image_in[g])
        bh, bl = basis_halves(g)
        both = dot1(bh, beside(ih, il), 0, 0)
        value = both[:, :GROUP] + (both[:, GROUP:] + dot1(bl, ih, 0, 0))
        coeffs_part[pl.ds(pl.multiple_of(g * depth, depth), depth)] = value
        return first

    def local_residual(i, first):
        g = first + i
        bh, bl = basis_halves(g)
        ch, cl = split(coeffs_ref[pl.ds(pl.multiple_of(g * depth, depth), depth)])
        both = dot1(bh, beside(ch, cl), 1, 0)
        value = image_in[g] - (both[:, :GROUP] + (both[:, GROUP:] + dot1(bl, ch, 1, 0)))
        residual_ref[:, pl.ds(pl.multiple_of(g * GROUP, GROUP), GROUP)] = value
        rh, rl = split(value)
        square = dot1(rh, beside(rh, rl), 0, 0)
        cross = square[:, GROUP:]
        gram_part[pl.ds(pl.multiple_of(g * GROUP, GROUP), GROUP)] = square[:, :GROUP] + (cross + cross.T)
        return first

    def bounds(shares):
        ends = [0]
        for share in shares:
            ends.append(ends[-1] + 64 * share)
        return ends

    def swap(key, shares, part_ref, part):
        ends = bounds(shares)
        size = ends[part + 1] - ends[part]
        start = (1 - core) * ends[-1] + ends[part]
        return copy(part_ref.at[pl.ds(start, size)], buffers[key][0].at[pl.ds(ends[part], size)], partner)

    def scatter(key, shares, source, part, stage):
        axis = ORDERS[part][stage]
        size = shares[part] * 4 ** (2 - stage)
        got = buffers[key][1][3 * part + stage]
        return [
            copy(
                source.at[pl.ds((place[axis] + by) % 4 * size, size)], got.at[by - 1],
                device_of(moved(place, axis, by), core),
            )
            for by in (1, 2, 3)
        ]

    def begin(key, shares, part_ref, part, swapped):
        ends = bounds(shares)
        size = ends[part + 1] - ends[part]
        mine = core * ends[-1] + ends[part]
        swapped.wait_recv()
        from_core = buffers[key][0]
        rows = pl.ds(ends[part], size)
        from_core[rows] = from_core[rows] + part_ref[pl.ds(mine, size)]
        source = from_core.at[rows]
        return source, scatter(key, shares, source, part, 0)

    def offset(shares, part, stages):
        ends = bounds(shares)
        at = core * ends[-1] + ends[part]
        for stage in range(stages):
            at = at + place[ORDERS[part][stage]] * (shares[part] * 4 ** (2 - stage))
        return at

    def gather(shares, out_ref, part, stage):
        axis = ORDERS[part][stage]
        size = shares[part] * 4 ** (2 - stage)
        rows = out_ref.at[pl.ds(offset(shares, part, stage + 1), size)]
        return [copy(rows, rows, device_of(moved(place, axis, by), core)) for by in (1, 2, 3)]

    def arrive(copies):
        for made in copies:
            made.wait_recv()

    def sum_up(key, shares, begun, out_ref):
        live = dict(enumerate(begun))
        for stage in range(3):
            for part, share in enumerate(shares):
                source, copies = live[part]
                arrive(copies)
                axis = ORDERS[part][stage]
                size = share * 4 ** (2 - stage)
                got = buffers[key][1][3 * part + stage]
                value = source[pl.ds(place[axis] * size, size)] + got[0] + got[1] + got[2]
                if stage < 2:
                    acc = buffers[key][2][2 * part + stage]
                    acc[...] = value
                    live[part] = (acc, scatter(key, shares, acc, part, stage + 1))
                else:
                    out_ref[pl.ds(offset(shares, part, 3), share)] = value
                    live[part] = gather(shares, out_ref, part, 2)
        for stage in (2, 1, 0):
            for part in range(len(shares)):
                arrive(live[part])
                if stage:
                    live[part] = gather(shares, out_ref, part, stage - 1)
                else:
                    yield part

    def give(shares, out_ref, part):
        ends = bounds(shares)
        rows = out_ref.at[pl.ds(core * ends[-1] + ends[part], ends[part + 1] - ends[part])]
        return copy(rows, rows, partner)

    spans = [(end // depth, last // depth) for end, last in zip(bounds(COEFF_SHARES), bounds(COEFF_SHARES)[1:])]
    swapped = []
    for part, (low, high) in enumerate(spans):
        lax.fori_loop(low, high, local_coeffs, other_first, unroll=True)
        if part == 0:
            pl.semaphore_wait(barrier, 10)
        swapped.append(swap("coeffs", COEFF_SHARES, coeffs_part, part))
    begun = []
    for part, (low, high) in enumerate(spans):
        lax.fori_loop(low, high, local_coeffs, own_first, unroll=True)
        begun.append(begin("coeffs", COEFF_SHARES, coeffs_part, part, swapped[part]))
    given = []
    for part in sum_up("coeffs", COEFF_SHARES, begun, coeffs_ref):
        given.append(give(COEFF_SHARES, coeffs_ref, part))
        lax.fori_loop(*spans[part], local_residual, own_first, unroll=True)

    swapped = []
    for part, (low, high) in enumerate(spans):
        given[part].wait_recv()
        lax.fori_loop(low, high, local_residual, other_first, unroll=True)
        if part:
            swapped.append(swap("gram", GRAM_SHARES, gram_part, part - 1))
    begun = [begin("gram", GRAM_SHARES, gram_part, part, swapped[part]) for part in range(gram_count)]
    given = [give(GRAM_SHARES, gram_ref, part) for part in sum_up("gram", GRAM_SHARES, begun, gram_ref)]
    arrive(given)
    for made in pending:
        made.wait_send()


def orthogonalize(basis, image):
    count, rows, width = basis.shape
    groups = width // GROUP
    scratch = [
        pltpu.VMEM((groups, count, rows, GROUP), F32),
        pltpu.VMEM((groups, rows, GROUP), F32),
        pltpu.VMEM((groups * count * GROUP, GROUP), F32),
        pltpu.VMEM((groups * GROUP, GROUP), F32),
    ]
    copies = 0
    for shares in (COEFF_SHARES, GRAM_SHARES):
        scratch.append(pltpu.VMEM((64 * sum(shares), GROUP), F32))
        for share in shares:
            scratch += [pltpu.VMEM((3, share * 4 ** (2 - stage), GROUP), F32) for stage in range(3)]
        for share in shares:
            scratch += [pltpu.VMEM((share * 4 ** (2 - stage), GROUP), F32) for stage in range(2)]
        copies += 20 * len(shares)
    dma = pltpu.SemaphoreType.DMA
    anywhere = pl.BlockSpec(memory_space=pl.ANY)
    return pl.pallas_call(
        orthogonalize_kernel,
        out_shape=(
            jax.ShapeDtypeStruct((groups * count * GROUP, GROUP), F32),
            jax.ShapeDtypeStruct((rows, width), F32),
            jax.ShapeDtypeStruct((groups * GROUP, GROUP), F32),
        ),
        in_specs=[anywhere, anywhere],
        out_specs=(VMEM_SPEC, VMEM_SPEC, VMEM_SPEC),
        scratch_shapes=scratch + [dma((2, groups)), dma((copies,)), dma((copies,))],
        compiler_params=pltpu.CompilerParams(
            collective_id=1, has_side_effects=True, vmem_limit_bytes=60_000_000
        ),
        name="orthogonalize",
    )(basis, image)


STEP = 32
PIVOTS = 2


def factor_kernel(gram_ref, residual_ref, flat_ref, new_ref, factor_ref, coeffs_ref, work_ref, held, residual, new, factor, in_sem, out_sem):
    groups = gram_ref.shape[0]
    fetch = pltpu.make_async_copy(flat_ref, held, in_sem.at[0])
    fetch.start()
    bring = pltpu.make_async_copy(residual_ref, residual, in_sem.at[1])
    bring.start()
    shape = (GROUP, GROUP)
    row_of = lax.broadcasted_iota(jnp.int32, shape, 0)
    lane_of = lax.broadcasted_iota(jnp.int32, shape, 1)
    eye = jnp.where(row_of == lane_of, 1.0, 0.0).astype(F32)
    for g in range(groups):
        work_ref[g, :, :GROUP] = gram_ref[g]
        work_ref[g, :, GROUP:] = eye
    lane = lax.broadcasted_iota(jnp.int32, (8, GROUP), 1)
    sub = lax.broadcasted_iota(jnp.int32, (8, GROUP), 0)
    stores = [
        pltpu.make_async_copy(held.at[g], coeffs_ref.at[:, g], out_sem.at[0, g]) for g in range(groups)
    ]
    count = STEP // 8
    for block in range(GROUP // STEP):
        if block == 1:
            fetch.wait()
            for store in stores:
                store.start()
        s = block * STEP
        o = (s + 64) % GROUP
        ones = [jnp.where(lane == o + 8 * t + sub, 1.0, 0.0).astype(F32) for t in range(count)]
        inside = (lane >= s) & (lane < s + STEP)
        panels = [
            [jnp.where(inside, work_ref[g, s + 8 * t : s + 8 * t + 8, :GROUP], ones[t]) for t in range(count)]
            for g in range(groups)
        ]
        for first in range(0, STEP, PIVOTS):
            at, within = first // 8, first % 8
            for tiles in panels:
                columns = {
                    t: [
                        jnp.broadcast_to(tiles[t][:, s + first + q : s + first + q + 1], (8, GROUP))
                        for q in range(PIVOTS)
                    ]
                    for t in range(at, count)
                }
                for q in range(PIVOTS):
                    pivot = slice(within + q, within + q + 1)
                    inverse = 1.0 / columns[at][q][pivot]
                    scaled = tiles[at][pivot] * inverse
                    later = [columns[at][p][pivot] * inverse for p in range(q + 1, PIVOTS)]
                    for t in range(at, count):
                        column = columns[t][q]
                        if t == at:
                            column = jnp.where(sub > within + q, column, 0.0)
                        tiles[t] = tiles[t] - column * scaled
                        for p, value in zip(range(q + 1, PIVOTS), later):
                            columns[t][p] = columns[t][p] - column * value
        for g, tiles in enumerate(panels):
            for t in range(count):
                diagonal = jnp.sum(jnp.where(lane == s + 8 * t + sub, tiles[t], 0.0), axis=1, keepdims=True)
                tiles[t] = tiles[t] * (1.0 / jnp.sqrt(diagonal))
            inverse = jnp.concatenate(tiles, axis=0)[:, o : o + STEP]
            high = inverse.astype(BF16).astype(F32)
            left = jnp.concatenate([high, inverse - high, high], axis=1).astype(BF16)
            wh, wl = split(work_ref[g, s : s + STEP])
            rows = dot1(left, jnp.concatenate([wh, wh, wl], axis=0), 1, 0)
            work_ref[g, s : s + STEP] = rows
            if s + STEP < GROUP:
                rh, rl = split(rows)
                ah, al = rh[:, :GROUP], rl[:, :GROUP]
                update = dot1(jnp.concatenate([ah, al, ah], axis=0), jnp.concatenate([rh, rh, rl], axis=0), 0, 0)
                below = slice(s + STEP, GROUP)
                work_ref[g, below] = work_ref[g, below] - update[s + STEP :]
    bring.wait()
    for g in range(groups):
        factor[g] = jnp.where(row_of >= lane_of, work_ref[g, :, :GROUP].T, 0.0)
        store = pltpu.make_async_copy(factor.at[g], factor_ref.at[g], out_sem.at[2, g])
        store.start()
        stores.append(store)
        inverse = jnp.where(row_of >= lane_of, work_ref[g, :, GROUP:], 0.0)
        columns = slice(g * GROUP, (g + 1) * GROUP)
        nh, nl = split(inverse)
        weights = jnp.concatenate([beside(nh, nh), beside(nl, jnp.zeros_like(nl))], axis=0)
        both = dot1(beside(*split(residual[:, columns])), weights, 1, 1)
        new[g] = both[:, :GROUP] + both[:, GROUP:]
        store = pltpu.make_async_copy(new.at[g], new_ref.at[:, columns], out_sem.at[1, g])
        store.start()
        stores.append(store)
    for store in stores:
        store.wait()


def factor_and_solve(gram, residual, flat_coeffs, count):
    groups = gram.shape[0]
    anywhere = pl.BlockSpec(memory_space=pl.ANY)
    shape = (groups, count, GROUP, GROUP)
    return pl.pallas_call(
        factor_kernel,
        out_shape=(
            jax.ShapeDtypeStruct(residual.shape, F32),
            jax.ShapeDtypeStruct(gram.shape, F32),
            jax.ShapeDtypeStruct((count, groups, GROUP, GROUP), F32),
        ),
        in_specs=[VMEM_SPEC, anywhere, anywhere],
        out_specs=(anywhere, anywhere, anywhere),
        scratch_shapes=[
            pltpu.VMEM((groups, GROUP, 2 * GROUP), F32), pltpu.VMEM(shape, F32),
            pltpu.VMEM(residual.shape, F32), pltpu.VMEM((groups, residual.shape[0], GROUP), F32),
            pltpu.VMEM(gram.shape, F32), pltpu.SemaphoreType.DMA((2,)), pltpu.SemaphoreType.DMA((3, groups)),
        ],
        name="factor_and_solve",
    )(gram, residual, flat_coeffs.reshape(shape))


SLOTS = 7
SLOT_OFFSETS = (0, 1, -2, 2, -1, 3, -3)
SLOT_ORIGIN = (0, 1, 0, 0, 1, 1, 1)
CHUNKS = 4
ROWS = 256
PIECE = 256
TICKS = 4
AHEAD = 1
PLAN = ((1, 2), (3,), (4, 5), (6,))
BLOCK = 128
NEAR = 25


def place_strips(near_ref, index_ref, blk, sign):
    blocks = near_ref.shape[0]
    total = 32 * blocks
    at = lax.broadcasted_iota(jnp.int32, index_ref.shape, 1)
    offset = jnp.zeros(index_ref.shape, jnp.int32)
    for slot, by in enumerate(SLOT_OFFSETS):
        here = (at >= slot * blocks) & (at < (slot + 1) * blocks)
        offset = jnp.where(here, by * sign * blocks + at - slot * blocks, offset)
    offset = jnp.where(offset < 0, offset + total, offset)
    relative = near_ref[...] - blk * blocks
    relative = jnp.where(relative < 0, relative + total, relative)
    index = jnp.full(index_ref.shape, NEAR, jnp.int32)
    for k in range(NEAR):
        index = jnp.where(relative[:, k : k + 1] == offset, k, index)
    index_ref[...] = index


def apply_kernel(
    near_ref, strips_ref, vector_ref, out_ref,
    high_ref, low_ref, window, stage_even, stage_odd, image, index_held, index_ref, index_sem, strip_sem, copy_sem, entry_recv, recv_sem, exit_recv, own_send, relay_send, entry_send,
    exit_send,
):
    blk, rhs = lax.axis_index("blk"), lax.axis_index("rhs")
    x_lo, core = rhs // 2, rhs % 2
    odd = blk % 2
    sign = 1 - 2 * odd

    def peer(t):
        return (x_lo + t // 2) % 2, (core + t % 2) % 2

    def quarter(at):
        return ((at[0] + odd) % 2) * 2 + at[1]

    def group_device(t):
        x, c = peer(t)
        return {"blk": blk, "rhs": x * 2 + c}

    ahead = {"blk": (blk + 32 + 2 * sign) % 32, "rhs": rhs}
    behind = {"blk": (blk + 32 - 2 * sign) % 32, "rhs": rhs}
    partner = {"blk": blk + sign, "rhs": (1 - x_lo) * 2 + core}
    columns = quarter((x_lo, core)) * (CHUNKS * GROUP)

    def entry_rows(chunk, n):
        x, c = peer(n)
        return window.at[chunk, 0, pl.ds((x * 2 + c) * ROWS, ROWS)]

    def piece(chunk, slot, t, source=None):
        x, c = peer(2 * SLOT_ORIGIN[slot if source is None else source] + t)
        return window.at[chunk, slot, pl.ds((x * 2 + c) * PIECE, PIECE)]

    def remote(src, dst, send, recv, device):
        return pltpu.make_async_remote_copy(
            src_ref=src, dst_ref=dst, send_sem=send, recv_sem=recv, device_id=device, device_id_type=MESH
        )

    def strip_copy(i, lane):
        stage = (stage_even, stage_odd)[lane]
        return pltpu.make_async_copy(strips_ref.at[i], stage.at[pl.ds(0, NEAR)], strip_sem.at[lane])

    def own_copy(chunk):
        cols = pl.ds(pl.multiple_of(columns + chunk * GROUP, GROUP), GROUP)
        return pltpu.make_async_copy(vector_ref.at[:, cols], entry_rows(chunk, 0), copy_sem.at[chunk])

    def entry_copy(chunk, t):
        cols = pl.ds(pl.multiple_of(quarter(peer(t)) * (CHUNKS * GROUP) + chunk * GROUP, GROUP), GROUP)
        return remote(
            vector_ref.at[:, cols], entry_rows(chunk, 0), entry_send.at[chunk, t - 1], entry_recv.at[chunk, t - 1],
            group_device(t),
        )

    def exit_copy(chunk, t):
        x, c = peer(t)
        cols = pl.ds(pl.multiple_of(columns + chunk * GROUP, GROUP), GROUP)
        return remote(
            image.at[chunk, pl.ds((x * 2 + c) * ROWS, ROWS)], out_ref.at[:, cols], exit_send.at[chunk, t - 1],
            exit_recv.at[chunk, t - 1], group_device(t),
        )

    def send_copy(chunk, t, way):
        slot, device = ((1, partner), (2, ahead), (3, behind))[way]
        return remote(
            piece(chunk, 0, t), piece(chunk, slot, t, 0), own_send.at[chunk, t, way], recv_sem.at[chunk, slot, t], device
        )

    def relay_copy(chunk, t, way):
        source, slot, device = ((1, 5, behind), (3, 4, partner), (4, 6, ahead))[way]
        return remote(
            piece(chunk, source, t), piece(chunk, slot, t, source), relay_send.at[chunk, t, way],
            recv_sem.at[chunk, slot, t], device,
        )

    def arrived(chunk, slot, t):
        at = piece(chunk, slot, t)
        remote(at, at, own_send.at[chunk, t, 0], recv_sem.at[chunk, slot, t], partner).wait_recv()

    def send_own(chunk, t):
        if t == 0:
            own_copy(chunk).wait()
        else:
            at = entry_rows(chunk, t)
            remote(at, at, entry_send.at[chunk, 0], entry_recv.at[chunk, t - 1], partner).wait_recv()
        for way in range(3):
            send_copy(chunk, t, way).start()

    def relay(chunk, t, way):
        arrived(chunk, (1, 3, 4)[way], t)
        relay_copy(chunk, t, way).start()

    def build(i, lane):
        stage = (stage_even, stage_odd)[lane]
        strip_copy(i, lane).wait()
        rows = slice(i * BLOCK, (i + 1) * BLOCK)

        def one_slot(slot, carry):
            for j in range(8):
                at = slot * 8 + j
                high, low = split(stage[index_ref[i, at]])
                high_ref[slot, rows, j * BLOCK : (j + 1) * BLOCK] = high
                low_ref[slot, rows, j * BLOCK : (j + 1) * BLOCK] = low
            return carry

        lax.fori_loop(0, SLOTS, one_slot, 0)

        if i + 2 < 8:
            strip_copy(i + 2, lane).start()

    def multiply(chunk, slot):
        high, low = split(window[chunk, slot])
        both = dot1(high_ref[slot], beside(high, low), 1, 0)
        rest = dot1(low_ref[slot], high, 1, 0)
        image[chunk] = image[chunk] + (both[:, :GROUP] + (both[:, GROUP:] + rest))

    def finish(chunk):
        cols = pl.ds(pl.multiple_of(columns + chunk * GROUP, GROUP), GROUP)
        slot = SLOTS - 1
        high, low = split(window[chunk, slot])
        halves = beside(high, low)
        for t in (3, 2, 1, 0):
            x, c = peer(t)
            rows = pl.ds(pl.multiple_of((x * 2 + c) * ROWS, ROWS), ROWS)
            both = dot1(high_ref[slot, rows], halves, 1, 0)
            rest = dot1(low_ref[slot, rows], high, 1, 0)
            value = image[chunk, rows] + (both[:, :GROUP] + (both[:, GROUP:] + rest))
            if t:
                image[chunk, rows] = value
                exit_copy(chunk, t).start()
            else:
                out_ref[:, cols] = value

    def tick(chunk, t, first):
        now = True if first else chunk < CHUNKS
        back = chunk - 1

        def when(condition, action):
            if condition is True:
                action()
            else:
                pl.when(condition)(action)

        for way, lag in ((0, 1), (1, 1), (2, 2)):
            if t >= lag:
                when(now, functools.partial(relay, chunk, t - lag, way))
            elif not first:
                relay(back, t - lag + TICKS, way)
        if t + AHEAD < TICKS:
            when(now, lambda: send_own(chunk, t + AHEAD))
        else:
            when(True if first else chunk + 1 < CHUNKS, lambda: send_own(chunk + 1, t + AHEAD - TICKS))
        if not first:
            for slot in PLAN[t]:
                if slot in (2, 5, 6):
                    for u in range(TICKS):
                        arrived(back, slot, u)
                if slot == SLOTS - 1:
                    finish(back)
                else:
                    multiply(back, slot)
        if t == TICKS - 1:
            when(now, lambda: multiply(chunk, 0))

    for i in range(2):
        strip_copy(i, i).start()
    for chunk in range(CHUNKS):
        own_copy(chunk).start()

    barrier = pltpu.get_barrier_semaphore()
    for device in [partner, ahead, behind] + [group_device(t) for t in (1, 2, 3)]:
        pl.semaphore_signal(barrier, inc=1, device_id=device, device_id_type=MESH)
    place_strips(near_ref, index_held, blk, sign)
    table = pltpu.make_async_copy(index_held, index_ref, index_sem)
    table.start()
    pl.semaphore_wait(barrier, 6)

    for chunk in range(CHUNKS):
        for t in (2, 3, 1):
            entry_copy(chunk, t).start()
    for t in range(AHEAD):
        send_own(0, t)
    image[...] = jnp.zeros_like(image)
    for stage in (stage_even, stage_odd):
        stage[NEAR] = jnp.zeros_like(stage[NEAR])
    table.wait()
    for t in range(TICKS):
        rows = range(t * 8 // TICKS, (t + 1) * 8 // TICKS)
        if t == TICKS - 1:
            for i in rows:
                build(i, i % 2)
        tick(0, t, True)
        if t < TICKS - 1:
            for i in rows:
                build(i, i % 2)

    def body(chunk, carry):
        for t in range(TICKS):
            tick(chunk, t, False)
        return carry

    lax.fori_loop(1, CHUNKS + 1, body, 0)

    def drain(chunk, carry):
        for t in (1, 2, 3):
            exit_copy(chunk, t).wait_recv()
            exit_copy(chunk, t).wait_send()
            entry_copy(chunk, t).wait_send()
        for t in range(TICKS):
            for way in range(3):
                send_copy(chunk, t, way).wait_send()
                relay_copy(chunk, t, way).wait_send()
        return carry

    lax.fori_loop(0, CHUNKS, drain, 0)


def apply_near_field(strips, near_cols, vector_block):
    blocks, near = near_cols.shape
    rows, width = vector_block.shape
    anywhere = pl.BlockSpec(memory_space=pl.ANY)
    dma = pltpu.SemaphoreType.DMA
    size = blocks * BLOCK
    return pl.pallas_call(
        apply_kernel,
        out_shape=jax.ShapeDtypeStruct((rows, width), F32),
        in_specs=[VMEM_SPEC, anywhere, anywhere],
        out_specs=VMEM_SPEC,
        scratch_shapes=[
            pltpu.VMEM((SLOTS, size, size), BF16),
            pltpu.VMEM((SLOTS, size, size), BF16),
            pltpu.VMEM((CHUNKS, SLOTS, size, GROUP), F32),
            pltpu.VMEM((near + 1, BLOCK, BLOCK), F32),
            pltpu.VMEM((near + 1, BLOCK, BLOCK), F32),
            pltpu.VMEM((CHUNKS, size, GROUP), F32),
            pltpu.VMEM((blocks, 128), jnp.int32),
            pltpu.SMEM((blocks, 128), jnp.int32),
            dma(()), dma((2,)), dma((CHUNKS,)), dma((CHUNKS, 3)), dma((CHUNKS, SLOTS, TICKS)), dma((CHUNKS, 3)),
            dma((CHUNKS, TICKS, 3)), dma((CHUNKS, TICKS, 3)), dma((CHUNKS, 3)), dma((CHUNKS, 3)),
        ],
        compiler_params=pltpu.CompilerParams(
            collective_id=3, has_side_effects=True, vmem_limit_bytes=64_000_000
        ),
        name="apply_near_field",
    )(near_cols, strips, vector_block)


def local(strips, near_cols, vector_block, basis):
    image = apply_near_field(strips, near_cols, vector_block)
    flat_coeffs, residual, gram = orthogonalize(basis, image)
    gram = gram.reshape(-1, GROUP, GROUP)
    new_block, factor, coeffs = factor_and_solve(gram, residual, flat_coeffs, basis.shape[0])
    return (new_block, coeffs, factor)


def solution(mesh):
    placed = (
        P("blk", None, None, None),
        P("blk", None),
        P(("blk", "rhs"), None),
        P(None, ("blk", "rhs"), None),
    )
    return jax.shard_map(
        local,
        mesh=mesh,
        in_specs=placed,
        out_specs=(P(("blk", "rhs"), None), P(), P()),
        check_vma=False,
    )
```
